32 devices in a mesh: dp: 32 (over z, y, x, core).
Axes of the slice: x: 2, y: 2, z: 4, core: 2. Of those that a mesh axis runs over, the one named last changes fastest.
Arguments:
- tokens: bfloat16 [64, 577, 1024], P('dp'), may hold values from -6 to 6
- cotangent: bfloat16 [64, 577, 1024], P('dp'), may hold values from -6 to 6
- params: float32 [12595200], P('dp'), may hold values from -0.8 to 0.8
- moment_one: float32 [12595200], P('dp'), may hold values from -0.00024414062 to 0.00024414062
- moment_two: float32 [12595200], P('dp'), may hold values from 1.5879065e-09 to 7.939533e-09
Outputs:
- outputs: bfloat16 [64, 577, 1024], P('dp')
- grad_tokens: bfloat16 [64, 577, 1024], P('dp')
- weight_grad: float32 [12595200], P('dp')
- params_new: float32 [12595200], P('dp')
- moment_one_new: float32 [12595200], P('dp')
- moment_two_new: float32 [12595200], P('dp')
The draws below stay inside these ranges and needn't reach their ends.
All inputs are finite; a program needn't handle non-finite values.
Results may differ from the reference program's by a relative error of at most 0.0095.
Values may be sent and summed in bfloat16 or wider, within the bound.
A program may use at most 448 MiB of HBM per device.

```python
import math
import jax
import jax.numpy as jnp
from jax import lax

D = 1024
HEADS = 16
HEAD = 64
FF = 4096
SEQ = 577
STEP = 4
IMAGES = 64
P_SIZE = 12595200


def draw_params(key, part):
    positions = jnp.arange(P_SIZE)
    qkv_end = 3 * D * D
    out_end = qkv_end + D * D
    up_end = out_end + D * FF
    down_end = up_end + FF * D
    scales = jnp.where(positions < qkv_end, D ** (-0.5), jnp.where(positions < out_end, 6.0 * D ** (-0.5), jnp.where(positions < up_end, D ** (-0.5), jnp.where(positions < down_end, FF ** (-0.5), 0.2))))
    draws_raw = jnp.clip(jax.random.normal(key, (P_SIZE,), jnp.float32), -4.0, 4.0)
    return draws_raw * scales


def shard_levels(own_key, extent, cuts, least, high):
    def one(position, shards_of):
        steps = jax.random.uniform(jax.random.fold_in(jax.random.fold_in(own_key, 6), position), (shards_of,), jnp.float32, least / len(cuts), high / len(cuts))
        return jnp.repeat(jnp.exp(steps), extent[position] // shards_of).reshape((-1,) + (1,) * (len(extent) - position - 1))

    level = one(*cuts[0])
    for cut in cuts[1:]:
        level = level * one(*cut)
    return level


def gaussian(rng, shape, deviation, bound, split=(), held_as=jnp.bfloat16):
    values = jax.random.normal(rng, shape, jnp.float32) * deviation
    if len(split) > 0:
        values = shard_levels(rng, shape, split, -0.22, 0.18) * values
    return jnp.clip(values, min=-bound, max=bound).astype(held_as)


def setup_inputs(seed: int = 0) -> dict:
    splits = jax.random.split(jax.random.key(seed), 6)
    return {
        "tokens": gaussian(splits[0], (IMAGES, SEQ, D), 1.0, 6.0, ((0, 32),)),
        "cotangent": gaussian(splits[1], (IMAGES, SEQ, D), 1.0, 6.0, ((0, 32),)),
        "params": draw_params(jax.random.fold_in(splits[5], 71), 0),
        "moment_one": gaussian(splits[3], (P_SIZE,), (0.15 / P_SIZE ** 0.5), 0.00024414062, ((0, 32),), jnp.float32),
        "moment_two": jnp.clip(jnp.exp(math.log(7.939532586931364e-09) - 1.609438 * jax.random.uniform(splits[4], (P_SIZE,), jnp.float32) ** shard_levels(splits[4], (P_SIZE,), ((0, 32),), -0.2, 0.2)), 1.5879064729773518e-09, 7.939532586931364e-09),
    }


@jax.custom_vjp
def low(v):
    return lax.optimization_barrier(v.astype(jnp.bfloat16)).astype(jnp.float32)

@jax.custom_vjp
def low_back(v):
    return v

def low_keep(v):
    return (low(v), None)

def low_pass(kept, grad):
    return (grad,)

def back_keep(v):
    return (v, None)

def back_low(kept, grad):
    return (low(grad),)
low.defvjp(low_keep, low_pass)
low_back.defvjp(back_keep, back_low)
norm_eps = 1e-06
max_norm = 1.0
beta_one = 0.9
beta_two = 0.95
learn_rate = 0.02
decay_rate = 0.05
adam_eps = 1e-08
exact_mode = lax.Precision.HIGHEST

def unpack(flat):
    lengths = [3 * D * D, D * D, D * FF, FF * D, D, D, D, FF, D, D, D, D, D]
    pieces = []
    offset = 0
    for length in lengths:
        pieces.append(flat[offset:offset + length])
        offset = offset + length
    matrices = (pieces[0].reshape(D, 3 * D), pieces[1].reshape(D, D), pieces[2].reshape(D, FF), pieces[3].reshape(FF, D))
    return (matrices, tuple(pieces[4:]))

def layer_norm(values, shift, bias):
    center = values - lax.optimization_barrier(jnp.mean(values, axis=-1, keepdims=True))
    recip = lax.rsqrt(lax.optimization_barrier(jnp.mean(center * center, axis=-1, keepdims=True)) + norm_eps)
    return center * recip * (1.0 + shift) + bias

def forward(params, image):
    matrices, vectors = unpack(low(params))
    w_qkv, w_out, w_up, w_down = matrices
    b_query, b_value, b_out, b_up, b_down, shift_one, bias_one, shift_two, bias_two = vectors
    normed = low(layer_norm(image, shift_one, bias_one))
    project = jnp.dot(normed, w_qkv, precision=exact_mode)
    query = low(low_back(project[:, :D] + b_query)).reshape(SEQ, HEADS, HEAD)
    key_part = low(low_back(project[:, D:2 * D])).reshape(SEQ, HEADS, HEAD)
    value_part = low(low_back(project[:, 2 * D:] + b_value)).reshape(SEQ, HEADS, HEAD)
    scores = low_back(jnp.einsum('qhd,khd->hqk', query, key_part, precision=exact_mode) * HEAD ** (-0.5))
    probs = low(jax.nn.softmax(scores, axis=-1))
    mixed = low(low_back(jnp.einsum('hqk,khd->qhd', probs, value_part, precision=exact_mode).reshape(SEQ, D)))
    hidden = image + low_back(jnp.dot(mixed, w_out, precision=exact_mode) + b_out)
    normed_two = low(layer_norm(hidden, shift_two, bias_two))
    pre = low_back(jnp.dot(normed_two, w_up, precision=exact_mode) + b_up)
    active = low(jax.nn.gelu(pre, approximate=False))
    return hidden + (jnp.dot(active, w_down, precision=exact_mode) + b_down)

def reference(tokens, cotangent, params, moment_one, moment_two):

    def one_image(running, inputs_pair):
        image, tangent = inputs_pair
        result, pullback = jax.vjp(forward, params, image.astype(jnp.float32))
        grad_params, grad_image = pullback(tangent.astype(jnp.float32))
        return (running + grad_params, (result.astype(jnp.bfloat16), grad_image.astype(jnp.bfloat16)))
    summed, (outputs, grad_tokens) = lax.scan(one_image, jnp.zeros_like(params), (tokens, cotangent))
    weight_grad = summed / IMAGES
    square_sum = jnp.sum(weight_grad * weight_grad)
    clip_factor = jnp.minimum(1.0, max_norm / (jnp.sqrt(square_sum) + 1e-06))
    clipped = clip_factor * weight_grad
    moment_one_new = beta_one * moment_one + (1.0 - beta_one) * clipped
    moment_two_new = beta_two * moment_two + (1.0 - beta_two) * clipped * clipped
    correct_one = 1.0 - beta_one ** STEP
    correct_two = 1.0 - beta_two ** STEP
    params_new = params - learn_rate * (moment_one_new / correct_one / (jnp.sqrt(moment_two_new / correct_two) + adam_eps) + decay_rate * params)
    return (outputs, grad_tokens, weight_grad, params_new, moment_one_new, moment_two_new)
```

```python
import functools

import jax
import jax.numpy as jnp
from jax import lax
from jax.experimental import pallas as pl
from jax.experimental.pallas import tpu as pltpu
from jax.sharding import PartitionSpec as P

D = 1024
FF = 4096
S = 577
SQ = 592
M = 2 * SQ
CH = 32
PIECES = 96
STEP = 4
BF = jnp.bfloat16
F32 = jnp.float32
MESH = pl.DeviceIdType.MESH
VMEM_ALL = 67043328

EPS = 1e-06
max_norm = 1.0
beta_one = 0.9
beta_two = 0.95
learn_rate = 0.02
decay_rate = 0.05
adam_eps = 1e-08
SCORE = 0.125 * 1.4426950408889634


def nt(a, b):
    return lax.dot_general(a, b, (((1,), (1,)), ((), ())), preferred_element_type=F32)


def nn(a, b):
    return jnp.dot(a, b, preferred_element_type=F32)


def tn(a, b):
    return lax.dot_general(a, b, (((0,), (0,)), ((), ())), preferred_element_type=F32)


def rows_at(c):
    return pl.ds(pl.multiple_of(c * CH, CH), CH)


def full(shape):
    return pl.BlockSpec(shape, lambda *_: (0,) * len(shape), pipeline_mode=pl.Buffered(1))


class Ctx:
    def __init__(s):
        me=lax.axis_index("dp"); s.me=me
        s.core=me%2; s.x=(me//2)%2; s.y=(me//4)%2; s.z=me//8
        s.sib=me+1-2*s.core
        xp=me+2*(1-2*s.x); yp=me+4*(1-2*s.y)
        s.ap=xp+(yp-xp)*s.core
        s.bp=yp+(xp-yp)*s.core
        s.astep=2+2*s.core; s.bstep=4-2*s.core
        s.abit=s.x+(s.y-s.x)*s.core; s.bbit=s.y+(s.x-s.y)*s.core
        s.up=me+8; s.dn=me-8
        s.hasup=s.z<3; s.hasdn=s.z>0
    def barrier(s):
        bar=pltpu.get_barrier_semaphore()
        for p in (s.sib,s.ap,s.bp): pl.semaphore_signal(bar,inc=1,device_id=(p,),device_id_type=MESH)
        @pl.when(s.hasup)
        def _(): pl.semaphore_signal(bar,inc=1,device_id=(s.up,),device_id_type=MESH)
        @pl.when(s.hasdn)
        def _(): pl.semaphore_signal(bar,inc=1,device_id=(s.dn,),device_id_type=MESH)
        pl.semaphore_wait(bar,3+jnp.where(s.hasup,1,0)+jnp.where(s.hasdn,1,0))
class Gather:
    NSEND=3*(5+6*4+7*2+7+7)
    def __init__(s,own,w,ssem,rsem,lsem,K=3,vec=None):
        c=s.c=Ctx(); s.own,s.w,s.ssem,s.rsem,s.lsem=own,w,ssem,rsem,lsem
        s.K=K; s.pend=[]; s.ns=0; s.steps=[]
        TRUE=None
        s.start=s._start
        for dist in range(1,6):
            for sg in (1,-1):
                for kind in ("z","a","b","ba"):
                    extra={"z":0,"a":1,"b":1,"ba":2}[kind]
                    dz=dist-extra
                    if dz<0 or dz>3 or (kind=="z" and dz==0) or (dz==0 and sg<0): continue
                    s.steps.append(functools.partial(s._item,kind,sg*dz))
        s.steps.append(s._finish)
    def _send(s,src,p,to,cond):
        i=s.ns; s.ns+=1
        cp=pltpu.make_async_remote_copy(src,s.w.at[p],s.ssem.at[i],s.rsem.at[p],device_id=(to,),device_id_type=MESH)
        if cond is None: cp.start()
        else:
            @pl.when(cond)
            def _(): cp.start()
        s.pend.append((cp,cond))
    def _start(s):
        c=s.c
        for k in range(s.K):
            p=c.me*s.K+k; src=s.own.at[k]
            s._send(src,p,c.up,c.hasup); s._send(src,p,c.dn,c.hasdn)
            s._send(src,p,c.bp,None); s._send(src,p,c.ap,None); s._send(src,p,c.sib,None)
        s.loc=[]
        for k in range(s.K):
            cp=pltpu.make_async_copy(s.own.at[k],s.w.at[c.me*s.K+k],s.lsem.at[k]); cp.start(); s.loc.append(cp)
    def _wait(s,p):
        pltpu.make_async_copy(s.w.at[p],s.w.at[p],s.rsem.at[p]).wait()
    def _item(s,kind,dz):
        c=s.c
        zz=c.z+dz
        fl=jnp.int32(0)
        src=c.me+8*dz
        if "a" in kind: src=src+c.astep*(1-2*c.abit)
        if "b" in kind: src=src+c.bstep*(1-2*c.bbit)
        valid=None if dz==0 else ((zz<4) if dz>0 else (zz>=0))
        def body():
            for k in range(s.K):
                p=src*s.K+k
                s._wait(p)
                sends=[]
                if kind=="z":
                    sends.append((c.dn,c.hasdn) if dz>0 else (c.up,c.hasup))
                if kind in("z","a"): sends.append((c.bp,None))
                if kind=="z": sends.append((c.ap,None))
                sends.append((c.sib,None))
                for to,cond in sends:
                    i=s.ns; s.ns+=1
                    cp=pltpu.make_async_remote_copy(s.w.at[p],s.w.at[p],s.ssem.at[i],s.rsem.at[p],device_id=(to,),device_id_type=MESH)
                    if cond is None: cp.start()
                    else:
                        @pl.when(cond)
                        def _(): cp.start()
                    s.pend.append((kind,dz,p,i,to,cond,valid))
        if valid is None: body()
        else: pl.when(valid)(body)
    def _finish(s):
        c=s.c
        def sibw(i,_):
            chip=i//s.K; k=i%s.K
            s._wait((2*chip+1-c.core)*s.K+k)
            return 0
        lax.fori_loop(0,16*s.K,sibw,0)
        for e in s.pend:
            if len(e)==2:
                cp,cond=e
                if cond is None: cp.wait_send()
                else: pl.when(cond)(cp.wait_send)
            else:
                kind,dz,p,i,to,cond,valid=e
                def w(i=i):
                    pltpu.make_async_copy(s.w.at[0],s.w.at[0],s.ssem.at[i]).wait()
                cc=cond if valid is None else (valid if cond is None else jnp.logical_and(cond,valid))
                if cc is None: w()
                else: pl.when(cc)(w)
        for cp in s.loc: cp.wait()
def gather_kernel(own_ref,w_ref,ssem,rsem,lsem):
    g=Gather(own_ref,w_ref,ssem,rsem,lsem)
    g.c.barrier()
    g.start()
    for st in g.steps: st()
def gather(own):
    return pl.pallas_call(gather_kernel,out_shape=jax.ShapeDtypeStruct((96,128,1024),BF),
       in_specs=[pl.BlockSpec(memory_space=pltpu.VMEM)],out_specs=pl.BlockSpec(memory_space=pl.ANY),
       scratch_shapes=[pltpu.SemaphoreType.DMA((Gather.NSEND,)),pltpu.SemaphoreType.DMA((96,)),pltpu.SemaphoreType.DMA((3,))],
       compiler_params=pltpu.CompilerParams(collective_id=1,has_side_effects=True),name="gather")(own)

class Reduce:
    K=3
    @staticmethod
    def counts(lo,hi):
        nz=hi-lo+1; K=Reduce.K
        return dict(S=nz*4*K,B=nz*2*K,A=nz*K,Z=(nz+1)*K,send=nz*2*K+nz*K+6*K)
    @staticmethod
    def scratch(lo,hi,nst=4):
        c=Reduce.counts(lo,hi); pc=lambda n: pltpu.VMEM((n,128,1024),BF); sem=lambda n: pltpu.SemaphoreType.DMA((n,))
        return [pc(c["S"]),pc(c["B"]),pc(c["A"]),pc(c["Z"]),pc(nst),sem(c["S"]),sem(c["S"]),sem(c["B"]),sem(c["A"]),sem(c["Z"]),sem(c["send"]),sem(nst)]
    def __init__(s,c,lo,hi,parts,out,scr,scale):
        s.c,s.lo,s.hi,s.parts,s.out,s.scale=c,lo,hi,parts,out,scale
        s.S,s.B,s.A,s.Z,s.st,s.sS,s.rS,s.rB,s.rA,s.rZ,s.ss,s.ls=scr
        s.nst=s.st.shape[0]; s.nz=hi-lo+1
        s.deferred=[]; s.ns=0; s.waits=[]
        K=s.K
        its=[]
        for zz in range(hi,lo-1,-1):
            for fa in (1,0):
                for k in range(K): its.append(("b",zz,1,fa,k))
        for zz in range(hi,lo-1,-1):
            for k in range(K): its.append(("a",zz,0,1,k))
        for dist in (3,2,1,0):
            for sg in ((1,-1) if dist else (1,)):
                for k in range(K): its.append(("z",sg*dist,0,0,k))
        s.its=its
        s.steps=[functools.partial(s._item,i) for i in range(len(its))]+[s._finish]
    def _dest(s,zz,fb,fa,color_core):
        c=s.c
        cc=color_core
        astep=2+2*cc; bstep=4-2*cc
        abit=c.x+(c.y-c.x)*cc; bbit=c.y+(c.x-c.y)*cc
        b=bbit+fb*(1-2*bbit); a=abit+fa*(1-2*abit)
        return zz*8+cc+bstep*b+astep*a
    def _src(s,p,fn):
        if len(s.parts)==1:
            lo,hi,ref=s.parts[0]; fn(ref.at[p-lo]); return
        for lo,hi,ref in s.parts:
            @pl.when(jnp.logical_and(p>=lo,p<hi))
            def _(): fn(ref.at[jnp.clip(p-lo,0,hi-lo-1)])
    def _slotS(s,zz,fb,fa,k): return (((zz-s.lo)*2+fb)*2+fa)*s.K+k
    def send_sibling(s):
        c=s.c; oc=1-c.core
        for (kind,zz,fb,fa,k) in s._order():
            p=s._dest(zz,fb,fa,oc)*s.K+k; sl=s._slotS(zz,fb,fa,k)
            def go(r): pltpu.make_async_remote_copy(r,s.S.at[sl],s.sS.at[sl],s.rS.at[sl],device_id=(c.sib,),device_id_type=MESH).start()
            s._src(p,go)
    def _order(s):
        o=[]
        for it in s.its:
            if it[0] in "ba": o.append(it)
        for zz in range(s.hi,s.lo-1,-1):
            for k in range(s.K): o.append(("z",zz,0,0,k))
        return o
    def _info(s,i):
        kind,zz,fb,fa,k=s.its[i]; valid=None
        if kind=="z":
            zz=s.c.z+zz; valid=jnp.logical_and(zz>=s.lo,zz<=s.hi)
        return kind,zz,fb,fa,k,valid
    def _load(s,i):
        if i>=len(s.its): return
        kind,zz,fb,fa,k,valid=s._info(i)
        p=s._dest(zz,fb,fa,s.c.core)*s.K+k
        def go(r): pltpu.make_async_copy(r,s.st.at[i%s.nst],s.ls.at[i%s.nst]).start()
        if valid is None: s._src(p,go)
        else: pl.when(valid)(lambda: s._src(p,go))
    def prefetch(s):
        for i in range(s.nst-1): s._load(i)
    def _flush(s):
        for f in s.deferred: f()
        s.deferred=[]
    def _wait(s,ref,sem): pltpu.make_async_copy(ref,ref,sem).wait()
    def _sum(s,srcs,dst,scale=None):
        def body(r,_):
            rr=pl.ds(pl.multiple_of(r*16,16),16)
            t=srcs[0][rr,:].astype(F32)
            for q in srcs[1:]: t=t+q[rr,:].astype(F32)
            if scale is not None: t=t*scale
            dst[rr,:]=t.astype(dst.dtype)
            return 0
        lax.fori_loop(0,8,body,0)
    def _item(s,i):
        c=s.c; K=s.K
        kind,zz,fb,fa,k,valid=s._info(i)
        dist=s.its[i][1] if kind=="z" else None
        def main():
            own=s.st.at[i%s.nst]
            s._wait(own,s.ls.at[i%s.nst])
            sl=s._slotS(zz,fb,fa,k)
            srcs=[own,s.S.at[sl]]; s._wait(s.S.at[sl],s.rS.at[sl])
            if kind in "az":
                bi=((zz-s.lo)*2+fa)*K+k; srcs.append(s.B.at[bi]); s._wait(s.B.at[bi],s.rB.at[bi])
            if kind=="z":
                ai=(zz-s.lo)*K+k; srcs.append(s.A.at[ai]); s._wait(s.A.at[ai],s.rA.at[ai])
            return sl,srcs
        def send(sl,dst,rsem,to,n):
            return pltpu.make_async_remote_copy(s.S.at[sl],dst,s.ss.at[n],rsem,device_id=(to,),device_id_type=MESH)
        prev=s.deferred; s.deferred=[]
        if kind in "ba":
            sl,srcs=main()
            s._sum(srcs,s.S.at[sl])
            n=s.ns; s.ns+=1
            if kind=="b":
                bi=((zz-s.lo)*2+fa)*K+k; cp=send(sl,s.B.at[bi],s.rB.at[bi],c.bp,n)
            else:
                ai=(zz-s.lo)*K+k; cp=send(sl,s.A.at[ai],s.rA.at[ai],c.ap,n)
            s.deferred.append(cp.start); s.waits.append((n,None))
        elif dist!=0:
            n=s.ns; s.ns+=1
            upw=dist>0
            zi=(zz-s.lo)*K+k
            has=c.hasdn if upw else c.hasup
            @pl.when(valid)
            def _():
                sl,srcs=main()
                @pl.when(has)
                def _():
                    s._wait(s.Z.at[zi],s.rZ.at[zi]); s._sum(srcs+[s.Z.at[zi]],s.S.at[sl])
                @pl.when(jnp.logical_not(has))
                def _(): s._sum(srcs,s.S.at[sl])
            last=jnp.logical_and(zz==c.z-1,not upw)
            zo=jnp.where(last,s.nz*K+k,zi)
            def st():
                @pl.when(valid)
                def _():
                    send(s._slotS(zz,fb,fa,k),s.Z.at[zo],s.rZ.at[zo],c.up if upw else c.dn,n).start()
            s.deferred.append(st); s.waits.append((n,valid))
        else:
            @pl.when(valid)
            def _():
                sl,srcs=main()
                z1=s.Z.at[(zz-s.lo)*K+k]; r1=s.rZ.at[(zz-s.lo)*K+k]; z2=s.Z.at[s.nz*K+k]; r2=s.rZ.at[s.nz*K+k]
                @pl.when(jnp.logical_and(c.hasdn,c.hasup))
                def _():
                    s._wait(z1,r1); s._wait(z2,r2); s._sum(srcs+[z1,z2],s.out.at[k],s.scale)
                @pl.when(jnp.logical_not(c.hasup))
                def _():
                    s._wait(z1,r1); s._sum(srcs+[z1],s.out.at[k],s.scale)
                @pl.when(jnp.logical_not(c.hasdn))
                def _():
                    s._wait(z2,r2); s._sum(srcs+[z2],s.out.at[k],s.scale)
        for f in prev: f()
        s._load(i+s.nst-1)
    def _finish(s):
        s._flush()
        for n,valid in s.waits:
            w=functools.partial(s._wait,s.S.at[0],s.ss.at[n])
            if valid is None: w()
            else: pl.when(valid)(w)
        def sw(i,_):
            s._wait(s.S.at[0],s.sS.at[i]); return 0
        lax.fori_loop(0,s.S.shape[0],sw,0)
def reduce_kernel(*refs,lo,hi,ranges,scale):
    n=len(ranges)
    parts=[(a,b,r) for (a,b),r in zip(ranges,refs[:n])]
    out=refs[n]; scr=refs[n+1:]
    c=Ctx()
    rd=Reduce(c,lo,hi,parts,out,scr,scale)
    c.barrier()
    rd.send_sibling(); rd.prefetch()
    for st in rd.steps: st()
def reduce_(arrs,lo,hi,ranges,scale,cid=2):
    return pl.pallas_call(functools.partial(reduce_kernel,lo=lo,hi=hi,ranges=ranges,scale=scale),out_shape=jax.ShapeDtypeStruct((3,128,1024),F32),
       in_specs=[pl.BlockSpec(memory_space=pl.ANY)]*len(arrs),out_specs=pl.BlockSpec(memory_space=pltpu.VMEM),
       scratch_shapes=Reduce.scratch(lo,hi),
       compiler_params=pltpu.CompilerParams(collective_id=cid,has_side_effects=True,vmem_limit_bytes=60<<20),name=f"reduce{lo}{hi}")(*arrs)


def qkv_kernel(x_ref, vec_ref, w_ref, out_ref, n_ref):
    j = pl.program_id(0)

    @pl.when(j == 0)
    def _():
        for i in range(2):

            def block(rows, dst):
                v = x_ref[i, rows, :].astype(F32)
                c = v - jnp.mean(v, axis=1, keepdims=True)
                rc = lax.rsqrt(jnp.mean(c * c, axis=1, keepdims=True) + EPS)
                return (c * rc * (1.0 + vec_ref[8:9, :]) + vec_ref[9:10, :]).astype(BF)

            def one(c, _):
                n_ref[i, rows_at(c), :] = block(rows_at(c), None)
                return 0

            lax.fori_loop(0, 18, one, 0)
            last = block(slice(576, 577), None).astype(F32)
            n_ref[i, 576:592, :] = jnp.concatenate([last, jnp.zeros((15, D), F32)], axis=0).astype(BF)

    w = w_ref[...].reshape(D, D)
    bias = jnp.where(j == 0, vec_ref[0:1, :], jnp.where(j == 2, vec_ref[1:2, :], 0.0))
    for i in range(2):
        out_ref[0, i] = (nn(n_ref[i], w) + bias).astype(BF)


def qkv(x, vec, w):
    return pl.pallas_call(
        qkv_kernel,
        grid=(3,),
        in_specs=[full((2, S, D)), full((16, D)), pl.BlockSpec((8, 1, 128, D), lambda j: (0, j, 0, 0))],
        out_specs=[pl.BlockSpec((1, 2, SQ, D), lambda j: (j, 0, 0, 0)), full((2, SQ, D))],
        out_shape=[jax.ShapeDtypeStruct((3, 2, SQ, D), BF), jax.ShapeDtypeStruct((2, SQ, D), BF)],
        compiler_params=pltpu.CompilerParams(vmem_limit_bytes=VMEM_ALL),
        name="qkv",
    )(x, vec, w.reshape(32, 3, 128, D))


def padded(v):
    return jnp.concatenate([v, jnp.zeros((640 - SQ, 128), v.dtype)], axis=0)


def attend_pair(q, k, v):
    lane = lax.broadcasted_iota(jnp.int32, (1, 128), 1)
    k = padded(k)
    v = padded(v)
    outs = []
    for h in range(2):
        mine = lane < 64 if h == 0 else lane >= 64
        s = nt(jnp.where(mine, q, jnp.zeros_like(q)), k)
        s = jnp.concatenate([s[:, :512], jnp.where(lane < S - 512, s[:, 512:], -1e30)], axis=1)
        top = jnp.max(s, axis=1, keepdims=True)
        p = jnp.exp2((s - top) * SCORE)
        total = jnp.sum(p, axis=1, keepdims=True)
        outs.append(nn(p.astype(BF), v) * (1.0 / total))
    return jnp.where(lane < 64, outs[0], outs[1]).astype(BF)


def attend_kernel(q_ref, k_ref, v_ref, o_ref):
    half = SQ // 2
    for r in range(2):
        rows = slice(r * half, (r + 1) * half)
        o_ref[0, rows, :] = attend_pair(q_ref[0, 0, rows, :], k_ref[0, 0], v_ref[0, 0])


def attend(z):
    spec = lambda j: pl.BlockSpec((1, 1, SQ, 128), lambda i, h: (j, i, 0, h))
    return pl.pallas_call(
        attend_kernel,
        grid=(2, 8),
        in_specs=[spec(0), spec(1), spec(2)],
        out_specs=pl.BlockSpec((1, SQ, 128), lambda i, h: (i, 0, h)),
        out_shape=jax.ShapeDtypeStruct((2, SQ, D), BF),
        compiler_params=pltpu.CompilerParams(vmem_limit_bytes=VMEM_ALL),
        name="attend",
    )(z, z, z)


def attend_back_pair(q, k, v, do):
    lane = lax.broadcasted_iota(jnp.int32, (1, 128), 1)
    real = lax.broadcasted_iota(jnp.int32, (16, 1), 0) < S - 576
    q = padded(q)
    do = padded(do)
    dqs, dks, dvs = [], [], []
    for h in range(2):
        mine = lane < 64 if h == 0 else lane >= 64
        s = nt(jnp.where(mine, k, jnp.zeros_like(k)), q)
        s = jnp.concatenate([s[:576], jnp.where(real, s[576:], -1e30)], axis=0)
        top = jnp.max(s, axis=0, keepdims=True)
        p = jnp.exp2((s - top) * SCORE)
        p = p * (1.0 / jnp.sum(p, axis=0, keepdims=True))
        dvs.append(nn(p.astype(BF), do))
        dp = nt(jnp.where(mine, v, jnp.zeros_like(v)), do)
        ds = (p * (dp - jnp.sum(p * dp, axis=0, keepdims=True))).astype(BF)
        dks.append(nn(ds, q))
        dqs.append(tn(ds, k))
    pick = lambda pair, scale: (jnp.where(lane < 64, pair[0], pair[1]) * scale).astype(BF)
    return pick(dqs, 0.125)[:SQ], pick(dks, 0.125), pick(dvs, 1.0)


def attend_back_kernel(q_ref, k_ref, v_ref, do_ref, out_ref):
    dq, dk, dv = attend_back_pair(q_ref[0, 0], k_ref[0, 0], v_ref[0, 0], do_ref[0])
    out_ref[0, 0] = dq
    out_ref[1, 0] = dk
    out_ref[2, 0] = dv


def attend_back(z, do):
    spec = lambda j: pl.BlockSpec((1, 1, SQ, 128), lambda i, h: (j, i, 0, h))
    return pl.pallas_call(
        attend_back_kernel,
        grid=(2, 8),
        in_specs=[spec(0), spec(1), spec(2), pl.BlockSpec((1, SQ, 128), lambda i, h: (i, 0, h))],
        out_specs=pl.BlockSpec((3, 1, SQ, 128), lambda i, h: (0, i, 0, h)),
        out_shape=jax.ShapeDtypeStruct((3, 2, SQ, D), BF),
        compiler_params=pltpu.CompilerParams(vmem_limit_bytes=VMEM_ALL),
        name="attend_back",
    )(z, z, z, do)


def mlp_kernel(x_ref,g_ref,mix_ref,vec_ref,wo_ref,wu_ref,wd_ref,
               out_ref,gup_ref,gdn_ref,gout_ref,dmix_ref,dhid_ref,gvec_ref,
               n2,gs,acc,dn,stat,*,FB,NB):
    jb=pl.program_id(0)
    hid=dhid_ref
    @pl.when(jb==0)
    def _():
        wo=wo_ref[...].reshape(D,D)
        for i in range(2):
            hid[i*SQ:(i+1)*SQ,:]=nn(mix_ref[i],wo)
            gs[i*SQ:i*SQ+576,:]=g_ref[i,:576,:]
            gs[i*SQ+576:(i+1)*SQ,:]=jnp.concatenate([g_ref[i,576:577,:].astype(F32),jnp.zeros((15,D),F32)],axis=0).astype(BF)
            def addx(c,_):
                r=pl.multiple_of(c*CH,CH)
                hid[pl.ds(i*SQ+r,CH),:]+=x_ref[i,pl.ds(r,CH),:].astype(F32)+vec_ref[2:3,:]
                return 0
            lax.fori_loop(0,18,addx,0)
            hid[i*SQ+576:i*SQ+577,:]+=x_ref[i,576:577,:].astype(F32)+vec_ref[2:3,:]
        acc[...]=jnp.zeros_like(acc); dn[...]=jnp.zeros_like(dn)
        gvec_ref[...]=jnp.zeros_like(gvec_ref)
        def ln(c,_):
            r=pl.ds(pl.multiple_of(c*CH,CH),CH)
            h=hid[r,:]
            mu=jnp.mean(h,axis=1,keepdims=True)
            ce=h-mu
            rc=lax.rsqrt(jnp.mean(ce*ce,axis=1,keepdims=True)+EPS)
            n2[r,:]=(ce*rc*(1.0+vec_ref[10:11,:])+vec_ref[11:12,:]).astype(BF)
            stat[r,0:1]=mu; stat[r,1:2]=rc
            return 0
        lax.fori_loop(0,M//CH,ln,0)
        def gsum(c,a):
            r=pl.ds(pl.multiple_of(c*CH,CH),CH)
            return a+gs[r,:].astype(F32)
        t=lax.fori_loop(0,M//CH,gsum,jnp.zeros((CH,D),F32))
        gvec_ref[7:8,:]=jnp.sum(t,axis=0,keepdims=True)
    wu=wu_ref[...].reshape(D,FB); wd=wd_ref[...].reshape(FB,D)
    nper=D//FB
    row=vec_ref[pl.ds(3+jb//nper,1),:]
    bup=row[:,:FB]
    for t in range(1,nper): bup=jnp.where(jb%nper==t,row[:,t*FB:(t+1)*FB],bup)
    g=gs[...]; n=n2[...]
    pre=nn(n,wu)+bup
    cdf=0.5*(1.0+lax.erf(pre*0.7071067811865476))
    act=(pre*cdf).astype(BF)
    slope=cdf+pre*0.3989422804014327*jnp.exp(-0.5*pre*pre)
    dpf=nt(g,wd)*slope
    dp=dpf.astype(BF)
    acc[...]+=nn(act,wd)
    dn[...]+=nt(dp,wu)
    gup_ref[...]=tn(n,dp).astype(BF).reshape(gup_ref.shape)
    gdn_ref[...]=tn(act,g).astype(BF).reshape(gdn_ref.shape)
    bsum=jnp.sum(dp.astype(F32),axis=0,keepdims=True)
    for t in range(nper):
        @pl.when(jb%nper==t)
        def _(): gvec_ref[pl.ds(3+jb//nper,1),t*FB:(t+1)*FB]=bsum
    @pl.when(jb==NB-1)
    def _():
        for i in range(2):
            def ob(c,_):
                r=pl.multiple_of(c*CH,CH)
                out_ref[i,pl.ds(r,CH),:]=(hid[pl.ds(i*SQ+r,CH),:]+(acc[pl.ds(i*SQ+r,CH),:]+vec_ref[7:8,:])).astype(BF)
                return 0
            lax.fori_loop(0,18,ob,0)
            out_ref[i,576:577,:]=(hid[i*SQ+576:i*SQ+577,:]+(acc[i*SQ+576:i*SQ+577,:]+vec_ref[7:8,:])).astype(BF)
        def bk(c,car):
            a,b,d=car
            r=pl.ds(pl.multiple_of(c*CH,CH),CH)
            mu=stat[r,0:1]; rc=stat[r,1:2]
            xh=(hid[r,:]-mu)*rc
            dd=dn[r,:]
            e=dd*(1.0+vec_ref[10:11,:])
            dh=gs[r,:].astype(F32)+rc*(e-jnp.mean(e,axis=1,keepdims=True)-xh*jnp.mean(e*xh,axis=1,keepdims=True))
            dhid_ref[r,:]=dh
            db=dh.astype(BF)
            n2[r,:]=db
            return (a+dd*xh,b+dd,d+db.astype(F32))
        zz=jnp.zeros((CH,D),F32)
        a,b,d=lax.fori_loop(0,M//CH,bk,(zz,zz,zz))
        gvec_ref[10:11,:]=jnp.sum(a,axis=0,keepdims=True)
        gvec_ref[11:12,:]=jnp.sum(b,axis=0,keepdims=True)
        gvec_ref[2:3,:]=jnp.sum(d,axis=0,keepdims=True)
        db=n2[...]
        wo=wo_ref[...].reshape(D,D)
        dmix_ref[...]=nt(db,wo).astype(BF).reshape(2,SQ,D)
        gout_ref[...]=tn(mix_ref[...].reshape(M,D),db).astype(BF).reshape(8,128,D)
def mlp(x,g,mix,vec,W,FB=512):
    NB=4096//FB; nper=D//FB
    W4=W.reshape(96,4,32,1024)
    return pl.pallas_call(functools.partial(mlp_kernel,FB=FB,NB=NB),grid=(NB,),
      in_specs=[full((2,S,D)),full((2,S,D)),full((2,SQ,D)),full((16,D)),
        pl.BlockSpec((8,128,D),lambda j:(3,0,0),pipeline_mode=pl.Buffered(1)),
        pl.BlockSpec((32,1,32,FB),lambda j:(1,j//nper,0,j%nper)),
        pl.BlockSpec((FB//128,128,D),lambda j:(64//(FB//128)+j,0,0))],
      out_specs=[full((2,S,D)),pl.BlockSpec((32,1,32,FB),lambda j:(0,j//nper,0,j%nper)),
        pl.BlockSpec((FB//128,128,D),lambda j:(j,0,0)),full((8,128,D)),full((2,SQ,D)),full((M,D)),full((16,D))],
      out_shape=[jax.ShapeDtypeStruct((2,S,D),BF),jax.ShapeDtypeStruct((32,4,32,D),BF),jax.ShapeDtypeStruct((32,128,D),BF),
        jax.ShapeDtypeStruct((8,128,D),BF),jax.ShapeDtypeStruct((2,SQ,D),BF),jax.ShapeDtypeStruct((M,D),F32),jax.ShapeDtypeStruct((16,D),F32)],
      scratch_shapes=[pltpu.VMEM((M,D),BF),pltpu.VMEM((M,D),BF),pltpu.VMEM((M,D),F32),pltpu.VMEM((M,D),F32),pltpu.VMEM((M,128),F32)],
      compiler_params=pltpu.CompilerParams(vmem_limit_bytes=67043328),name=f"mlp{FB}")(x,g,mix,vec,W,W4,W)


def tail_kernel(x_ref, dz_ref, n_ref, dhid_ref, vec_ref, w_ref, gvin_ref, gx_ref, gw_ref, gvec_ref, acc):
    j = pl.program_id(0)

    @pl.when(j == 0)
    def _():
        gvec_ref[...] = gvin_ref[...]
        acc[...] = jnp.zeros_like(acc)

    w = w_ref[...].reshape(D, D)
    dz = dz_ref[0].reshape(M, D)
    acc[...] += nt(dz, w)
    gw_ref[...] = tn(n_ref[...].reshape(M, D), dz).astype(BF).reshape(8, 1, 128, D)

    @pl.when(j != 1)
    def _():
        def add(c, t):
            return t + dz_ref[0, 0, pl.ds(c * 16, 16), :].astype(F32) + dz_ref[0, 1, pl.ds(c * 16, 16), :].astype(F32)

        t = lax.fori_loop(0, SQ // 16, add, jnp.zeros((16, D), F32))
        gvec_ref[pl.ds(j // 2, 1), :] = jnp.sum(t, axis=0, keepdims=True)

    @pl.when(j == 2)
    def _():
        def back(x, dd, dh):
            v = x.astype(F32)
            ce = v - jnp.mean(v, axis=1, keepdims=True)
            rc = lax.rsqrt(jnp.mean(ce * ce, axis=1, keepdims=True) + EPS)
            xh = ce * rc
            e = dd * (1.0 + vec_ref[8:9, :])
            g = dh + rc * (e - jnp.mean(e, axis=1, keepdims=True) - xh * jnp.mean(e * xh, axis=1, keepdims=True))
            return g.astype(BF), dd * xh, dd

        a = b = jnp.zeros((CH, D), F32)
        la = lb = jnp.zeros((1, D), F32)
        for i in range(2):

            def one(c, carry):
                r = rows_at(c)
                r2 = pl.ds(pl.multiple_of(i * SQ + c * CH, 16), CH)
                g, s1, s2 = back(x_ref[i, r, :], acc[r2, :], dhid_ref[r2, :])
                gx_ref[i, r, :] = g
                return carry[0] + s1, carry[1] + s2

            a, b = lax.fori_loop(0, 18, one, (a, b))
            r2 = slice(i * SQ + 576, i * SQ + 577)
            g, s1, s2 = back(x_ref[i, 576:577, :], acc[r2, :], dhid_ref[r2, :])
            gx_ref[i, 576:577, :] = g
            la, lb = la + s1, lb + s2
        gvec_ref[8:9, :] = jnp.sum(a, axis=0, keepdims=True) + la
        gvec_ref[9:10, :] = jnp.sum(b, axis=0, keepdims=True) + lb


def tail(x, dz, n1, dhid, vec, w, gvec):
    return pl.pallas_call(
        tail_kernel,
        grid=(3,),
        in_specs=[
            full((2, S, D)),
            pl.BlockSpec((1, 2, SQ, D), lambda j: (j, 0, 0, 0)),
            full((2, SQ, D)),
            full((M, D)),
            full((16, D)),
            pl.BlockSpec((8, 1, 128, D), lambda j: (0, j, 0, 0)),
            full((16, D)),
        ],
        out_specs=[full((2, S, D)), pl.BlockSpec((8, 1, 128, D), lambda j: (0, j, 0, 0)), full((16, D))],
        out_shape=[
            jax.ShapeDtypeStruct((2, S, D), BF),
            jax.ShapeDtypeStruct((8, 3, 128, D), BF),
            jax.ShapeDtypeStruct((16, D), F32),
        ],
        scratch_shapes=[pltpu.VMEM((M, D), F32)],
        compiler_params=pltpu.CompilerParams(vmem_limit_bytes=VMEM_ALL),
        name="tail",
    )(x, dz, n1, dhid, vec, w.reshape(32, 3, 128, D), gvec)


def to_pieces(rows, first):
    n = rows.shape[0] // 128
    plain = rows.reshape(n, 128, D)
    three = rows.reshape(n // 3, 128, 3, D).transpose(0, 2, 1, 3).reshape(n, 128, D)
    four = rows.reshape(n, 32, 4, D).transpose(0, 2, 1, 3).reshape(n, 128, D)
    p = first + lax.broadcasted_iota(jnp.int32, (n, 1, 1), 0)
    return jnp.where(p < 24, three, jnp.where((p >= 32) & (p < 64), four, plain))


def from_pieces(pieces, first):
    n = pieces.shape[0]
    plain = pieces.reshape(n * 128, D)
    three = pieces.reshape(n // 3, 3, 128, D).transpose(0, 2, 1, 3).reshape(n * 128, D)
    four = pieces.reshape(n, 4, 32, D).transpose(0, 2, 1, 3).reshape(n * 128, D)
    p = first + lax.broadcasted_iota(jnp.int32, (n * 128, 1), 0) // 128
    return jnp.where(p < 24, three, jnp.where((p >= 32) & (p < 64), four, plain))


def update(params, moment_one, moment_two, weight_grad, square_sum):
    clip_factor = jnp.minimum(1.0, max_norm / (jnp.sqrt(square_sum) + 1e-06))
    clipped = clip_factor * weight_grad
    moment_one_new = beta_one * moment_one + (1.0 - beta_one) * clipped
    moment_two_new = beta_two * moment_two + (1.0 - beta_two) * clipped * clipped
    correct_one = 1.0 - beta_one**STEP
    correct_two = 1.0 - beta_two**STEP
    params_new = params - learn_rate * (
        moment_one_new / correct_one / (jnp.sqrt(moment_two_new / correct_two) + adam_eps) + decay_rate * params
    )
    return params_new, moment_one_new, moment_two_new


def shards(tokens, cotangent, params, moment_one, moment_two):
    n = lax.axis_size("dp")
    me = lax.axis_index("dp")
    shard_len = params.shape[0]
    images_all = tokens.shape[0] * n
    mats = PIECES * 128 * D
    quick = n == 32
    if quick:
        unit = 128
        extra = 12 * D // unit
        own_units = shard_len // unit
        gap = extra // n
        low = params.reshape(own_units, unit)
        before = lax.ppermute(low[own_units - extra :].astype(BF), "dp", [(i, (i + 1) % n) for i in range(n)])
        joined = jnp.concatenate([before.astype(F32), low], axis=0)
        aligned = lax.dynamic_slice(joined, (extra - gap * me, 0), (own_units - gap, unit))
        own = to_pieces(aligned.reshape(-1, D), 3 * me).astype(BF)
        vec_own = low[own_units - extra :].reshape(12, D).astype(BF).astype(F32)
        vec = lax.psum(jnp.where(me == n - 1, vec_own, 0.0), "dp")
        w = gather(own)
    else:
        flat = lax.all_gather(params.astype(BF), "dp", axis=0, tiled=True)
        w = to_pieces(flat[:mats].reshape(-1, D), 0)
        vec = flat[mats:].reshape(12, D).astype(F32)
    vec = jnp.pad(vec, ((0, 4), (0, 0)))
    z, n1 = qkv(tokens, vec, w)
    mixed = attend(z)
    outputs, gup, gdn, gout, dmix, dhid, gvec = mlp(tokens, cotangent, mixed, vec, w)
    dz = attend_back(z, dmix)
    grad_tokens, gqkv, gvec = tail(tokens, dz, n1, dhid, vec, w, gvec)
    parts = [gqkv.reshape(24, 128, D), gout, gup.reshape(32, 128, D), gdn]
    if quick:
        chunk = reduce_(parts, 0, 3, [(0, 24), (24, 32), (32, 64), (64, 96)], 1.0 / images_all)
        gv = lax.psum(gvec[:12], "dp") / images_all
        rows = from_pieces(chunk, 3 * me).reshape(own_units - gap, unit)
        after = lax.ppermute(rows[:extra], "dp", [(i, (i - 1) % n) for i in range(n)])
        after = jnp.where(me == n - 1, gv.reshape(extra, unit), after)
        joined = jnp.concatenate([rows, after], axis=0)
        weight_grad = lax.dynamic_slice(joined, (gap * me, 0), (own_units, unit)).reshape(shard_len)
    else:
        flat = jnp.concatenate([from_pieces(jnp.concatenate(parts, axis=0), 0).reshape(-1), gvec[:12].reshape(-1).astype(BF)])
        arrived = lax.all_to_all(flat.reshape(n, shard_len), "dp", split_axis=0, concat_axis=0, tiled=True)
        weight_grad = jnp.sum(arrived.astype(F32), axis=0) / images_all
    square_sum = lax.psum(jnp.sum(weight_grad * weight_grad), "dp")
    news = update(params, moment_one, moment_two, weight_grad, square_sum)
    return (outputs, grad_tokens, weight_grad, *news)


def solution(mesh):
    in_specs = (P("dp", None, None), P("dp", None, None), P("dp"), P("dp"), P("dp"))
    out_specs = (P("dp", None, None), P("dp", None, None), P("dp"), P("dp"), P("dp"), P("dp"))
    return jax.shard_map(shards, mesh=mesh, in_specs=in_specs, out_specs=out_specs, check_vma=False)
```

```python
import functools

import jax
import jax.numpy as jnp
from jax import lax
from jax.experimental import pallas as pl
from jax.experimental.pallas import tpu as pltpu
from jax.sharding import PartitionSpec as P

D = 1024
FF = 4096
S = 577
SQ = 592
M = 2 * SQ
CH = 32
PIECES = 96
STEP = 4
BF = jnp.bfloat16
F32 = jnp.float32
MESH = pl.DeviceIdType.MESH
VMEM_ALL = 67043328
EARLY = 1
PER = 2
FRONT_HI = 3
BPER = 3

EPS = 1e-06
max_norm = 1.0
beta_one = 0.9
beta_two = 0.95
learn_rate = 0.02
decay_rate = 0.05
adam_eps = 1e-08
SCORE = 0.125 * 1.4426950408889634


def nt(a, b):
    return lax.dot_general(a, b, (((1,), (1,)), ((), ())), preferred_element_type=F32)


def nn(a, b):
    return jnp.dot(a, b, preferred_element_type=F32)


def tn(a, b):
    return lax.dot_general(a, b, (((0,), (0,)), ((), ())), preferred_element_type=F32)


def rows_at(c):
    return pl.ds(pl.multiple_of(c * CH, CH), CH)


def full(shape):
    return pl.BlockSpec(shape, lambda *_: (0,) * len(shape), pipeline_mode=pl.Buffered(1))


class Ctx:
    def __init__(s):
        me=lax.axis_index("dp"); s.me=me
        s.core=me%2; s.x=(me//2)%2; s.y=(me//4)%2; s.z=me//8
        s.sib=me+1-2*s.core
        xp=me+2*(1-2*s.x); yp=me+4*(1-2*s.y)
        s.ap=xp+(yp-xp)*s.core
        s.bp=yp+(xp-yp)*s.core
        s.astep=2+2*s.core; s.bstep=4-2*s.core
        s.abit=s.x+(s.y-s.x)*s.core; s.bbit=s.y+(s.x-s.y)*s.core
        s.up=me+8; s.dn=me-8
        s.hasup=s.z<3; s.hasdn=s.z>0
    def barrier(s,extra=None):
        bar=pltpu.get_barrier_semaphore()
        for p in (s.sib,s.ap,s.bp): pl.semaphore_signal(bar,inc=1,device_id=(p,),device_id_type=MESH)
        @pl.when(s.hasup)
        def _(): pl.semaphore_signal(bar,inc=1,device_id=(s.up,),device_id_type=MESH)
        @pl.when(s.hasdn)
        def _(): pl.semaphore_signal(bar,inc=1,device_id=(s.dn,),device_id_type=MESH)
        more=0 if extra is None else extra
        pl.semaphore_wait(bar,3+jnp.where(s.hasup,1,0)+jnp.where(s.hasdn,1,0)+more)
class Gather:
    K = 3

    @staticmethod
    def sems(lo, hi):
        dma = lambda n: pltpu.SemaphoreType.DMA((n,))
        return [dma(3 * 96), dma(24 * (hi - lo + 1)), dma(3)]

    def __init__(s, c, lo, hi, own, w, sems):
        s.c, s.lo, s.hi, s.own, s.w = c, lo, hi, own, w
        s.ssem, s.rsem, s.lsem = sems
        s.ns = 0
        s.pend = []
        s.steps = []
        kinds = (("z", 0), ("a", 1), ("b", 1), ("ba", 2))
        for dist in range(1, 6):
            for k in range(s.K):
                if lo == hi:
                    continue
                for sign in (1, -1):
                    for kind, extra in kinds:
                        dz = dist - extra
                        if dz < 0 or (kind == "z" and dz == 0) or (dz == 0 and sign < 0):
                            continue
                        if (sign > 0 and dz > hi) or (sign < 0 and dz > 3 - lo):
                            continue
                        s.steps.append(functools.partial(s.item, kind, sign * dz, k))
        if lo == hi:
            s.steps = [functools.partial(s.item, kind, None, k) for kind, _ in kinds[:1] for k in range(s.K)]
            s.steps += [functools.partial(s.item, kind, None, k) for k in range(s.K) for kind in ("a", "b")]
            s.steps += [functools.partial(s.item, "ba", None, k) for k in range(s.K)]

    def inside(s, zz):
        return jnp.logical_and(zz >= s.lo, zz <= s.hi)

    def slot(s, dev, k):
        return s.rsem.at[jnp.clip((dev - 8 * s.lo) * s.K + k, 0, 24 * (s.hi - s.lo + 1) - 1)]

    def send(s, src, dev, k, to, *conds):
        i = s.ns
        s.ns += 1
        cp = pltpu.make_async_remote_copy(
            src, s.w.at[dev, k], s.ssem.at[i], s.slot(dev, k), device_id=(to,), device_id_type=MESH
        )
        conds = [f for f in conds if f is not None]
        s.pend.append((i, conds))
        s.when(conds, cp.start)

    @staticmethod
    def when(conds, fn):
        if conds:
            pl.when(functools.reduce(jnp.logical_and, [f() for f in conds]))(fn)
        else:
            fn()

    def mine(s):
        return s.inside(s.c.z)

    def start(s, ks, routes):
        c = s.c
        to = dict(
            dn=(c.dn, lambda: c.hasdn), up=(c.up, lambda: c.hasup), b=(c.bp, None), a=(c.ap, None), s=(c.sib, None)
        )

        @pl.when(s.mine())
        def _():
            for k in ks:
                for r in routes:
                    s.send(s.own.at[k], c.me, k, to[r][0], to[r][1])
                    i, conds = s.pend.pop()
                    s.pend.append((i, conds + [s.mine]))

    def keep(s):
        @pl.when(s.mine())
        def _():
            for k in range(s.K):
                pltpu.make_async_copy(s.own.at[k], s.w.at[s.c.me, k], s.lsem.at[k]).start()

    def keep_wait(s):
        @pl.when(s.mine())
        def _():
            for k in range(s.K):
                pltpu.make_async_copy(s.own.at[k], s.w.at[s.c.me, k], s.lsem.at[k]).wait()

    def wait(s, dev, k):
        r = s.w.at[dev, k]
        pltpu.make_async_copy(r, r, s.slot(dev, k)).wait()

    def item(s, kind, dz, k):
        c = s.c
        if dz is None:
            src = c.me + 8 * (s.lo - c.z)
            valid = (lambda: c.z != s.lo) if kind == "z" else None
        else:
            src = c.me + 8 * dz
            valid = lambda: s.inside(c.z + dz)
        if "a" in kind:
            src = src + c.astep * (1 - 2 * c.abit)
        if "b" in kind:
            src = src + c.bstep * (1 - 2 * c.bbit)

        def body():
            s.wait(src, k)
            r = s.w.at[src, k]
            if kind == "z":
                if (dz is None and s.lo < 3) or (dz is not None and dz < 0):
                    beyond = (lambda: c.z > s.lo) if dz is None and s.lo > 0 else None
                    s.send(r, src, k, c.up, lambda: c.hasup, valid, beyond)
                if (dz is None and s.lo > 0) or (dz is not None and dz > 0):
                    beyond = (lambda: c.z < s.lo) if dz is None and s.lo < 3 else None
                    s.send(r, src, k, c.dn, lambda: c.hasdn, valid, beyond)
            if kind in ("z", "a"):
                s.send(r, src, k, c.bp, valid)
            if kind == "z":
                s.send(r, src, k, c.ap, valid)
            s.send(r, src, k, c.sib, valid)

        s.when([] if valid is None else [valid], body)

    def sibling(s):
        c = s.c

        def one(i, _):
            s.wait(8 * s.lo + 2 * (i // s.K) + 1 - c.core, i % s.K)
            return 0

        lax.fori_loop(0, 4 * (s.hi - s.lo + 1) * s.K, one, 0)

    def sent(s):
        for i, conds in s.pend:
            r = s.w.at[0, 0]
            s.when(conds, pltpu.make_async_copy(r, r, s.ssem.at[i]).wait)


class Vector:
    def __init__(s, c, own, vec, sem):
        s.c, s.own, s.vec, s.sem = c, own, vec, sem
        s.n = 31

    def tell(s):
        bar = pltpu.get_barrier_semaphore()

        @pl.when(s.c.me != s.n)
        def _():
            pl.semaphore_signal(bar, inc=1, device_id=(s.n,), device_id_type=MESH)

    def copy(s, to):
        return pltpu.make_async_remote_copy(
            s.own, s.vec, s.sem.at[to], s.sem.at[s.n], device_id=(to,), device_id_type=MESH
        )

    def start(s):
        @pl.when(s.c.me == s.n)
        def _():
            s.vec[...] = s.own[...]

            def one(i, _):
                s.copy(i).start()
                return 0

            lax.fori_loop(0, s.n, one, 0)

    def wait(s):
        @pl.when(s.c.me != s.n)
        def _():
            pltpu.make_async_copy(s.vec, s.vec, s.sem.at[s.n]).wait()

    def sent(s):
        @pl.when(s.c.me == s.n)
        def _():
            def one(i, _):
                s.copy(i).wait_send()
                return 0

            lax.fori_loop(0, s.n, one, 0)

class Reduce:
    K = 3

    @staticmethod
    def scratch(lo, hi, stage):
        nz = hi - lo + 1
        pieces = lambda n: pltpu.VMEM((n, 128, D), BF)
        dma = lambda n: pltpu.SemaphoreType.DMA((n,))
        sizes = [12 * nz, 6 * nz, 3 * nz, 3 * nz + 3]
        return (
            [pieces(n) for n in sizes]
            + [pieces(stage)]
            + [dma(12 * nz)]
            + [dma(n) for n in sizes]
            + [dma(12 * nz), dma(stage)]
        )

    def __init__(s, c, lo, hi, parts, out, scr, scale, order, direct=False):
        s.c, s.lo, s.hi, s.parts, s.out, s.scale, s.order, s.direct = c, lo, hi, parts, out, scale, order, direct
        s.S, s.B, s.A, s.Z, s.stage, s.sent_s, s.got_s, s.got_b, s.got_a, s.got_z, s.sent, s.loaded = scr
        s.nst = s.stage.shape[0]
        s.nz = hi - lo + 1
        s.later = []
        s.waits = []
        s.steps = [functools.partial(s.item, i) for i in range(len(order))]

    def owner(s, zz, fb, fa, core):
        c = s.c
        astep = 2 + 2 * core
        bstep = 4 - 2 * core
        abit = c.x + (c.y - c.x) * core
        bbit = c.y + (c.x - c.y) * core
        return zz * 8 + core + bstep * (bbit + fb * (1 - 2 * bbit)) + astep * (abit + fa * (1 - 2 * abit))

    def source(s, p, fn):
        if len(s.parts) == 1:
            lo, hi, ref = s.parts[0]
            fn(ref.at[p - lo])
            return
        for lo, hi, ref in s.parts:

            @pl.when(jnp.logical_and(p >= lo, p < hi))
            def _():
                fn(ref.at[jnp.clip(p - lo, 0, hi - lo - 1)])

    def slot(s, zz, fb, fa, k):
        return (((zz - s.lo) * 2 + fb) * 2 + fa) * s.K + k

    def places(s, order=None):
        for kind, zz, fa, k in order or s.order:
            yield zz, 1 if kind == "b" else 0, fa, k

    def zero(s):
        c = s.c

        def clear(n):
            s.Z[n] = jnp.zeros((128, D), BF)

        for n in range(3 * s.nz + 3):
            at_zero = n < 3 * s.nz
            at_three = n >= 3 * s.nz or s.lo + n // 3 < 3
            if at_zero:
                pl.when(c.z == 0)(functools.partial(clear, n))
            if at_three:
                pl.when(c.z == 3)(functools.partial(clear, n))

    def to_sibling(s, order=None):
        c = s.c
        for zz, fb, fa, k in s.places(order):
            n = s.slot(zz, fb, fa, k)

            def go(r, n=n):
                pltpu.make_async_remote_copy(
                    r, s.S.at[n], s.sent_s.at[n], s.got_s.at[n], device_id=(c.sib,), device_id_type=MESH
                ).start()

            s.source(s.owner(zz, fb, fa, 1 - c.core) * s.K + k, go)

    def load(s, i):
        if s.direct or i >= len(s.order):
            return
        (place,) = s.places([s.order[i]])
        n = i % s.nst

        def go(r):
            pltpu.make_async_copy(r, s.stage.at[n], s.loaded.at[n]).start()

        s.source(s.owner(*place[:3], s.c.core) * s.K + place[3], go)

    def prefetch(s):
        for i in range(s.nst - 1):
            s.load(i)

    def flush(s):
        for f in s.later:
            f()
        s.later = []

    @staticmethod
    def wait(ref, sem):
        pltpu.make_async_copy(ref, ref, sem).wait()

    @staticmethod
    def sum(srcs, dst, scale=None):
        def rows(r, _):
            rr = pl.ds(pl.multiple_of(r * 16, 16), 16)
            t = srcs[0][rr, :].astype(F32)
            for q in srcs[1:]:
                t = t + q[rr, :].astype(F32)
            if scale is not None:
                t = t * scale
            dst[rr, :] = t.astype(dst.dtype)
            return 0

        lax.fori_loop(0, 8, rows, 0)

    def item(s, i):
        c, K = s.c, s.K
        kind, zz, fa, k = s.order[i]
        fb = 1 if kind == "b" else 0
        if s.direct:
            lo, hi, ref = s.parts[0]
            own = ref.at[s.owner(zz, fb, fa, c.core) * K + k - lo]
        else:
            own = s.stage.at[i % s.nst]
            s.wait(own, s.loaded.at[i % s.nst])
        s.flush()
        n = s.slot(zz, fb, fa, k)
        out = s.S.at[n]
        srcs = [own, out]
        s.wait(out, s.got_s.at[n])
        bi = ((zz - s.lo) * 2 + fa) * K + k
        ai = zi = (zz - s.lo) * K + k
        z2 = s.nz * K + k
        if kind in "az":
            srcs.append(s.B.at[bi])
            s.wait(s.B.at[bi], s.got_b.at[bi])
        if kind == "z":
            srcs.append(s.A.at[ai])
            s.wait(s.A.at[ai], s.got_a.at[ai])

        def send(dst, sem, to):
            return pltpu.make_async_remote_copy(
                s.S.at[n], dst, s.sent.at[n], sem, device_id=(to,), device_id_type=MESH
            )

        if kind == "b":
            s.sum(srcs, out)
            s.later.append(send(s.B.at[bi], s.got_b.at[bi], c.bp).start)
            s.waits.append((n, None))
        elif kind == "a":
            s.sum(srcs, out)
            s.later.append(send(s.A.at[ai], s.got_a.at[ai], c.ap).start)
            s.waits.append((n, None))
        else:
            comes = jnp.where(c.z <= zz, c.z, 3 - c.z)
            pl.when(comes > 0)(functools.partial(s.wait, s.Z.at[zi], s.got_z.at[zi]))
            srcs.append(s.Z.at[zi])

            @pl.when(c.z != zz)
            def _():
                s.sum(srcs, out)

            @pl.when(c.z == zz)
            def _():
                pl.when(c.hasup)(functools.partial(s.wait, s.Z.at[z2], s.got_z.at[z2]))
                s.sum(srcs + [s.Z.at[z2]], s.out.at[k], s.scale)

            def on():
                @pl.when(c.z < zz)
                def _():
                    send(s.Z.at[zi], s.got_z.at[zi], c.up).start()

                to = jnp.where(c.z == zz + 1, z2, zi)

                @pl.when(c.z > zz)
                def _():
                    send(s.Z.at[to], s.got_z.at[to], c.dn).start()

            s.later.append(on)
            s.waits.append((n, zz))
        s.load(i + s.nst - 1)

    def finish(s):
        s.flush()
        for n, zz in s.waits:
            w = functools.partial(s.wait, s.S.at[0], s.sent.at[n])
            if zz is None:
                w()
            else:
                pl.when(s.c.z != zz)(w)

        def one(i, _):
            s.wait(s.S.at[0], s.sent_s.at[i])
            return 0

        lax.fori_loop(0, 12 * s.nz, one, 0)


def reduce_order(lo, hi):
    order = []
    planes = list(range(hi, lo - 1, -1))
    b = lambda zz: [("b", zz, fa, k) for fa in (1, 0) for k in range(3)]
    a = lambda zz: [("a", zz, 1, k) for k in range(3)]
    z = lambda zz: [("z", zz, 0, k) for k in range(3)]
    for i in range(len(planes) + 2):
        if i < len(planes):
            order += b(planes[i])
        if 1 <= i <= len(planes):
            order += a(planes[i - 1])
        if i >= 2:
            order += z(planes[i - 2])
    return order


def qkv_kernel(x_ref, vec_ref, w_ref, out_ref, n_ref):
    j = pl.program_id(0)

    @pl.when(j == 0)
    def _():
        for i in range(2):

            def block(rows, dst):
                v = x_ref[i, rows, :].astype(F32)
                c = v - jnp.mean(v, axis=1, keepdims=True)
                rc = lax.rsqrt(jnp.mean(c * c, axis=1, keepdims=True) + EPS)
                return (c * rc * (1.0 + vec_ref[8:9, :]) + vec_ref[9:10, :]).astype(BF)

            def one(c, _):
                n_ref[i, rows_at(c), :] = block(rows_at(c), None)
                return 0

            lax.fori_loop(0, 18, one, 0)
            last = block(slice(576, 577), None).astype(F32)
            n_ref[i, 576:592, :] = jnp.concatenate([last, jnp.zeros((15, D), F32)], axis=0).astype(BF)

    w = w_ref[...].reshape(D, D)
    bias = jnp.where(j == 0, vec_ref[0:1, :], jnp.where(j == 2, vec_ref[1:2, :], 0.0))
    for i in range(2):
        out_ref[0, i] = (nn(n_ref[i], w) + bias).astype(BF)


def qkv(x, vec, w):
    return pl.pallas_call(
        qkv_kernel,
        grid=(3,),
        in_specs=[full((2, S, D)), full((16, D)), pl.BlockSpec((8, 1, 128, D), lambda j: (0, j, 0, 0))],
        out_specs=[pl.BlockSpec((1, 2, SQ, D), lambda j: (j, 0, 0, 0)), full((2, SQ, D))],
        out_shape=[jax.ShapeDtypeStruct((3, 2, SQ, D), BF), jax.ShapeDtypeStruct((2, SQ, D), BF)],
        compiler_params=pltpu.CompilerParams(vmem_limit_bytes=VMEM_ALL),
        name="qkv",
    )(x, vec, w.reshape(32, 3, 128, D))


def padded(v):
    return jnp.concatenate([v, jnp.zeros((640 - SQ, 128), v.dtype)], axis=0)


def attend_pair(q, k, v):
    lane = lax.broadcasted_iota(jnp.int32, (1, 128), 1)
    k = padded(k)
    v = padded(v)
    outs = []
    for h in range(2):
        mine = lane < 64 if h == 0 else lane >= 64
        s = nt(jnp.where(mine, q, jnp.zeros_like(q)), k)
        s = jnp.concatenate([s[:, :512], jnp.where(lane < S - 512, s[:, 512:], -1e30)], axis=1)
        top = jnp.max(s, axis=1, keepdims=True)
        p = jnp.exp2((s - top) * SCORE)
        total = jnp.sum(p, axis=1, keepdims=True)
        outs.append(nn(p.astype(BF), v) * (1.0 / total))
    return jnp.where(lane < 64, outs[0], outs[1]).astype(BF)


def attend_kernel(q_ref, k_ref, v_ref, o_ref):
    half = SQ // 2
    for r in range(2):
        rows = slice(r * half, (r + 1) * half)
        o_ref[0, rows, :] = attend_pair(q_ref[0, 0, rows, :], k_ref[0, 0], v_ref[0, 0])


def attend(z):
    spec = lambda j: pl.BlockSpec((1, 1, SQ, 128), lambda i, h: (j, i, 0, h))
    return pl.pallas_call(
        attend_kernel,
        grid=(2, 8),
        in_specs=[spec(0), spec(1), spec(2)],
        out_specs=pl.BlockSpec((1, SQ, 128), lambda i, h: (i, 0, h)),
        out_shape=jax.ShapeDtypeStruct((2, SQ, D), BF),
        compiler_params=pltpu.CompilerParams(vmem_limit_bytes=VMEM_ALL),
        name="attend",
    )(z, z, z)


def norm_block(v, vec_ref):
    v = v.astype(F32)
    ce = v - jnp.mean(v, axis=1, keepdims=True)
    rc = lax.rsqrt(jnp.mean(ce * ce, axis=1, keepdims=True) + EPS)
    return (ce * rc * (1.0 + vec_ref[8:9, :]) + vec_ref[9:10, :]).astype(BF)


def norm_one(x_ref, vec_ref, n_ref):
    for i in range(2):

        def one(c, _):
            n_ref[i, rows_at(c), :] = norm_block(x_ref[i, rows_at(c), :], vec_ref)
            return 0

        lax.fori_loop(0, 18, one, 0)
        last = norm_block(x_ref[i, 576:577, :], vec_ref).astype(F32)
        n_ref[i, 576:592, :] = jnp.concatenate([last, jnp.zeros((15, D), F32)], axis=0).astype(BF)


def front_kernel(own, vec_own, x_ref, w, vec, z_ref, n_ref, mix_ref, vlow, wq, qsem, vsem, *sems):
    c = Ctx()
    zero = Gather(c, 0, 0, own, w, sems[:3])
    rest = Gather(c, 1, FRONT_HI, own, w, sems[3:])
    vector = Vector(c, vec_own, vlow, vsem)
    vector.tell()
    c.barrier(jnp.where(c.me == 31, 31, 0))
    vector.start()
    zero.start((0, 1, 2), ("up", "b", "a", "s"))
    rest.start((0, 1, 2), ("dn",))
    rest.start(range(EARLY), ("b", "a"))
    rest.start((0, 1, 2), ("s",))
    zero.keep()
    rest.keep()
    for step in zero.steps[:3]:
        step()
    for step in zero.steps[3:]:
        step()
    rest.start((0, 1, 2), ("up",))
    rest.start(range(EARLY, 3), ("b", "a"))
    zero.keep_wait()
    zero.sibling()
    loads = [pltpu.make_async_copy(w.at[0:8, j], wq.at[j % 2], qsem.at[j]) for j in range(3)]
    loads[0].start()
    loads[1].start()
    vector.wait()
    vec[...] = vlow[...].astype(F32)
    norm_one(x_ref, vec, n_ref)
    per = PER
    steps = list(rest.steps)
    for j in range(3):
        for step in steps[:per]:
            step()
        steps = steps[per:]
        loads[j].wait()
        for i in range(2):
            r = nn(n_ref[i], wq[j % 2].reshape(D, D))
            if j != 1:
                r = r + vec[j // 2 : j // 2 + 1, :]
            z_ref[j, i] = r.astype(BF)
        if j == 0:
            loads[2].start()

    def pair(t, _):
        for n in range(16):
            if steps[n * per : (n + 1) * per]:

                @pl.when(t == n)
                def _():
                    for step in steps[n * per : (n + 1) * per]:
                        step()

        i = t // 8
        cols = pl.ds(pl.multiple_of((t % 8) * 128, 128), 128)
        half = SQ // 2
        k = z_ref[1, i, :, cols]
        v = z_ref[2, i, :, cols]
        for r in range(2):
            rows = slice(r * half, (r + 1) * half)
            mix_ref[i, rows, cols] = attend_pair(z_ref[0, i, rows, cols], k, v)
        return 0

    lax.fori_loop(0, 16, pair, 0)
    for step in steps[16 * per :]:
        step()
    rest.sibling()
    rest.keep_wait()
    zero.sent()
    rest.sent()
    vector.sent()


def front(own, vec_own, x):
    vm = pl.BlockSpec(memory_space=pltpu.VMEM)
    dma = lambda n: pltpu.SemaphoreType.DMA((n,))
    return pl.pallas_call(
        front_kernel,
        in_specs=[vm, vm, vm],
        out_specs=[pl.BlockSpec(memory_space=pl.ANY), vm, vm, vm, vm],
        out_shape=[
            jax.ShapeDtypeStruct((32, 3, 128, D), BF),
            jax.ShapeDtypeStruct((16, D), F32),
            jax.ShapeDtypeStruct((3, 2, SQ, D), BF),
            jax.ShapeDtypeStruct((2, SQ, D), BF),
            jax.ShapeDtypeStruct((2, SQ, D), BF),
        ],
        scratch_shapes=[pltpu.VMEM((16, D), BF), pltpu.VMEM((2, 8, 128, D), BF), dma(3), dma(32)]
        + Gather.sems(0, 0)
        + Gather.sems(1, FRONT_HI),
        compiler_params=pltpu.CompilerParams(collective_id=1, has_side_effects=True, vmem_limit_bytes=VMEM_ALL),
        name="front",
    )(own, vec_own, x)


def attend_back_pair(q, k, v, do):
    lane = lax.broadcasted_iota(jnp.int32, (1, 128), 1)
    real = lax.broadcasted_iota(jnp.int32, (16, 1), 0) < S - 576
    q = padded(q)
    do = padded(do)
    dqs, dks, dvs = [], [], []
    for h in range(2):
        mine = lane < 64 if h == 0 else lane >= 64
        s = nt(jnp.where(mine, k, jnp.zeros_like(k)), q)
        s = jnp.concatenate([s[:576], jnp.where(real, s[576:], -1e30)], axis=0)
        top = jnp.max(s, axis=0, keepdims=True)
        p = jnp.exp2((s - top) * SCORE)
        p = p * (1.0 / jnp.sum(p, axis=0, keepdims=True))
        dvs.append(nn(p.astype(BF), do))
        dp = nt(jnp.where(mine, v, jnp.zeros_like(v)), do)
        ds = (p * (dp - jnp.sum(p * dp, axis=0, keepdims=True))).astype(BF)
        dks.append(nn(ds, q))
        dqs.append(tn(ds, k))
    pick = lambda pair, scale: (jnp.where(lane < 64, pair[0], pair[1]) * scale).astype(BF)
    return pick(dqs, 0.125)[:SQ], pick(dks, 0.125), pick(dvs, 1.0)


def attend_back_kernel(q_ref, k_ref, v_ref, do_ref, out_ref):
    dq, dk, dv = attend_back_pair(q_ref[0, 0], k_ref[0, 0], v_ref[0, 0], do_ref[0])
    out_ref[0, 0] = dq
    out_ref[1, 0] = dk
    out_ref[2, 0] = dv


def attend_back(z, do):
    spec = lambda j: pl.BlockSpec((1, 1, SQ, 128), lambda i, h: (j, i, 0, h))
    return pl.pallas_call(
        attend_back_kernel,
        grid=(2, 8),
        in_specs=[spec(0), spec(1), spec(2), pl.BlockSpec((1, SQ, 128), lambda i, h: (i, 0, h))],
        out_specs=pl.BlockSpec((3, 1, SQ, 128), lambda i, h: (0, i, 0, h)),
        out_shape=jax.ShapeDtypeStruct((3, 2, SQ, D), BF),
        compiler_params=pltpu.CompilerParams(vmem_limit_bytes=VMEM_ALL),
        name="attend_back",
    )(z, z, z, do)


def mlp_kernel(x_ref,g_ref,mix_ref,vec_ref,wo_ref,wu_ref,wd_ref,
               out_ref,gup_ref,gdn_ref,gout_ref,dmix_ref,dhid_ref,gvec_ref,
               n2,gs,acc,dn,stat,*,FB,NB):
    jb=pl.program_id(0)
    hid=dhid_ref
    @pl.when(jb==0)
    def _():
        wo=wo_ref[...].reshape(D,D)
        for i in range(2):
            hid[i*SQ:(i+1)*SQ,:]=nn(mix_ref[i],wo)
            gs[i*SQ:i*SQ+576,:]=g_ref[i,:576,:]
            gs[i*SQ+576:(i+1)*SQ,:]=jnp.concatenate([g_ref[i,576:577,:].astype(F32),jnp.zeros((15,D),F32)],axis=0).astype(BF)
            def addx(c,_):
                r=pl.multiple_of(c*CH,CH)
                hid[pl.ds(i*SQ+r,CH),:]+=x_ref[i,pl.ds(r,CH),:].astype(F32)+vec_ref[2:3,:]
                return 0
            lax.fori_loop(0,18,addx,0)
            hid[i*SQ+576:i*SQ+577,:]+=x_ref[i,576:577,:].astype(F32)+vec_ref[2:3,:]
        acc[...]=jnp.zeros_like(acc); dn[...]=jnp.zeros_like(dn)
        gvec_ref[...]=jnp.zeros_like(gvec_ref)
        def ln(c,_):
            r=pl.ds(pl.multiple_of(c*CH,CH),CH)
            h=hid[r,:]
            mu=jnp.mean(h,axis=1,keepdims=True)
            ce=h-mu
            rc=lax.rsqrt(jnp.mean(ce*ce,axis=1,keepdims=True)+EPS)
            n2[r,:]=(ce*rc*(1.0+vec_ref[10:11,:])+vec_ref[11:12,:]).astype(BF)
            stat[r,0:1]=mu; stat[r,1:2]=rc
            return 0
        lax.fori_loop(0,M//CH,ln,0)
        def gsum(c,a):
            r=pl.ds(pl.multiple_of(c*CH,CH),CH)
            return a+gs[r,:].astype(F32)
        t=lax.fori_loop(0,M//CH,gsum,jnp.zeros((CH,D),F32))
        gvec_ref[7:8,:]=jnp.sum(t,axis=0,keepdims=True)
    wu=wu_ref[...].reshape(D,FB); wd=wd_ref[...].reshape(FB,D)
    nper=D//FB
    row=vec_ref[pl.ds(3+jb//nper,1),:]
    bup=row[:,:FB]
    for t in range(1,nper): bup=jnp.where(jb%nper==t,row[:,t*FB:(t+1)*FB],bup)
    g=gs[...]; n=n2[...]
    pre=nn(n,wu)+bup
    cdf=0.5*(1.0+lax.erf(pre*0.7071067811865476))
    act=(pre*cdf).astype(BF)
    slope=cdf+pre*0.3989422804014327*jnp.exp(-0.5*pre*pre)
    dpf=nt(g,wd)*slope
    dp=dpf.astype(BF)
    acc[...]+=nn(act,wd)
    dn[...]+=nt(dp,wu)
    gup_ref[...]=tn(n,dp).astype(BF).reshape(gup_ref.shape)
    gdn_ref[...]=tn(act,g).astype(BF).reshape(gdn_ref.shape)
    bsum=jnp.sum(dp.astype(F32),axis=0,keepdims=True)
    for t in range(nper):
        @pl.when(jb%nper==t)
        def _(): gvec_ref[pl.ds(3+jb//nper,1),t*FB:(t+1)*FB]=bsum
    @pl.when(jb==NB-1)
    def _():
        for i in range(2):
            def ob(c,_):
                r=pl.multiple_of(c*CH,CH)
                out_ref[i,pl.ds(r,CH),:]=(hid[pl.ds(i*SQ+r,CH),:]+(acc[pl.ds(i*SQ+r,CH),:]+vec_ref[7:8,:])).astype(BF)
                return 0
            lax.fori_loop(0,18,ob,0)
            out_ref[i,576:577,:]=(hid[i*SQ+576:i*SQ+577,:]+(acc[i*SQ+576:i*SQ+577,:]+vec_ref[7:8,:])).astype(BF)
        def bk(c,car):
            a,b,d=car
            r=pl.ds(pl.multiple_of(c*CH,CH),CH)
            mu=stat[r,0:1]; rc=stat[r,1:2]
            xh=(hid[r,:]-mu)*rc
            dd=dn[r,:]
            e=dd*(1.0+vec_ref[10:11,:])
            dh=gs[r,:].astype(F32)+rc*(e-jnp.mean(e,axis=1,keepdims=True)-xh*jnp.mean(e*xh,axis=1,keepdims=True))
            dhid_ref[r,:]=dh
            db=dh.astype(BF)
            n2[r,:]=db
            return (a+dd*xh,b+dd,d+db.astype(F32))
        zz=jnp.zeros((CH,D),F32)
        a,b,d=lax.fori_loop(0,M//CH,bk,(zz,zz,zz))
        gvec_ref[10:11,:]=jnp.sum(a,axis=0,keepdims=True)
        gvec_ref[11:12,:]=jnp.sum(b,axis=0,keepdims=True)
        gvec_ref[2:3,:]=jnp.sum(d,axis=0,keepdims=True)
        db=n2[...]
        wo=wo_ref[...].reshape(D,D)
        dmix_ref[...]=nt(db,wo).astype(BF).reshape(2,SQ,D)
        gout_ref[...]=tn(mix_ref[...].reshape(M,D),db).astype(BF).reshape(8,128,D)
def mlp(x,g,mix,vec,W,FB=512):
    NB=4096//FB; nper=D//FB
    W4=W.reshape(96,4,32,1024)
    return pl.pallas_call(functools.partial(mlp_kernel,FB=FB,NB=NB),grid=(NB,),
      in_specs=[full((2,S,D)),full((2,S,D)),full((2,SQ,D)),full((16,D)),
        pl.BlockSpec((8,128,D),lambda j:(3,0,0),pipeline_mode=pl.Buffered(1)),
        pl.BlockSpec((32,1,32,FB),lambda j:(1,j//nper,0,j%nper)),
        pl.BlockSpec((FB//128,128,D),lambda j:(64//(FB//128)+j,0,0))],
      out_specs=[full((2,S,D)),pl.BlockSpec((32,1,32,FB),lambda j:(0,j//nper,0,j%nper)),
        pl.BlockSpec((FB//128,128,D),lambda j:(j,0,0)),full((8,128,D)),full((2,SQ,D)),full((M,D)),full((16,D))],
      out_shape=[jax.ShapeDtypeStruct((2,S,D),BF),jax.ShapeDtypeStruct((32,4,32,D),BF),jax.ShapeDtypeStruct((32,128,D),BF),
        jax.ShapeDtypeStruct((8,128,D),BF),jax.ShapeDtypeStruct((2,SQ,D),BF),jax.ShapeDtypeStruct((M,D),F32),jax.ShapeDtypeStruct((16,D),F32)],
      scratch_shapes=[pltpu.VMEM((M,D),BF),pltpu.VMEM((M,D),BF),pltpu.VMEM((M,D),F32),pltpu.VMEM((M,D),F32),pltpu.VMEM((M,128),F32)],
      compiler_params=pltpu.CompilerParams(vmem_limit_bytes=67043328),name=f"mlp{FB}")(x,g,mix,vec,W,W4,W)


def tail_kernel(x_ref, dz_ref, n_ref, dhid_ref, vec_ref, w_ref, gvin_ref, gx_ref, gw_ref, gvec_ref, acc):
    j = pl.program_id(0)

    @pl.when(j == 0)
    def _():
        gvec_ref[...] = gvin_ref[...]
        acc[...] = jnp.zeros_like(acc)

    w = w_ref[...].reshape(D, D)
    dz = dz_ref[0].reshape(M, D)
    acc[...] += nt(dz, w)
    gw_ref[...] = tn(n_ref[...].reshape(M, D), dz).astype(BF).reshape(8, 1, 128, D)

    @pl.when(j != 1)
    def _():
        def add(c, t):
            return t + dz_ref[0, 0, pl.ds(c * 16, 16), :].astype(F32) + dz_ref[0, 1, pl.ds(c * 16, 16), :].astype(F32)

        t = lax.fori_loop(0, SQ // 16, add, jnp.zeros((16, D), F32))
        gvec_ref[pl.ds(j // 2, 1), :] = jnp.sum(t, axis=0, keepdims=True)

    @pl.when(j == 2)
    def _():
        def back(x, dd, dh):
            v = x.astype(F32)
            ce = v - jnp.mean(v, axis=1, keepdims=True)
            rc = lax.rsqrt(jnp.mean(ce * ce, axis=1, keepdims=True) + EPS)
            xh = ce * rc
            e = dd * (1.0 + vec_ref[8:9, :])
            g = dh + rc * (e - jnp.mean(e, axis=1, keepdims=True) - xh * jnp.mean(e * xh, axis=1, keepdims=True))
            return g.astype(BF), dd * xh, dd

        a = b = jnp.zeros((CH, D), F32)
        la = lb = jnp.zeros((1, D), F32)
        for i in range(2):

            def one(c, carry):
                r = rows_at(c)
                r2 = pl.ds(pl.multiple_of(i * SQ + c * CH, 16), CH)
                g, s1, s2 = back(x_ref[i, r, :], acc[r2, :], dhid_ref[r2, :])
                gx_ref[i, r, :] = g
                return carry[0] + s1, carry[1] + s2

            a, b = lax.fori_loop(0, 18, one, (a, b))
            r2 = slice(i * SQ + 576, i * SQ + 577)
            g, s1, s2 = back(x_ref[i, 576:577, :], acc[r2, :], dhid_ref[r2, :])
            gx_ref[i, 576:577, :] = g
            la, lb = la + s1, lb + s2
        gvec_ref[8:9, :] = jnp.sum(a, axis=0, keepdims=True) + la
        gvec_ref[9:10, :] = jnp.sum(b, axis=0, keepdims=True) + lb


def tail(x, dz, n1, dhid, vec, w, gvec):
    return pl.pallas_call(
        tail_kernel,
        grid=(3,),
        in_specs=[
            full((2, S, D)),
            pl.BlockSpec((1, 2, SQ, D), lambda j: (j, 0, 0, 0)),
            full((2, SQ, D)),
            full((M, D)),
            full((16, D)),
            pl.BlockSpec((8, 1, 128, D), lambda j: (0, j, 0, 0)),
            full((16, D)),
        ],
        out_specs=[full((2, S, D)), pl.BlockSpec((8, 1, 128, D), lambda j: (0, j, 0, 0)), full((16, D))],
        out_shape=[
            jax.ShapeDtypeStruct((2, S, D), BF),
            jax.ShapeDtypeStruct((8, 3, 128, D), BF),
            jax.ShapeDtypeStruct((16, D), F32),
        ],
        scratch_shapes=[pltpu.VMEM((M, D), F32)],
        compiler_params=pltpu.CompilerParams(vmem_limit_bytes=VMEM_ALL),
        name="tail",
    )(x, dz, n1, dhid, vec, w.reshape(32, 3, 128, D), gvec)

def back_kernel(z_ref, do_ref, *refs, lo, hi, ranges, scale, per):
    n = len(ranges)
    parts = [(a, b, r) for (a, b), r in zip(ranges, refs[:n])]
    dz_ref, chunk = refs[n : n + 2]
    c = Ctx()
    order = reduce_order(lo, hi)
    red = Reduce(c, lo, hi, parts, chunk, refs[n + 2 :], scale, order)
    red.zero()
    chunk[...] = jnp.zeros_like(chunk)
    c.barrier()
    red.to_sibling()
    red.prefetch()

    def pair(t, _):
        for m in range(16):
            if red.steps[m * per : (m + 1) * per]:

                @pl.when(t == m)
                def _():
                    for step in red.steps[m * per : (m + 1) * per]:
                        step()
                    red.flush()

        i = t // 8
        cols = pl.ds(pl.multiple_of((t % 8) * 128, 128), 128)
        dq, dk, dv = attend_back_pair(z_ref[0, i, :, cols], z_ref[1, i, :, cols], z_ref[2, i, :, cols], do_ref[i, :, cols])
        dz_ref[0, i, :, cols] = dq
        dz_ref[1, i, :, cols] = dk
        dz_ref[2, i, :, cols] = dv
        return 0

    lax.fori_loop(0, 16, pair, 0)
    for step in red.steps[16 * per :]:
        step()
    red.finish()


def back(z, do, parts, lo, hi, ranges, scale, per=BPER):
    vm = pl.BlockSpec(memory_space=pltpu.VMEM)
    return pl.pallas_call(
        functools.partial(back_kernel, lo=lo, hi=hi, ranges=ranges, scale=scale, per=per),
        in_specs=[vm, vm] + [pl.BlockSpec(memory_space=pl.ANY)] * len(parts),
        out_specs=[vm, vm],
        out_shape=[jax.ShapeDtypeStruct((3, 2, SQ, D), BF), jax.ShapeDtypeStruct((3, 128, D), F32)],
        scratch_shapes=Reduce.scratch(lo, hi, 4),
        compiler_params=pltpu.CompilerParams(collective_id=2, has_side_effects=True, vmem_limit_bytes=VMEM_ALL),
        name="back",
    )(z, do, *parts)


def back_norm(x, dd, dh, vec_ref):
    v = x.astype(F32)
    ce = v - jnp.mean(v, axis=1, keepdims=True)
    rc = lax.rsqrt(jnp.mean(ce * ce, axis=1, keepdims=True) + EPS)
    xh = ce * rc
    e = dd * (1.0 + vec_ref[8:9, :])
    g = dh + rc * (e - jnp.mean(e, axis=1, keepdims=True) - xh * jnp.mean(e * xh, axis=1, keepdims=True))
    return g.astype(BF), dd * xh


def tail_quick_kernel(
    x_ref, dz_ref, n_ref, dhid_ref, vec_ref, gvin_ref, w, gx_ref, chunk, gvec_ref, acc, gw, wq, qsem, *scr, scale
):
    c = Ctx()
    order = [(kind, 0, fa, k) for k in range(3) for kind, fa in (("b", 1), ("b", 0), ("a", 1), ("z", 0))]
    red = Reduce(c, 0, 0, [(0, 24, gw)], chunk, scr, scale, order, direct=True)
    loads = [pltpu.make_async_copy(w.at[0:8, j], wq.at[j % 2], qsem.at[j]) for j in range(3)]
    loads[0].start()
    loads[1].start()
    red.zero()
    chunk[...] = jnp.zeros_like(chunk)
    gvec_ref[...] = gvin_ref[...]
    c.barrier()
    queue = list(red.steps)

    def take(*ids):
        for i in ids:
            queue[i]()

    def weights(j):
        g = tn(n_ref[...].reshape(M, D), dz_ref[j].reshape(M, D)).astype(BF)
        for d in range(8):
            gw[3 * d + j] = g[128 * d : 128 * (d + 1)]

    def colsum(j):
        def add(r, t):
            rr = pl.ds(pl.multiple_of(r * 16, 16), 16)
            return t + dz_ref[j, 0, rr, :].astype(F32) + dz_ref[j, 1, rr, :].astype(F32)

        t = lax.fori_loop(0, SQ // 16, add, jnp.zeros((16, D), F32))
        gvec_ref[j // 2 : j // 2 + 1, :] = jnp.sum(t, axis=0, keepdims=True)

    def inputs(j):
        loads[j].wait()
        wj = wq[j % 2].reshape(D, D)
        for i in range(2):
            r = nt(dz_ref[j, i], wj)
            rows = slice(i * SQ, (i + 1) * SQ)
            acc[rows, :] = r if j == 0 else acc[rows, :] + r

    some = lambda k: [o for o in order if o[3] == k]
    weights(0)
    colsum(0)
    red.to_sibling(some(0))
    weights(1)
    red.to_sibling(some(1))
    take(0, 1)
    weights(2)
    take(4, 5, 2)
    red.to_sibling(some(2))
    inputs(0)
    loads[2].start()
    take(8, 9, 6, 3)
    red.flush()
    inputs(1)
    take(10, 7)
    red.flush()
    inputs(2)
    take(11)
    red.flush()
    colsum(2)
    a = b = jnp.zeros((CH, D), F32)
    la = lb = jnp.zeros((1, D), F32)
    for i in range(2):

        def one(t, carry):
            r = rows_at(t)
            r2 = pl.ds(pl.multiple_of(i * SQ + t * CH, 16), CH)
            dd = acc[r2, :]
            g, s1 = back_norm(x_ref[i, r, :], dd, dhid_ref[r2, :], vec_ref)
            gx_ref[i, r, :] = g
            return carry[0] + s1, carry[1] + dd

        a, b = lax.fori_loop(0, 18, one, (a, b))
        r2 = slice(i * SQ + 576, i * SQ + 577)
        dd = acc[r2, :]
        g, s1 = back_norm(x_ref[i, 576:577, :], dd, dhid_ref[r2, :], vec_ref)
        gx_ref[i, 576:577, :] = g
        la, lb = la + s1, lb + dd
    gvec_ref[8:9, :] = jnp.sum(a, axis=0, keepdims=True) + la
    gvec_ref[9:10, :] = jnp.sum(b, axis=0, keepdims=True) + lb
    red.finish()


def tail_quick(x, dz, n1, dhid, vec, gvec, w, scale):
    vm = pl.BlockSpec(memory_space=pltpu.VMEM)
    return pl.pallas_call(
        functools.partial(tail_quick_kernel, scale=scale),
        in_specs=[vm] * 6 + [pl.BlockSpec(memory_space=pl.ANY)],
        out_specs=[vm] * 3,
        out_shape=[
            jax.ShapeDtypeStruct((2, S, D), BF),
            jax.ShapeDtypeStruct((3, 128, D), F32),
            jax.ShapeDtypeStruct((16, D), F32),
        ],
        scratch_shapes=[
            pltpu.VMEM((M, D), F32),
            pltpu.VMEM((24, 128, D), BF),
            pltpu.VMEM((2, 8, 128, D), BF),
            pltpu.SemaphoreType.DMA((3,)),
        ]
        + Reduce.scratch(0, 0, 1),
        compiler_params=pltpu.CompilerParams(collective_id=3, has_side_effects=True, vmem_limit_bytes=VMEM_ALL),
        name="tail_quick",
    )(x, dz, n1, dhid, vec, gvec, w)


def close_kernel(chunk_a, chunk_b, gvec, p_ref, m_ref, v_ref, wg, pn, mn, vn, flat, e, es, ea, eb, ez, sem, *, scale):
    c = Ctx()
    me = c.me
    bar = pltpu.get_barrier_semaphore()
    others = [c.sib, c.ap, c.bp] + [lax.rem(me + 8 * i, 32) for i in (1, 2, 3)]
    for to in others:
        pl.semaphore_signal(bar, inc=1, device_id=(to,), device_id_type=MESH)
    first, last = me == 0, me == 31

    @pl.when(jnp.logical_not(first))
    def _():
        pl.semaphore_signal(bar, inc=1, device_id=(me - 1,), device_id_type=MESH)

    @pl.when(jnp.logical_not(last))
    def _():
        pl.semaphore_signal(bar, inc=1, device_id=(me + 1,), device_id_type=MESH)

    def unfold(src, k, kind):
        for t in range(8):
            cols = slice(128 * t, 128 * (t + 1))
            if kind == 0:
                flat[pl.ds(8 * k + t, 128, stride=24), :] = src[k, :, cols]
            elif kind == 1:
                flat[pl.ds(1024 * k + t, 128, stride=8), :] = src[k, :, cols]
            else:
                for j in range(4):
                    flat[pl.ds(1024 * k + 8 * j + t, 32, stride=32), :] = src[k, 32 * j : 32 * j + 32, cols]

    for k in range(3):
        p = 3 * me + k
        up = jnp.logical_and(p >= 32, p < 64)
        pl.when(c.z == 0)(functools.partial(unfold, chunk_b, k, 0))
        pl.when(up)(functools.partial(unfold, chunk_a, k, 2))
        pl.when(jnp.logical_and(c.z > 0, jnp.logical_not(up)))(functools.partial(unfold, chunk_a, k, 1))

    def square(i, t):
        v = flat[pl.ds(pl.multiple_of(i * 64, 64), 64), :]
        return t + v * v

    sq = jnp.sum(lax.fori_loop(0, 48, square, jnp.zeros((64, 128), F32)))
    e[0:16, :] = gvec[...]
    e[16:24, :] = jnp.full((8, D), sq, F32)
    pl.semaphore_wait(bar, 6 + jnp.where(first, 0, 1) + jnp.where(last, 0, 1))
    head = flat.at[0:96]
    room = flat.at[3072:3168]
    edge = pltpu.make_async_remote_copy(
        head, room, sem.at[14], sem.at[15], device_id=(jnp.maximum(me - 1, 0),), device_id_type=MESH
    )
    pl.when(jnp.logical_not(first))(edge.start)
    for n, (to, dst) in enumerate(((c.sib, es), (c.ap, ea), (c.bp, eb))):
        cp = pltpu.make_async_remote_copy(e, dst, sem.at[n], sem.at[3 + n], device_id=(to,), device_id_type=MESH)
        cp.start()
        cp.wait()
        e[...] = e[...] + dst[...]
    ez[c.z] = e[...]
    cps = []
    for i in (1, 2, 3):
        to = lax.rem(me + 8 * i, 32)
        cp = pltpu.make_async_remote_copy(
            e, ez.at[c.z], sem.at[6 + i], sem.at[9 + i], device_id=(to,), device_id_type=MESH
        )
        cp.start()
        cps.append(cp)
    for i in (1, 2, 3):
        cps[i - 1].wait_send()
        zz = lax.rem(c.z + 4 - i, 4)
        pltpu.make_async_copy(ez.at[zz], ez.at[zz], sem.at[9 + i]).wait()
    total = ((ez[0] + ez[1]) + ez[2]) + ez[3]
    vec = total[0:12, :] * scale
    square_sum = total[16:17, 0:1] + jnp.sum(vec * vec)
    clip = jnp.minimum(1.0, max_norm / (jnp.sqrt(square_sum) + 1e-06))

    @pl.when(last)
    def _():
        for t in range(8):
            flat[pl.ds(3072 + t, 12, stride=8), :] = vec[:, 128 * t : 128 * (t + 1)]

    @pl.when(jnp.logical_not(last))
    def _():
        pltpu.make_async_copy(room, room, sem.at[15]).wait()

    pl.when(jnp.logical_not(first))(edge.wait_send)

    def apply(g, rows):
        w = clip * g
        m1 = beta_one * m_ref[rows, :] + (1.0 - beta_one) * w
        m2 = beta_two * v_ref[rows, :] + (1.0 - beta_two) * w * w
        par = p_ref[rows, :]
        step = m1 / (1.0 - beta_one**STEP) / (jnp.sqrt(m2 / (1.0 - beta_two**STEP)) + adam_eps)
        wg[rows, :] = g
        pn[rows, :] = par - learn_rate * (step + decay_rate * par)
        mn[rows, :] = m1
        vn[rows, :] = m2

    def block(i, _):
        apply(flat[pl.ds(i * 64 + 3 * me, 64), :], pl.ds(pl.multiple_of(i * 64, 64), 64))
        return 0

    lax.fori_loop(0, 48, block, 0)
    apply(flat[pl.ds(3072 + 3 * me, 3), :], slice(3072, 3075))


def close(chunk_a, chunk_b, gvec, params, moment_one, moment_two, scale):
    vm = pl.BlockSpec(memory_space=pltpu.VMEM)
    own = jax.ShapeDtypeStruct((3075, 128), F32)
    small = pltpu.VMEM((24, D), F32)
    return pl.pallas_call(
        functools.partial(close_kernel, scale=scale),
        in_specs=[vm] * 6,
        out_specs=[vm] * 4,
        out_shape=[own] * 4,
        scratch_shapes=[pltpu.VMEM((3168, 128), F32)]
        + [small] * 4
        + [pltpu.VMEM((4, 24, D), F32), pltpu.SemaphoreType.DMA((16,))],
        compiler_params=pltpu.CompilerParams(collective_id=4, has_side_effects=True, vmem_limit_bytes=VMEM_ALL),
        name="close",
    )(chunk_a, chunk_b, gvec, *(v.reshape(3075, 128) for v in (params, moment_one, moment_two)))


def to_pieces(rows, first):
    n = rows.shape[0] // 128
    plain = rows.reshape(n, 128, D)
    three = rows.reshape(n // 3, 128, 3, D).transpose(0, 2, 1, 3).reshape(n, 128, D)
    four = rows.reshape(n, 32, 4, D).transpose(0, 2, 1, 3).reshape(n, 128, D)
    p = first + lax.broadcasted_iota(jnp.int32, (n, 1, 1), 0)
    return jnp.where(p < 24, three, jnp.where((p >= 32) & (p < 64), four, plain))


def from_pieces(pieces, first):
    n = pieces.shape[0]
    plain = pieces.reshape(n * 128, D)
    three = pieces.reshape(n // 3, 3, 128, D).transpose(0, 2, 1, 3).reshape(n * 128, D)
    four = pieces.reshape(n, 4, 32, D).transpose(0, 2, 1, 3).reshape(n * 128, D)
    p = first + lax.broadcasted_iota(jnp.int32, (n * 128, 1), 0) // 128
    return jnp.where(p < 24, three, jnp.where((p >= 32) & (p < 64), four, plain))


def update(params, moment_one, moment_two, weight_grad, square_sum):
    clip_factor = jnp.minimum(1.0, max_norm / (jnp.sqrt(square_sum) + 1e-06))
    clipped = clip_factor * weight_grad
    moment_one_new = beta_one * moment_one + (1.0 - beta_one) * clipped
    moment_two_new = beta_two * moment_two + (1.0 - beta_two) * clipped * clipped
    correct_one = 1.0 - beta_one**STEP
    correct_two = 1.0 - beta_two**STEP
    params_new = params - learn_rate * (
        moment_one_new / correct_one / (jnp.sqrt(moment_two_new / correct_two) + adam_eps) + decay_rate * params
    )
    return params_new, moment_one_new, moment_two_new


def shards(tokens, cotangent, params, moment_one, moment_two):
    n = lax.axis_size("dp")
    me = lax.axis_index("dp")
    shard_len = params.shape[0]
    images_all = tokens.shape[0] * n
    mats = PIECES * 128 * D
    scale = 1.0 / images_all
    if n == 32:
        unit = 128
        extra = 12 * D // unit
        own_units = shard_len // unit
        gap = extra // n
        low = params.reshape(own_units, unit)
        before = lax.ppermute(low[own_units - extra :].astype(BF), "dp", [(i, (i + 1) % n) for i in range(n)])
        joined = jnp.concatenate([before.astype(F32), low], axis=0)
        aligned = lax.dynamic_slice(joined, (extra - gap * me, 0), (own_units - gap, unit))
        own = to_pieces(aligned.reshape(-1, D), 3 * me).astype(BF)
        vec_own = jnp.pad(low[own_units - extra :].reshape(12, D), ((0, 4), (0, 0))).astype(BF)
        w, vec, z, n1, mixed = front(own, vec_own, tokens)
        flat_w = w.reshape(PIECES, 128, D)
        outputs, gup, gdn, gout, dmix, dhid, gvec = mlp(tokens, cotangent, mixed, vec, flat_w)
        parts = [gout, gup.reshape(32, 128, D), gdn]
        dz, chunk_a = back(z, dmix, parts, 1, 3, [(24, 32), (32, 64), (64, 96)], scale)
        grad_tokens, chunk_b, gvec = tail_quick(tokens, dz, n1, dhid, vec, gvec, w, scale)
        news = close(chunk_a, chunk_b, gvec, params, moment_one, moment_two, scale)
        return (outputs, grad_tokens, *(v.reshape(shard_len) for v in news))
    flat = lax.all_gather(params.astype(BF), "dp", axis=0, tiled=True)
    w = to_pieces(flat[:mats].reshape(-1, D), 0)
    vec = jnp.pad(flat[mats:].reshape(12, D).astype(F32), ((0, 4), (0, 0)))
    z, n1 = qkv(tokens, vec, w)
    mixed = attend(z)
    outputs, gup, gdn, gout, dmix, dhid, gvec = mlp(tokens, cotangent, mixed, vec, w)
    dz = attend_back(z, dmix)
    grad_tokens, gqkv, gvec = tail(tokens, dz, n1, dhid, vec, w, gvec)
    parts = [gqkv.reshape(24, 128, D), gout, gup.reshape(32, 128, D), gdn]
    flat = jnp.concatenate([from_pieces(jnp.concatenate(parts, axis=0), 0).reshape(-1), gvec[:12].reshape(-1).astype(BF)])
    arrived = lax.all_to_all(flat.reshape(n, shard_len), "dp", split_axis=0, concat_axis=0, tiled=True)
    weight_grad = jnp.sum(arrived.astype(F32), axis=0) * scale
    square_sum = lax.psum(jnp.sum(weight_grad * weight_grad), "dp")
    news = update(params, moment_one, moment_two, weight_grad, square_sum)
    return (outputs, grad_tokens, weight_grad, *news)


def solution(mesh):
    in_specs = (P("dp", None, None), P("dp", None, None), P("dp"), P("dp"), P("dp"))
    out_specs = (P("dp", None, None), P("dp", None, None), P("dp"), P("dp"), P("dp"), P("dp"))
    return jax.shard_map(shards, mesh=mesh, in_specs=in_specs, out_specs=out_specs, check_vma=False)
```

```python
import functools

import jax
import jax.numpy as jnp
from jax import lax
from jax.experimental import pallas as pl
from jax.experimental.pallas import tpu as pltpu
from jax.sharding import PartitionSpec as P

D = 1024
FF = 4096
S = 577
SQ = 592
M = 2 * SQ
CH = 32
PIECES = 96
STEP = 4
BF = jnp.bfloat16
F32 = jnp.float32
MESH = pl.DeviceIdType.MESH
VMEM_ALL = 67043328
EARLY = 1
PER = 2
FRONT_HI = 3

EPS = 1e-06
max_norm = 1.0
beta_one = 0.9
beta_two = 0.95
learn_rate = 0.02
decay_rate = 0.05
adam_eps = 1e-08
SCORE = 0.125 * 1.4426950408889634


def nt(a, b):
    return lax.dot_general(a, b, (((1,), (1,)), ((), ())), preferred_element_type=F32)


def nn(a, b):
    return jnp.dot(a, b, preferred_element_type=F32)


def tn(a, b):
    return lax.dot_general(a, b, (((0,), (0,)), ((), ())), preferred_element_type=F32)


def rows_at(c):
    return pl.ds(pl.multiple_of(c * CH, CH), CH)


def full(shape):
    return pl.BlockSpec(shape, lambda *_: (0,) * len(shape), pipeline_mode=pl.Buffered(1))


class Ctx:
    def __init__(s):
        me=lax.axis_index("dp"); s.me=me
        s.core=me%2; s.x=(me//2)%2; s.y=(me//4)%2; s.z=me//8
        s.sib=me+1-2*s.core
        xp=me+2*(1-2*s.x); yp=me+4*(1-2*s.y)
        s.ap=xp+(yp-xp)*s.core
        s.bp=yp+(xp-yp)*s.core
        s.astep=2+2*s.core; s.bstep=4-2*s.core
        s.abit=s.x+(s.y-s.x)*s.core; s.bbit=s.y+(s.x-s.y)*s.core
        s.up=me+8; s.dn=me-8
        s.hasup=s.z<3; s.hasdn=s.z>0
    def barrier(s,extra=None):
        bar=pltpu.get_barrier_semaphore()
        for p in (s.sib,s.ap,s.bp): pl.semaphore_signal(bar,inc=1,device_id=(p,),device_id_type=MESH)
        @pl.when(s.hasup)
        def _(): pl.semaphore_signal(bar,inc=1,device_id=(s.up,),device_id_type=MESH)
        @pl.when(s.hasdn)
        def _(): pl.semaphore_signal(bar,inc=1,device_id=(s.dn,),device_id_type=MESH)
        more=0 if extra is None else extra
        pl.semaphore_wait(bar,3+jnp.where(s.hasup,1,0)+jnp.where(s.hasdn,1,0)+more)
class Gather:
    K = 3

    @staticmethod
    def sems(lo, hi):
        dma = lambda n: pltpu.SemaphoreType.DMA((n,))
        return [dma(3 * 96), dma(24 * (hi - lo + 1)), dma(3)]

    def __init__(s, c, lo, hi, own, w, sems, base=0):
        s.base = base
        s.c, s.lo, s.hi, s.own, s.w = c, lo, hi, own, w
        s.ssem, s.rsem, s.lsem = sems
        s.ns = 0
        s.pend = []
        s.steps = []
        kinds = (("z", 0), ("a", 1), ("b", 1), ("ba", 2))
        for dist in range(1, 6):
            for k in range(s.K):
                if lo == hi:
                    continue
                for sign in (1, -1):
                    for kind, extra in kinds:
                        dz = dist - extra
                        if dz < 0 or (kind == "z" and dz == 0) or (dz == 0 and sign < 0):
                            continue
                        if (sign > 0 and dz > hi) or (sign < 0 and dz > 3 - lo):
                            continue
                        s.steps.append(functools.partial(s.item, kind, sign * dz, k))
        if lo == hi:
            s.steps = [functools.partial(s.item, kind, None, k) for kind, _ in kinds[:1] for k in range(s.K)]
            s.steps += [functools.partial(s.item, kind, None, k) for k in range(s.K) for kind in ("a", "b")]
            s.steps += [functools.partial(s.item, "ba", None, k) for k in range(s.K)]

    def inside(s, zz):
        return jnp.logical_and(zz >= s.lo, zz <= s.hi)

    def slot(s, dev, k):
        return s.rsem.at[jnp.clip((dev - 8 * s.lo) * s.K + k, 0, 24 * (s.hi - s.lo + 1) - 1)]

    def send(s, src, dev, k, to, *conds):
        i = s.ns
        s.ns += 1
        cp = pltpu.make_async_remote_copy(
            src, s.w.at[jnp.clip(dev - s.base, 0, s.w.shape[0] - 1), k], s.ssem.at[i], s.slot(dev, k), device_id=(to,), device_id_type=MESH
        )
        conds = [f for f in conds if f is not None]
        s.pend.append((i, conds))
        s.when(conds, cp.start)

    @staticmethod
    def when(conds, fn):
        if conds:
            pl.when(functools.reduce(jnp.logical_and, [f() for f in conds]))(fn)
        else:
            fn()

    def at_me(s):
        return jnp.clip(s.c.me - s.base, 0, 8 * (s.hi + 1) - s.base - 1)

    def mine(s):
        return s.inside(s.c.z)

    def start(s, ks, routes):
        c = s.c
        to = dict(
            dn=(c.dn, lambda: c.hasdn), up=(c.up, lambda: c.hasup), b=(c.bp, None), a=(c.ap, None), s=(c.sib, None)
        )

        @pl.when(s.mine())
        def _():
            for k in ks:
                for r in routes:
                    s.send(s.own.at[k], c.me, k, to[r][0], to[r][1])
                    i, conds = s.pend.pop()
                    s.pend.append((i, conds + [s.mine]))

    def keep(s):
        @pl.when(s.mine())
        def _():
            for k in range(s.K):
                pltpu.make_async_copy(s.own.at[k], s.w.at[s.at_me(), k], s.lsem.at[k]).start()

    def keep_wait(s):
        @pl.when(s.mine())
        def _():
            for k in range(s.K):
                pltpu.make_async_copy(s.own.at[k], s.w.at[s.at_me(), k], s.lsem.at[k]).wait()

    def wait(s, dev, k):
        r = s.w.at[dev - s.base, k]
        pltpu.make_async_copy(r, r, s.slot(dev, k)).wait()

    def item(s, kind, dz, k):
        c = s.c
        if dz is None:
            src = c.me + 8 * (s.lo - c.z)
            valid = (lambda: c.z != s.lo) if kind == "z" else None
        else:
            src = c.me + 8 * dz
            valid = lambda: s.inside(c.z + dz)
        if "a" in kind:
            src = src + c.astep * (1 - 2 * c.abit)
        if "b" in kind:
            src = src + c.bstep * (1 - 2 * c.bbit)

        def body():
            s.wait(src, k)
            r = s.w.at[src - s.base, k]
            if kind == "z":
                if (dz is None and s.lo < 3) or (dz is not None and dz < 0):
                    beyond = (lambda: c.z > s.lo) if dz is None and s.lo > 0 else None
                    s.send(r, src, k, c.up, lambda: c.hasup, valid, beyond)
                if (dz is None and s.lo > 0) or (dz is not None and dz > 0):
                    beyond = (lambda: c.z < s.lo) if dz is None and s.lo < 3 else None
                    s.send(r, src, k, c.dn, lambda: c.hasdn, valid, beyond)
            if kind in ("z", "a"):
                s.send(r, src, k, c.bp, valid)
            if kind == "z":
                s.send(r, src, k, c.ap, valid)
            s.send(r, src, k, c.sib, valid)

        s.when([] if valid is None else [valid], body)

    def sibling(s, ks=(0, 1, 2)):
        c = s.c

        def one(i, _):
            for k in ks:
                s.wait(8 * s.lo + 2 * i + 1 - c.core, k)
            return 0

        lax.fori_loop(0, 4 * (s.hi - s.lo + 1), one, 0)

    def sent(s):
        for i, conds in s.pend:
            r = s.w.at[0, 0]
            s.when(conds, pltpu.make_async_copy(r, r, s.ssem.at[i]).wait)


class Vector:
    def __init__(s, c, own, vec, sem):
        s.c, s.own, s.vec, s.sem = c, own, vec, sem
        s.n = 31

    def tell(s):
        bar = pltpu.get_barrier_semaphore()

        @pl.when(s.c.me != s.n)
        def _():
            pl.semaphore_signal(bar, inc=1, device_id=(s.n,), device_id_type=MESH)

    def copy(s, to):
        return pltpu.make_async_remote_copy(
            s.own, s.vec, s.sem.at[to], s.sem.at[s.n], device_id=(to,), device_id_type=MESH
        )

    def start(s):
        @pl.when(s.c.me == s.n)
        def _():
            s.vec[...] = s.own[...]

            def one(i, _):
                s.copy(i).start()
                return 0

            lax.fori_loop(0, s.n, one, 0)

    def wait(s):
        @pl.when(s.c.me != s.n)
        def _():
            pltpu.make_async_copy(s.vec, s.vec, s.sem.at[s.n]).wait()

    def sent(s):
        @pl.when(s.c.me == s.n)
        def _():
            def one(i, _):
                s.copy(i).wait_send()
                return 0

            lax.fori_loop(0, s.n, one, 0)

class Reduce:
    K = 3

    @staticmethod
    def scratch(lo, hi, stage):
        nz = hi - lo + 1
        pieces = lambda n: pltpu.VMEM((n, 128, D), BF)
        dma = lambda n: pltpu.SemaphoreType.DMA((n,))
        sizes = [12 * nz, 6 * nz, 3 * nz, 3 * nz + 3]
        return (
            [pieces(n) for n in sizes]
            + [pieces(stage)]
            + [dma(12 * nz)]
            + [dma(n) for n in sizes]
            + [dma(12 * nz), dma(stage)]
        )

    def __init__(s, c, lo, hi, parts, out, scr, scale, order, direct=False, auto=True):
        s.auto = auto
        s.c, s.lo, s.hi, s.parts, s.out, s.scale, s.order, s.direct = c, lo, hi, parts, out, scale, order, direct
        s.S, s.B, s.A, s.Z, s.stage, s.sent_s, s.got_s, s.got_b, s.got_a, s.got_z, s.sent, s.loaded = scr
        s.nst = s.stage.shape[0]
        s.nz = hi - lo + 1
        s.later = []
        s.waits = []
        s.steps = [functools.partial(s.item, i) for i in range(len(order))]

    def owner(s, zz, fb, fa, core):
        c = s.c
        astep = 2 + 2 * core
        bstep = 4 - 2 * core
        abit = c.x + (c.y - c.x) * core
        bbit = c.y + (c.x - c.y) * core
        return zz * 8 + core + bstep * (bbit + fb * (1 - 2 * bbit)) + astep * (abit + fa * (1 - 2 * abit))

    def source(s, p, fn):
        if len(s.parts) == 1:
            lo, hi, ref = s.parts[0]
            fn(ref.at[p - lo])
            return
        for lo, hi, ref in s.parts:

            @pl.when(jnp.logical_and(p >= lo, p < hi))
            def _():
                fn(ref.at[jnp.clip(p - lo, 0, hi - lo - 1)])

    def slot(s, zz, fb, fa, k):
        return (((zz - s.lo) * 2 + fb) * 2 + fa) * s.K + k

    def places(s, order=None):
        for kind, zz, fa, k in order or s.order:
            if kind != "f":
                yield zz, 1 if kind == "b" else 0, fa, k

    def zero(s):
        c = s.c

        def clear(n):
            s.Z[n] = jnp.zeros((128, D), BF)

        for n in range(3 * s.nz + 3):
            at_zero = n < 3 * s.nz
            at_three = n >= 3 * s.nz or s.lo + n // 3 < 3
            if at_zero:
                pl.when(c.z == 0)(functools.partial(clear, n))
            if at_three:
                pl.when(c.z == 3)(functools.partial(clear, n))

    def to_sibling(s, order=None):
        c = s.c
        for zz, fb, fa, k in s.places(order):
            n = s.slot(zz, fb, fa, k)

            def go(r, n=n):
                pltpu.make_async_remote_copy(
                    r, s.S.at[n], s.sent_s.at[n], s.got_s.at[n], device_id=(c.sib,), device_id_type=MESH
                ).start()

            s.source(s.owner(zz, fb, fa, 1 - c.core) * s.K + k, go)

    def load(s, i):
        if s.direct or i >= len(s.order):
            return
        kind, zz, fa, k = s.order[i]
        n = i % s.nst

        def go(r):
            pltpu.make_async_copy(r, s.stage.at[n], s.loaded.at[n]).start()

        s.source(s.owner(zz, 1 if kind == "b" else 0, fa, s.c.core) * s.K + k, go)

    def prefetch(s):
        for i in range(s.nst - 1):
            s.load(i)

    def flush(s):
        for f in s.later:
            f()
        s.later = []

    @staticmethod
    def wait(ref, sem):
        pltpu.make_async_copy(ref, ref, sem).wait()

    @staticmethod
    def sum(srcs, dst, scale=None):
        def rows(r, _):
            rr = pl.ds(pl.multiple_of(r * 16, 16), 16)
            t = srcs[0][rr, :].astype(F32)
            for q in srcs[1:]:
                t = t + q[rr, :].astype(F32)
            if scale is not None:
                t = t * scale
            dst[rr, :] = t.astype(dst.dtype)
            return 0

        lax.fori_loop(0, 8, rows, 0)

    def item(s, i):
        c, K = s.c, s.K
        kind, zz, fa, k = s.order[i]
        fb = 1 if kind == "b" else 0
        if s.direct:
            lo, hi, ref = s.parts[0]
            own = ref.at[s.owner(zz, fb, fa, c.core) * K + k - lo]
        else:
            own = s.stage.at[i % s.nst]
            s.wait(own, s.loaded.at[i % s.nst])
        s.flush()
        n = s.slot(zz, fb, fa, k)
        out = s.S.at[n]
        bi = ((zz - s.lo) * 2 + fa) * K + k
        zi = (zz - s.lo) * K + k
        z2 = s.nz * K + k

        def gather(kinds):
            srcs = [own]
            if "S" in kinds:
                srcs.append((out, s.got_s.at[n]))
            if "B" in kinds:
                srcs.append((s.B.at[bi], s.got_b.at[bi]))
            if "A" in kinds:
                srcs.append((s.A.at[zi], s.got_a.at[zi]))
            for pair in srcs[1:]:
                s.wait(*pair)
            return srcs[:1] + [ref for ref, _ in srcs[1:]]

        def send(dst, sem, to):
            return pltpu.make_async_remote_copy(
                out, dst, s.sent.at[n], sem, device_id=(to,), device_id_type=MESH
            )

        if kind == "b":
            s.sum(gather("S"), out)
            s.later.append(send(s.B.at[bi], s.got_b.at[bi], c.bp).start)
            s.waits.append((n, None))
        elif kind == "a":
            s.sum(gather("SB"), out)
            s.later.append(send(s.A.at[zi], s.got_a.at[zi], c.ap).start)
            s.waits.append((n, None))
        elif kind == "z":

            @pl.when(c.z != zz)
            def _():
                srcs = gather("SBA")
                comes = jnp.where(c.z <= zz, c.z, 3 - c.z)
                pl.when(comes > 0)(functools.partial(s.wait, s.Z.at[zi], s.got_z.at[zi]))
                s.sum(srcs + [s.Z.at[zi]], out)

            def on():
                @pl.when(c.z < zz)
                def _():
                    send(s.Z.at[zi], s.got_z.at[zi], c.up).start()

                to = jnp.where(c.z == zz + 1, z2, zi)

                @pl.when(c.z > zz)
                def _():
                    send(s.Z.at[to], s.got_z.at[to], c.dn).start()

            s.later.append(on)
            s.waits.append((n, zz))
        else:

            @pl.when(c.z == zz)
            def _():
                srcs = gather("SBA")
                pl.when(c.hasdn)(functools.partial(s.wait, s.Z.at[zi], s.got_z.at[zi]))
                pl.when(c.hasup)(functools.partial(s.wait, s.Z.at[z2], s.got_z.at[z2]))
                s.sum(srcs + [s.Z.at[zi], s.Z.at[z2]], s.out.at[k], s.scale)

        if s.auto:
            s.load(i + s.nst - 1)

    def finish(s):
        s.flush()
        for n, zz in s.waits:
            w = functools.partial(s.wait, s.S.at[0], s.sent.at[n])
            if zz is None:
                w()
            else:
                pl.when(s.c.z != zz)(w)

        for place in s.places():
            s.wait(s.S.at[0], s.sent_s.at[s.slot(*place)])


BACK_STEPS = (
    ("b301", "b211", "b310", "b212",),
    ("b312", "b300", "b210",),
    ("b311", "b110", "a211", "b100", "b201",),
    (),
    (),
    ("b302",),
    ("a311",),
    ("a310",),
    ("z301", "a312", "a210",),
    ("z300", "b200", "a110", "b202",),
    ("a212", "b111", "z302", "z201",),
    (),
    ("z200", "b112",),
    ("b101", "a111", "z100",),
    ("b102", "z202", "f302", "a112", "f301", "f300", "z101",),
    ("f101", "f201", "f100", "f202", "z102",),
    ("f102", "f200",),
)
TAIL_STEPS = (
    (),
    (),
    ("b000", "b010",),
    ("b011", "b001",),
    ("a010", "a011", "b012", "b002",),
    ("z000",),
    ("a012", "f000", "z001",),
    ("f001", "z002",),
    ("f002",),
)


def reduce_order(groups):
    order = [(t[0], int(t[1]), int(t[2]), int(t[3])) for g in groups for t in g]
    ends = [sum(len(g) for g in groups[: i + 1]) for i in range(len(groups))]
    return order, [list(range(e - len(g), e)) for e, g in zip(ends, groups)]


def qkv_kernel(x_ref, vec_ref, w_ref, out_ref, n_ref):
    j = pl.program_id(0)

    @pl.when(j == 0)
    def _():
        for i in range(2):

            def block(rows, dst):
                v = x_ref[i, rows, :].astype(F32)
                c = v - jnp.mean(v, axis=1, keepdims=True)
                rc = lax.rsqrt(jnp.mean(c * c, axis=1, keepdims=True) + EPS)
                return (c * rc * (1.0 + vec_ref[8:9, :]) + vec_ref[9:10, :]).astype(BF)

            def one(c, _):
                n_ref[i, rows_at(c), :] = block(rows_at(c), None)
                return 0

            lax.fori_loop(0, 18, one, 0)
            last = block(slice(576, 577), None).astype(F32)
            n_ref[i, 576:592, :] = jnp.concatenate([last, jnp.zeros((15, D), F32)], axis=0).astype(BF)

    w = w_ref[...].reshape(D, D)
    bias = jnp.where(j == 0, vec_ref[0:1, :], jnp.where(j == 2, vec_ref[1:2, :], 0.0))
    for i in range(2):
        out_ref[0, i] = (nn(n_ref[i], w) + bias).astype(BF)


def qkv(x, vec, w):
    return pl.pallas_call(
        qkv_kernel,
        grid=(3,),
        in_specs=[full((2, S, D)), full((16, D)), pl.BlockSpec((8, 1, 128, D), lambda j: (0, j, 0, 0))],
        out_specs=[pl.BlockSpec((1, 2, SQ, D), lambda j: (j, 0, 0, 0)), full((2, SQ, D))],
        out_shape=[jax.ShapeDtypeStruct((3, 2, SQ, D), BF), jax.ShapeDtypeStruct((2, SQ, D), BF)],
        compiler_params=pltpu.CompilerParams(vmem_limit_bytes=VMEM_ALL),
        name="qkv",
    )(x, vec, w.reshape(32, 3, 128, D))


def padded(v):
    return jnp.concatenate([v, jnp.zeros((640 - SQ, 128), v.dtype)], axis=0)


def attend_pair(q, k, v):
    lane = lax.broadcasted_iota(jnp.int32, (1, 128), 1)
    k = padded(k)
    v = padded(v)
    outs = []
    for h in range(2):
        mine = lane < 64 if h == 0 else lane >= 64
        s = nt(jnp.where(mine, q, jnp.zeros_like(q)), k)
        s = jnp.concatenate([s[:, :512], jnp.where(lane < S - 512, s[:, 512:], -1e30)], axis=1)
        top = jnp.max(s, axis=1, keepdims=True)
        p = jnp.exp2((s - top) * SCORE)
        total = jnp.sum(p, axis=1, keepdims=True)
        outs.append(nn(p.astype(BF), v) * (1.0 / total))
    return jnp.where(lane < 64, outs[0], outs[1]).astype(BF)


def attend_kernel(q_ref, k_ref, v_ref, o_ref):
    half = SQ // 2
    for r in range(2):
        rows = slice(r * half, (r + 1) * half)
        o_ref[0, rows, :] = attend_pair(q_ref[0, 0, rows, :], k_ref[0, 0], v_ref[0, 0])


def attend(z):
    spec = lambda j: pl.BlockSpec((1, 1, SQ, 128), lambda i, h: (j, i, 0, h))
    return pl.pallas_call(
        attend_kernel,
        grid=(2, 8),
        in_specs=[spec(0), spec(1), spec(2)],
        out_specs=pl.BlockSpec((1, SQ, 128), lambda i, h: (i, 0, h)),
        out_shape=jax.ShapeDtypeStruct((2, SQ, D), BF),
        compiler_params=pltpu.CompilerParams(vmem_limit_bytes=VMEM_ALL),
        name="attend",
    )(z, z, z)


def norm_block(v, vec_ref):
    v = v.astype(F32)
    ce = v - jnp.mean(v, axis=1, keepdims=True)
    rc = lax.rsqrt(jnp.mean(ce * ce, axis=1, keepdims=True) + EPS)
    return (ce * rc * (1.0 + vec_ref[8:9, :]) + vec_ref[9:10, :]).astype(BF)


def norm_one(x_ref, vec_ref, n_ref):
    for i in range(2):

        def one(c, _):
            n_ref[i, rows_at(c), :] = norm_block(x_ref[i, rows_at(c), :], vec_ref)
            return 0

        lax.fori_loop(0, 18, one, 0)
        last = norm_block(x_ref[i, 576:577, :], vec_ref).astype(F32)
        n_ref[i, 576:592, :] = jnp.concatenate([last, jnp.zeros((15, D), F32)], axis=0).astype(BF)


def front_kernel(own, vec_own, x_ref, w, vec, z_ref, n_ref, mix_ref, vlow, wq, qsem, vsem, *sems):
    c = Ctx()
    zero = Gather(c, 0, 0, own, w, sems[:3])
    rest = Gather(c, 1, FRONT_HI, own, w, sems[3:])
    vector = Vector(c, vec_own, vlow, vsem)
    vector.tell()
    c.barrier(jnp.where(c.me == 31, 31, 0))
    vector.start()
    zero.start((0, 1, 2), ("up", "b", "a", "s"))
    rest.start((0, 1, 2), ("dn",))
    rest.start(range(EARLY), ("b", "a"))
    rest.start((0, 1, 2), ("s",))
    zero.keep()
    rest.keep()
    for step in zero.steps[:3]:
        step()
    for step in zero.steps[3:]:
        step()
    rest.start((0, 1, 2), ("up",))
    rest.start(range(EARLY, 3), ("b", "a"))
    zero.keep_wait()
    zero.sibling()
    loads = [pltpu.make_async_copy(w.at[0:8, j], wq.at[j % 2], qsem.at[j]) for j in range(3)]
    loads[0].start()
    loads[1].start()
    vector.wait()
    vec[...] = vlow[...].astype(F32)
    norm_one(x_ref, vec, n_ref)
    per = PER
    steps = list(rest.steps)
    for j in range(3):
        for step in steps[:per]:
            step()
        steps = steps[per:]
        loads[j].wait()
        for i in range(2):
            r = nn(n_ref[i], wq[j % 2].reshape(D, D))
            if j != 1:
                r = r + vec[j // 2 : j // 2 + 1, :]
            z_ref[j, i] = r.astype(BF)
        if j == 0:
            loads[2].start()

    def pair(t, _):
        for n in range(16):
            if steps[n * per : (n + 1) * per]:

                @pl.when(t == n)
                def _():
                    for step in steps[n * per : (n + 1) * per]:
                        step()

        i = t // 8
        cols = pl.ds(pl.multiple_of((t % 8) * 128, 128), 128)
        half = SQ // 2
        k = z_ref[1, i, :, cols]
        v = z_ref[2, i, :, cols]
        for r in range(2):
            rows = slice(r * half, (r + 1) * half)
            mix_ref[i, rows, cols] = attend_pair(z_ref[0, i, rows, cols], k, v)
        return 0

    lax.fori_loop(0, 16, pair, 0)
    for step in steps[16 * per :]:
        step()
    rest.sibling()
    rest.keep_wait()
    zero.sent()
    rest.sent()
    vector.sent()


def front(own, vec_own, x):
    vm = pl.BlockSpec(memory_space=pltpu.VMEM)
    dma = lambda n: pltpu.SemaphoreType.DMA((n,))
    return pl.pallas_call(
        front_kernel,
        in_specs=[vm, vm, vm],
        out_specs=[pl.BlockSpec(memory_space=pl.ANY), vm, vm, vm, vm],
        out_shape=[
            jax.ShapeDtypeStruct((32, 3, 128, D), BF),
            jax.ShapeDtypeStruct((16, D), F32),
            jax.ShapeDtypeStruct((3, 2, SQ, D), BF),
            jax.ShapeDtypeStruct((2, SQ, D), BF),
            jax.ShapeDtypeStruct((2, SQ, D), BF),
        ],
        scratch_shapes=[pltpu.VMEM((16, D), BF), pltpu.VMEM((2, 8, 128, D), BF), dma(3), dma(32)]
        + Gather.sems(0, 0)
        + Gather.sems(1, FRONT_HI),
        compiler_params=pltpu.CompilerParams(collective_id=1, has_side_effects=True, vmem_limit_bytes=VMEM_ALL),
        name="front",
    )(own, vec_own, x)


def attend_back_pair(q, k, v, do):
    lane = lax.broadcasted_iota(jnp.int32, (1, 128), 1)
    real = lax.broadcasted_iota(jnp.int32, (16, 1), 0) < S - 576
    q = padded(q)
    do = padded(do)
    dqs, dks, dvs = [], [], []
    for h in range(2):
        mine = lane < 64 if h == 0 else lane >= 64
        s = nt(jnp.where(mine, k, jnp.zeros_like(k)), q)
        s = jnp.concatenate([s[:576], jnp.where(real, s[576:], -1e30)], axis=0)
        top = jnp.max(s, axis=0, keepdims=True)
        p = jnp.exp2((s - top) * SCORE)
        p = p * (1.0 / jnp.sum(p, axis=0, keepdims=True))
        dvs.append(nn(p.astype(BF), do))
        dp = nt(jnp.where(mine, v, jnp.zeros_like(v)), do)
        ds = (p * (dp - jnp.sum(p * dp, axis=0, keepdims=True))).astype(BF)
        dks.append(nn(ds, q))
        dqs.append(tn(ds, k))
    pick = lambda pair, scale: (jnp.where(lane < 64, pair[0], pair[1]) * scale).astype(BF)
    return pick(dqs, 0.125)[:SQ], pick(dks, 0.125), pick(dvs, 1.0)


def attend_back_kernel(q_ref, k_ref, v_ref, do_ref, out_ref):
    dq, dk, dv = attend_back_pair(q_ref[0, 0], k_ref[0, 0], v_ref[0, 0], do_ref[0])
    out_ref[0, 0] = dq
    out_ref[1, 0] = dk
    out_ref[2, 0] = dv


def attend_back(z, do):
    spec = lambda j: pl.BlockSpec((1, 1, SQ, 128), lambda i, h: (j, i, 0, h))
    return pl.pallas_call(
        attend_back_kernel,
        grid=(2, 8),
        in_specs=[spec(0), spec(1), spec(2), pl.BlockSpec((1, SQ, 128), lambda i, h: (i, 0, h))],
        out_specs=pl.BlockSpec((3, 1, SQ, 128), lambda i, h: (0, i, 0, h)),
        out_shape=jax.ShapeDtypeStruct((3, 2, SQ, D), BF),
        compiler_params=pltpu.CompilerParams(vmem_limit_bytes=VMEM_ALL),
        name="attend_back",
    )(z, z, z, do)


def mlp_kernel(x_ref,g_ref,mix_ref,vec_ref,wo_ref,wu_ref,wd_ref,
               out_ref,gup_ref,gdn_ref,gout_ref,dmix_ref,dhid_ref,gvec_ref,
               n2,gs,acc,dn,stat,*,FB,NB):
    jb=pl.program_id(0)
    hid=dhid_ref
    @pl.when(jb==0)
    def _():
        wo=wo_ref[...].reshape(D,D)
        for i in range(2):
            hid[i*SQ:(i+1)*SQ,:]=nn(mix_ref[i],wo)
            gs[i*SQ:i*SQ+576,:]=g_ref[i,:576,:]
            gs[i*SQ+576:(i+1)*SQ,:]=jnp.concatenate([g_ref[i,576:577,:].astype(F32),jnp.zeros((15,D),F32)],axis=0).astype(BF)
            def addx(c,_):
                r=pl.multiple_of(c*CH,CH)
                hid[pl.ds(i*SQ+r,CH),:]+=x_ref[i,pl.ds(r,CH),:].astype(F32)+vec_ref[2:3,:]
                return 0
            lax.fori_loop(0,18,addx,0)
            hid[i*SQ+576:i*SQ+577,:]+=x_ref[i,576:577,:].astype(F32)+vec_ref[2:3,:]
        acc[...]=jnp.zeros_like(acc); dn[...]=jnp.zeros_like(dn)
        gvec_ref[...]=jnp.zeros_like(gvec_ref)
        def ln(c,_):
            r=pl.ds(pl.multiple_of(c*CH,CH),CH)
            h=hid[r,:]
            mu=jnp.mean(h,axis=1,keepdims=True)
            ce=h-mu
            rc=lax.rsqrt(jnp.mean(ce*ce,axis=1,keepdims=True)+EPS)
            n2[r,:]=(ce*rc*(1.0+vec_ref[10:11,:])+vec_ref[11:12,:]).astype(BF)
            stat[r,0:1]=mu; stat[r,1:2]=rc
            return 0
        lax.fori_loop(0,M//CH,ln,0)
        def gsum(c,a):
            r=pl.ds(pl.multiple_of(c*CH,CH),CH)
            return a+gs[r,:].astype(F32)
        t=lax.fori_loop(0,M//CH,gsum,jnp.zeros((CH,D),F32))
        gvec_ref[7:8,:]=jnp.sum(t,axis=0,keepdims=True)
    wu=wu_ref[...].reshape(D,FB); wd=wd_ref[...].reshape(FB,D)
    nper=D//FB
    row=vec_ref[pl.ds(3+jb//nper,1),:]
    bup=row[:,:FB]
    for t in range(1,nper): bup=jnp.where(jb%nper==t,row[:,t*FB:(t+1)*FB],bup)
    g=gs[...]; n=n2[...]
    pre=nn(n,wu)+bup
    cdf=0.5*(1.0+lax.erf(pre*0.7071067811865476))
    act=(pre*cdf).astype(BF)
    slope=cdf+pre*0.3989422804014327*jnp.exp(-0.5*pre*pre)
    dpf=nt(g,wd)*slope
    dp=dpf.astype(BF)
    acc[...]+=nn(act,wd)
    dn[...]+=nt(dp,wu)
    gup_ref[...]=tn(n,dp).astype(BF).reshape(gup_ref.shape)
    gdn_ref[...]=tn(act,g).astype(BF).reshape(gdn_ref.shape)
    bsum=jnp.sum(dp.astype(F32),axis=0,keepdims=True)
    for t in range(nper):
        @pl.when(jb%nper==t)
        def _(): gvec_ref[pl.ds(3+jb//nper,1),t*FB:(t+1)*FB]=bsum
    @pl.when(jb==NB-1)
    def _():
        for i in range(2):
            def ob(c,_):
                r=pl.multiple_of(c*CH,CH)
                out_ref[i,pl.ds(r,CH),:]=(hid[pl.ds(i*SQ+r,CH),:]+(acc[pl.ds(i*SQ+r,CH),:]+vec_ref[7:8,:])).astype(BF)
                return 0
            lax.fori_loop(0,18,ob,0)
            out_ref[i,576:577,:]=(hid[i*SQ+576:i*SQ+577,:]+(acc[i*SQ+576:i*SQ+577,:]+vec_ref[7:8,:])).astype(BF)
        def bk(c,car):
            a,b,d=car
            r=pl.ds(pl.multiple_of(c*CH,CH),CH)
            mu=stat[r,0:1]; rc=stat[r,1:2]
            xh=(hid[r,:]-mu)*rc
            dd=dn[r,:]
            e=dd*(1.0+vec_ref[10:11,:])
            dh=gs[r,:].astype(F32)+rc*(e-jnp.mean(e,axis=1,keepdims=True)-xh*jnp.mean(e*xh,axis=1,keepdims=True))
            dhid_ref[r,:]=dh
            db=dh.astype(BF)
            n2[r,:]=db
            return (a+dd*xh,b+dd,d+db.astype(F32))
        zz=jnp.zeros((CH,D),F32)
        a,b,d=lax.fori_loop(0,M//CH,bk,(zz,zz,zz))
        gvec_ref[10:11,:]=jnp.sum(a,axis=0,keepdims=True)
        gvec_ref[11:12,:]=jnp.sum(b,axis=0,keepdims=True)
        gvec_ref[2:3,:]=jnp.sum(d,axis=0,keepdims=True)
        db=n2[...]
        wo=wo_ref[...].reshape(D,D)
        dmix_ref[...]=nt(db,wo).astype(BF).reshape(2,SQ,D)
        gout_ref[...]=tn(mix_ref[...].reshape(M,D),db).astype(BF).reshape(8,128,D)
def mlp(x,g,mix,vec,W,FB=512):
    NB=4096//FB; nper=D//FB
    W4=W.reshape(96,4,32,1024)
    return pl.pallas_call(functools.partial(mlp_kernel,FB=FB,NB=NB),grid=(NB,),
      in_specs=[full((2,S,D)),full((2,S,D)),full((2,SQ,D)),full((16,D)),
        pl.BlockSpec((8,128,D),lambda j:(3,0,0),pipeline_mode=pl.Buffered(1)),
        pl.BlockSpec((32,1,32,FB),lambda j:(1,j//nper,0,j%nper)),
        pl.BlockSpec((FB//128,128,D),lambda j:(64//(FB//128)+j,0,0))],
      out_specs=[full((2,S,D)),pl.BlockSpec((32,1,32,FB),lambda j:(0,j//nper,0,j%nper)),
        pl.BlockSpec((FB//128,128,D),lambda j:(j,0,0)),full((8,128,D)),full((2,SQ,D)),full((M,D)),full((16,D))],
      out_shape=[jax.ShapeDtypeStruct((2,S,D),BF),jax.ShapeDtypeStruct((32,4,32,D),BF),jax.ShapeDtypeStruct((32,128,D),BF),
        jax.ShapeDtypeStruct((8,128,D),BF),jax.ShapeDtypeStruct((2,SQ,D),BF),jax.ShapeDtypeStruct((M,D),F32),jax.ShapeDtypeStruct((16,D),F32)],
      scratch_shapes=[pltpu.VMEM((M,D),BF),pltpu.VMEM((M,D),BF),pltpu.VMEM((M,D),F32),pltpu.VMEM((M,D),F32),pltpu.VMEM((M,128),F32)],
      compiler_params=pltpu.CompilerParams(vmem_limit_bytes=67043328),name=f"mlp{FB}")(x,g,mix,vec,W,W4,W)


def tail_kernel(x_ref, dz_ref, n_ref, dhid_ref, vec_ref, w_ref, gvin_ref, gx_ref, gw_ref, gvec_ref, acc):
    j = pl.program_id(0)

    @pl.when(j == 0)
    def _():
        gvec_ref[...] = gvin_ref[...]
        acc[...] = jnp.zeros_like(acc)

    w = w_ref[...].reshape(D, D)
    dz = dz_ref[0].reshape(M, D)
    acc[...] += nt(dz, w)
    gw_ref[...] = tn(n_ref[...].reshape(M, D), dz).astype(BF).reshape(8, 1, 128, D)

    @pl.when(j != 1)
    def _():
        def add(c, t):
            return t + dz_ref[0, 0, pl.ds(c * 16, 16), :].astype(F32) + dz_ref[0, 1, pl.ds(c * 16, 16), :].astype(F32)

        t = lax.fori_loop(0, SQ // 16, add, jnp.zeros((16, D), F32))
        gvec_ref[pl.ds(j // 2, 1), :] = jnp.sum(t, axis=0, keepdims=True)

    @pl.when(j == 2)
    def _():
        def back(x, dd, dh):
            v = x.astype(F32)
            ce = v - jnp.mean(v, axis=1, keepdims=True)
            rc = lax.rsqrt(jnp.mean(ce * ce, axis=1, keepdims=True) + EPS)
            xh = ce * rc
            e = dd * (1.0 + vec_ref[8:9, :])
            g = dh + rc * (e - jnp.mean(e, axis=1, keepdims=True) - xh * jnp.mean(e * xh, axis=1, keepdims=True))
            return g.astype(BF), dd * xh, dd

        a = b = jnp.zeros((CH, D), F32)
        la = lb = jnp.zeros((1, D), F32)
        for i in range(2):

            def one(c, carry):
                r = rows_at(c)
                r2 = pl.ds(pl.multiple_of(i * SQ + c * CH, 16), CH)
                g, s1, s2 = back(x_ref[i, r, :], acc[r2, :], dhid_ref[r2, :])
                gx_ref[i, r, :] = g
                return carry[0] + s1, carry[1] + s2

            a, b = lax.fori_loop(0, 18, one, (a, b))
            r2 = slice(i * SQ + 576, i * SQ + 577)
            g, s1, s2 = back(x_ref[i, 576:577, :], acc[r2, :], dhid_ref[r2, :])
            gx_ref[i, 576:577, :] = g
            la, lb = la + s1, lb + s2
        gvec_ref[8:9, :] = jnp.sum(a, axis=0, keepdims=True) + la
        gvec_ref[9:10, :] = jnp.sum(b, axis=0, keepdims=True) + lb


def tail(x, dz, n1, dhid, vec, w, gvec):
    return pl.pallas_call(
        tail_kernel,
        grid=(3,),
        in_specs=[
            full((2, S, D)),
            pl.BlockSpec((1, 2, SQ, D), lambda j: (j, 0, 0, 0)),
            full((2, SQ, D)),
            full((M, D)),
            full((16, D)),
            pl.BlockSpec((8, 1, 128, D), lambda j: (0, j, 0, 0)),
            full((16, D)),
        ],
        out_specs=[full((2, S, D)), pl.BlockSpec((8, 1, 128, D), lambda j: (0, j, 0, 0)), full((16, D))],
        out_shape=[
            jax.ShapeDtypeStruct((2, S, D), BF),
            jax.ShapeDtypeStruct((8, 3, 128, D), BF),
            jax.ShapeDtypeStruct((16, D), F32),
        ],
        scratch_shapes=[pltpu.VMEM((M, D), F32)],
        compiler_params=pltpu.CompilerParams(vmem_limit_bytes=VMEM_ALL),
        name="tail",
    )(x, dz, n1, dhid, vec, w.reshape(32, 3, 128, D), gvec)

def back_kernel(z_ref, do_ref, *refs, lo, hi, ranges, scale):
    n = len(ranges)
    parts = [(a, b, r) for (a, b), r in zip(ranges, refs[:n])]
    dz_ref, chunk = refs[n : n + 2]
    c = Ctx()
    order, groups = reduce_order(BACK_STEPS)
    red = Reduce(c, lo, hi, parts, chunk, refs[n + 2 :], scale, order)
    red.zero()
    chunk[...] = jnp.zeros_like(chunk)
    c.barrier()
    red.to_sibling()
    red.prefetch()

    def pair(t, _):
        for m in range(16):
            if groups[m]:

                @pl.when(t == m)
                def _():
                    for i in groups[m]:
                        red.steps[i]()
                    red.flush()

        i = t // 8
        cols = pl.ds(pl.multiple_of((t % 8) * 128, 128), 128)
        dq, dk, dv = attend_back_pair(z_ref[0, i, :, cols], z_ref[1, i, :, cols], z_ref[2, i, :, cols], do_ref[i, :, cols])
        dz_ref[0, i, :, cols] = dq
        dz_ref[1, i, :, cols] = dk
        dz_ref[2, i, :, cols] = dv
        return 0

    lax.fori_loop(0, 16, pair, 0)
    for i in groups[16]:
        red.steps[i]()
    red.finish()


def back(z, do, parts, lo, hi, ranges, scale):
    vm = pl.BlockSpec(memory_space=pltpu.VMEM)
    return pl.pallas_call(
        functools.partial(back_kernel, lo=lo, hi=hi, ranges=ranges, scale=scale),
        in_specs=[vm, vm] + [pl.BlockSpec(memory_space=pl.ANY)] * len(parts),
        out_specs=[vm, vm],
        out_shape=[jax.ShapeDtypeStruct((3, 2, SQ, D), BF), jax.ShapeDtypeStruct((3, 128, D), F32)],
        scratch_shapes=Reduce.scratch(lo, hi, 4),
        compiler_params=pltpu.CompilerParams(collective_id=2, has_side_effects=True, vmem_limit_bytes=VMEM_ALL),
        name="back",
    )(z, do, *parts)


def back_norm(x, dd, dh, vec_ref):
    v = x.astype(F32)
    ce = v - jnp.mean(v, axis=1, keepdims=True)
    rc = lax.rsqrt(jnp.mean(ce * ce, axis=1, keepdims=True) + EPS)
    xh = ce * rc
    e = dd * (1.0 + vec_ref[8:9, :])
    g = dh + rc * (e - jnp.mean(e, axis=1, keepdims=True) - xh * jnp.mean(e * xh, axis=1, keepdims=True))
    return g.astype(BF), dd * xh


def tail_quick_kernel(
    x_ref, dz_ref, n_ref, dhid_ref, vec_ref, gvin_ref, w, gx_ref, chunk, gvec_ref, acc, gw, wq, qsem, *scr, scale
):
    c = Ctx()
    order, groups = reduce_order(TAIL_STEPS)
    red = Reduce(c, 0, 0, [(0, 24, gw)], chunk, scr, scale, order, direct=True)
    loads = [pltpu.make_async_copy(w.at[0:8, j], wq.at[j % 2], qsem.at[j]) for j in range(3)]
    loads[0].start()
    loads[1].start()
    red.zero()
    chunk[...] = jnp.zeros_like(chunk)
    gvec_ref[...] = gvin_ref[...]
    c.barrier()

    def take(n):
        for i in groups[n]:
            red.steps[i]()
        red.flush()

    def weights(j):
        g = tn(n_ref[...].reshape(M, D), dz_ref[j].reshape(M, D)).astype(BF)
        for d in range(8):
            gw[3 * d + j] = g[128 * d : 128 * (d + 1)]

    def colsum(j):
        def add(r, t):
            rr = pl.ds(pl.multiple_of(r * 16, 16), 16)
            return t + dz_ref[j, 0, rr, :].astype(F32) + dz_ref[j, 1, rr, :].astype(F32)

        t = lax.fori_loop(0, SQ // 16, add, jnp.zeros((16, D), F32))
        gvec_ref[j // 2 : j // 2 + 1, :] = jnp.sum(t, axis=0, keepdims=True)

    def inputs(j):
        loads[j].wait()
        wj = wq[j % 2].reshape(D, D)
        for i in range(2):
            r = nt(dz_ref[j, i], wj)
            rows = slice(i * SQ, (i + 1) * SQ)
            acc[rows, :] = r if j == 0 else acc[rows, :] + r

    some = lambda k: [o for o in order if o[3] == k]
    weights(0)
    colsum(0)
    red.to_sibling(some(0))
    weights(1)
    red.to_sibling(some(1))
    take(2)
    weights(2)
    colsum(2)
    red.to_sibling(some(2))
    take(3)
    for j in range(3):
        inputs(j)
        if j == 0:
            loads[2].start()
        take(4 + j)
    a = b = jnp.zeros((CH, D), F32)
    la = lb = jnp.zeros((1, D), F32)
    for i in range(2):

        def one(t, carry):
            r = rows_at(t)
            r2 = pl.ds(pl.multiple_of(i * SQ + t * CH, 16), CH)
            dd = acc[r2, :]
            g, s1 = back_norm(x_ref[i, r, :], dd, dhid_ref[r2, :], vec_ref)
            gx_ref[i, r, :] = g
            return carry[0] + s1, carry[1] + dd

        a, b = lax.fori_loop(0, 18, one, (a, b))
        r2 = slice(i * SQ + 576, i * SQ + 577)
        dd = acc[r2, :]
        g, s1 = back_norm(x_ref[i, 576:577, :], dd, dhid_ref[r2, :], vec_ref)
        gx_ref[i, 576:577, :] = g
        la, lb = la + s1, lb + dd
        take(7 + i)
    gvec_ref[8:9, :] = jnp.sum(a, axis=0, keepdims=True) + la
    gvec_ref[9:10, :] = jnp.sum(b, axis=0, keepdims=True) + lb
    red.finish()


def tail_quick(x, dz, n1, dhid, vec, gvec, w, scale):
    vm = pl.BlockSpec(memory_space=pltpu.VMEM)
    return pl.pallas_call(
        functools.partial(tail_quick_kernel, scale=scale),
        in_specs=[vm] * 6 + [pl.BlockSpec(memory_space=pl.ANY)],
        out_specs=[vm] * 3,
        out_shape=[
            jax.ShapeDtypeStruct((2, S, D), BF),
            jax.ShapeDtypeStruct((3, 128, D), F32),
            jax.ShapeDtypeStruct((16, D), F32),
        ],
        scratch_shapes=[
            pltpu.VMEM((M, D), F32),
            pltpu.VMEM((24, 128, D), BF),
            pltpu.VMEM((2, 8, 128, D), BF),
            pltpu.SemaphoreType.DMA((3,)),
        ]
        + Reduce.scratch(0, 0, 1),
        compiler_params=pltpu.CompilerParams(collective_id=3, has_side_effects=True, vmem_limit_bytes=VMEM_ALL),
        name="tail_quick",
    )(x, dz, n1, dhid, vec, gvec, w)


def close_kernel(chunk_a, chunk_b, gvec, p_ref, m_ref, v_ref, wg, pn, mn, vn, flat, e, es, ea, eb, ez, sem, *, scale):
    c = Ctx()
    me = c.me
    bar = pltpu.get_barrier_semaphore()
    others = [c.sib, c.ap, c.bp] + [lax.rem(me + 8 * i, 32) for i in (1, 2, 3)]
    for to in others:
        pl.semaphore_signal(bar, inc=1, device_id=(to,), device_id_type=MESH)
    first, last = me == 0, me == 31

    @pl.when(jnp.logical_not(first))
    def _():
        pl.semaphore_signal(bar, inc=1, device_id=(me - 1,), device_id_type=MESH)

    @pl.when(jnp.logical_not(last))
    def _():
        pl.semaphore_signal(bar, inc=1, device_id=(me + 1,), device_id_type=MESH)

    def unfold(src, k, kind):
        for t in range(8):
            cols = slice(128 * t, 128 * (t + 1))
            if kind == 0:
                flat[pl.ds(8 * k + t, 128, stride=24), :] = src[k, :, cols]
            elif kind == 1:
                flat[pl.ds(1024 * k + t, 128, stride=8), :] = src[k, :, cols]
            else:
                for j in range(4):
                    flat[pl.ds(1024 * k + 8 * j + t, 32, stride=32), :] = src[k, 32 * j : 32 * j + 32, cols]

    for k in range(3):
        p = 3 * me + k
        up = jnp.logical_and(p >= 32, p < 64)
        pl.when(c.z == 0)(functools.partial(unfold, chunk_b, k, 0))
        pl.when(up)(functools.partial(unfold, chunk_a, k, 2))
        pl.when(jnp.logical_and(c.z > 0, jnp.logical_not(up)))(functools.partial(unfold, chunk_a, k, 1))

    def square(i, t):
        v = flat[pl.ds(pl.multiple_of(i * 64, 64), 64), :]
        return t + v * v

    sq = jnp.sum(lax.fori_loop(0, 48, square, jnp.zeros((64, 128), F32)))
    e[0:16, :] = gvec[...]
    e[16:24, :] = jnp.full((8, D), sq, F32)
    pl.semaphore_wait(bar, 6 + jnp.where(first, 0, 1) + jnp.where(last, 0, 1))
    head = flat.at[0:96]
    room = flat.at[3072:3168]
    edge = pltpu.make_async_remote_copy(
        head, room, sem.at[14], sem.at[15], device_id=(jnp.maximum(me - 1, 0),), device_id_type=MESH
    )
    pl.when(jnp.logical_not(first))(edge.start)
    for n, (to, dst) in enumerate(((c.sib, es), (c.ap, ea), (c.bp, eb))):
        cp = pltpu.make_async_remote_copy(e, dst, sem.at[n], sem.at[3 + n], device_id=(to,), device_id_type=MESH)
        cp.start()
        cp.wait()
        e[...] = e[...] + dst[...]
    ez[c.z] = e[...]
    cps = []
    for i in (1, 2, 3):
        to = lax.rem(me + 8 * i, 32)
        cp = pltpu.make_async_remote_copy(
            e, ez.at[c.z], sem.at[6 + i], sem.at[9 + i], device_id=(to,), device_id_type=MESH
        )
        cp.start()
        cps.append(cp)
    for i in (1, 2, 3):
        cps[i - 1].wait_send()
        zz = lax.rem(c.z + 4 - i, 4)
        pltpu.make_async_copy(ez.at[zz], ez.at[zz], sem.at[9 + i]).wait()
    total = ((ez[0] + ez[1]) + ez[2]) + ez[3]
    vec = total[0:12, :] * scale
    square_sum = total[16:17, 0:1] + jnp.sum(vec * vec)
    clip = jnp.minimum(1.0, max_norm / (jnp.sqrt(square_sum) + 1e-06))

    @pl.when(last)
    def _():
        for t in range(8):
            flat[pl.ds(3072 + t, 12, stride=8), :] = vec[:, 128 * t : 128 * (t + 1)]

    @pl.when(jnp.logical_not(last))
    def _():
        pltpu.make_async_copy(room, room, sem.at[15]).wait()

    pl.when(jnp.logical_not(first))(edge.wait_send)

    def apply(g, rows):
        w = clip * g
        m1 = beta_one * m_ref[rows, :] + (1.0 - beta_one) * w
        m2 = beta_two * v_ref[rows, :] + (1.0 - beta_two) * w * w
        par = p_ref[rows, :]
        step = m1 / (1.0 - beta_one**STEP) / (jnp.sqrt(m2 / (1.0 - beta_two**STEP)) + adam_eps)
        wg[rows, :] = g
        pn[rows, :] = par - learn_rate * (step + decay_rate * par)
        mn[rows, :] = m1
        vn[rows, :] = m2

    def block(i, _):
        apply(flat[pl.ds(i * 64 + 3 * me, 64), :], pl.ds(pl.multiple_of(i * 64, 64), 64))
        return 0

    lax.fori_loop(0, 48, block, 0)
    apply(flat[pl.ds(3072 + 3 * me, 3), :], slice(3072, 3075))


def close(chunk_a, chunk_b, gvec, params, moment_one, moment_two, scale):
    vm = pl.BlockSpec(memory_space=pltpu.VMEM)
    own = jax.ShapeDtypeStruct((3075, 128), F32)
    small = pltpu.VMEM((24, D), F32)
    return pl.pallas_call(
        functools.partial(close_kernel, scale=scale),
        in_specs=[vm] * 6,
        out_specs=[vm] * 4,
        out_shape=[own] * 4,
        scratch_shapes=[pltpu.VMEM((3168, 128), F32)]
        + [small] * 4
        + [pltpu.VMEM((4, 24, D), F32), pltpu.SemaphoreType.DMA((16,))],
        compiler_params=pltpu.CompilerParams(collective_id=4, has_side_effects=True, vmem_limit_bytes=VMEM_ALL),
        name="close",
    )(chunk_a, chunk_b, gvec, *(v.reshape(3075, 128) for v in (params, moment_one, moment_two)))


def to_pieces(rows, first):
    n = rows.shape[0] // 128
    plain = rows.reshape(n, 128, D)
    three = rows.reshape(n // 3, 128, 3, D).transpose(0, 2, 1, 3).reshape(n, 128, D)
    four = rows.reshape(n, 32, 4, D).transpose(0, 2, 1, 3).reshape(n, 128, D)
    p = first + lax.broadcasted_iota(jnp.int32, (n, 1, 1), 0)
    return jnp.where(p < 24, three, jnp.where((p >= 32) & (p < 64), four, plain))


def from_pieces(pieces, first):
    n = pieces.shape[0]
    plain = pieces.reshape(n * 128, D)
    three = pieces.reshape(n // 3, 3, 128, D).transpose(0, 2, 1, 3).reshape(n * 128, D)
    four = pieces.reshape(n, 4, 32, D).transpose(0, 2, 1, 3).reshape(n * 128, D)
    p = first + lax.broadcasted_iota(jnp.int32, (n * 128, 1), 0) // 128
    return jnp.where(p < 24, three, jnp.where((p >= 32) & (p < 64), four, plain))


def update(params, moment_one, moment_two, weight_grad, square_sum):
    clip_factor = jnp.minimum(1.0, max_norm / (jnp.sqrt(square_sum) + 1e-06))
    clipped = clip_factor * weight_grad
    moment_one_new = beta_one * moment_one + (1.0 - beta_one) * clipped
    moment_two_new = beta_two * moment_two + (1.0 - beta_two) * clipped * clipped
    correct_one = 1.0 - beta_one**STEP
    correct_two = 1.0 - beta_two**STEP
    params_new = params - learn_rate * (
        moment_one_new / correct_one / (jnp.sqrt(moment_two_new / correct_two) + adam_eps) + decay_rate * params
    )
    return params_new, moment_one_new, moment_two_new


def shards(tokens, cotangent, params, moment_one, moment_two):
    n = lax.axis_size("dp")
    me = lax.axis_index("dp")
    shard_len = params.shape[0]
    images_all = tokens.shape[0] * n
    mats = PIECES * 128 * D
    scale = 1.0 / images_all
    if n == 32:
        unit = 128
        extra = 12 * D // unit
        own_units = shard_len // unit
        gap = extra // n
        low = params.reshape(own_units, unit)
        before = lax.ppermute(low[own_units - extra :].astype(BF), "dp", [(i, (i + 1) % n) for i in range(n)])
        joined = jnp.concatenate([before.astype(F32), low], axis=0)
        aligned = lax.dynamic_slice(joined, (extra - gap * me, 0), (own_units - gap, unit))
        own = to_pieces(aligned.reshape(-1, D), 3 * me).astype(BF)
        vec_own = jnp.pad(low[own_units - extra :].reshape(12, D), ((0, 4), (0, 0))).astype(BF)
        w, vec, z, n1, mixed = front(own, vec_own, tokens)
        flat_w = w.reshape(PIECES, 128, D)
        outputs, gup, gdn, gout, dmix, dhid, gvec = mlp(tokens, cotangent, mixed, vec, flat_w)
        parts = [gout, gup.reshape(32, 128, D), gdn]
        dz, chunk_a = back(z, dmix, parts, 1, 3, [(24, 32), (32, 64), (64, 96)], scale)
        grad_tokens, chunk_b, gvec = tail_quick(tokens, dz, n1, dhid, vec, gvec, w, scale)
        news = close(chunk_a, chunk_b, gvec, params, moment_one, moment_two, scale)
        return (outputs, grad_tokens, *(v.reshape(shard_len) for v in news))
    flat = lax.all_gather(params.astype(BF), "dp", axis=0, tiled=True)
    w = to_pieces(flat[:mats].reshape(-1, D), 0)
    vec = jnp.pad(flat[mats:].reshape(12, D).astype(F32), ((0, 4), (0, 0)))
    z, n1 = qkv(tokens, vec, w)
    mixed = attend(z)
    outputs, gup, gdn, gout, dmix, dhid, gvec = mlp(tokens, cotangent, mixed, vec, w)
    dz = attend_back(z, dmix)
    grad_tokens, gqkv, gvec = tail(tokens, dz, n1, dhid, vec, w, gvec)
    parts = [gqkv.reshape(24, 128, D), gout, gup.reshape(32, 128, D), gdn]
    flat = jnp.concatenate([from_pieces(jnp.concatenate(parts, axis=0), 0).reshape(-1), gvec[:12].reshape(-1).astype(BF)])
    arrived = lax.all_to_all(flat.reshape(n, shard_len), "dp", split_axis=0, concat_axis=0, tiled=True)
    weight_grad = jnp.sum(arrived.astype(F32), axis=0) * scale
    square_sum = lax.psum(jnp.sum(weight_grad * weight_grad), "dp")
    news = update(params, moment_one, moment_two, weight_grad, square_sum)
    return (outputs, grad_tokens, weight_grad, *news)


def solution(mesh):
    in_specs = (P("dp", None, None), P("dp", None, None), P("dp"), P("dp"), P("dp"))
    out_specs = (P("dp", None, None), P("dp", None, None), P("dp"), P("dp"), P("dp"), P("dp"))
    return jax.shard_map(shards, mesh=mesh, in_specs=in_specs, out_specs=out_specs, check_vma=False)
```

```python
import functools

import jax
import jax.numpy as jnp
from jax import lax
from jax.experimental import pallas as pl
from jax.experimental.pallas import tpu as pltpu
from jax.sharding import PartitionSpec as P

D = 1024
FF = 4096
S = 577
SQ = 592
M = 2 * SQ
CH = 32
PIECES = 96
STEP = 4
BF = jnp.bfloat16
F32 = jnp.float32
MESH = pl.DeviceIdType.MESH
VMEM_ALL = 67043328

EPS = 1e-06
max_norm = 1.0
beta_one = 0.9
beta_two = 0.95
learn_rate = 0.02
decay_rate = 0.05
adam_eps = 1e-08
SCORE = 0.125 * 1.4426950408889634


def nt(a, b):
    return lax.dot_general(a, b, (((1,), (1,)), ((), ())), preferred_element_type=F32)


def nn(a, b):
    return jnp.dot(a, b, preferred_element_type=F32)


def tn(a, b):
    return lax.dot_general(a, b, (((0,), (0,)), ((), ())), preferred_element_type=F32)


def rows_at(c):
    return pl.ds(pl.multiple_of(c * CH, CH), CH)


def full(shape):
    return pl.BlockSpec(shape, lambda *_: (0,) * len(shape), pipeline_mode=pl.Buffered(1))


class Ctx:
    def __init__(s):
        me=lax.axis_index("dp"); s.me=me
        s.core=me%2; s.x=(me//2)%2; s.y=(me//4)%2; s.z=me//8
        s.sib=me+1-2*s.core
        xp=me+2*(1-2*s.x); yp=me+4*(1-2*s.y)
        s.ap=xp+(yp-xp)*s.core
        s.bp=yp+(xp-yp)*s.core
        s.astep=2+2*s.core; s.bstep=4-2*s.core
        s.abit=s.x+(s.y-s.x)*s.core; s.bbit=s.y+(s.x-s.y)*s.core
        s.up=me+8; s.dn=me-8
        s.hasup=s.z<3; s.hasdn=s.z>0
    def barrier(s,extra=None):
        bar=pltpu.get_barrier_semaphore()
        for p in (s.sib,s.ap,s.bp): pl.semaphore_signal(bar,inc=1,device_id=(p,),device_id_type=MESH)
        @pl.when(s.hasup)
        def _(): pl.semaphore_signal(bar,inc=1,device_id=(s.up,),device_id_type=MESH)
        @pl.when(s.hasdn)
        def _(): pl.semaphore_signal(bar,inc=1,device_id=(s.dn,),device_id_type=MESH)
        more=0 if extra is None else extra
        pl.semaphore_wait(bar,3+jnp.where(s.hasup,1,0)+jnp.where(s.hasdn,1,0)+more)
class Gather:
    K = 3

    def __init__(s, c, own, w, ssem, rsem, lsem):
        s.c, s.own, s.w, s.ssem, s.rsem, s.lsem = c, own, w, ssem, rsem, lsem
        s.ns = 0
        s.pend = []

    def slot(s, dev, k):
        return s.rsem.at[dev * s.K + k]

    @staticmethod
    def when(conds, fn):
        if conds:
            pl.when(functools.reduce(jnp.logical_and, [f() for f in conds]))(fn)
        else:
            fn()

    def send(s, src, dev, k, to, outer, *conds):
        i = s.ns
        s.ns += 1
        cp = pltpu.make_async_remote_copy(
            src, s.w.at[dev, k], s.ssem.at[i], s.slot(dev, k), device_id=(to,), device_id_type=MESH
        )
        s.pend.append((i, outer + list(conds)))
        s.when(list(conds), cp.start)

    def step(s, text):
        kind = text[0]
        zz, k = int(text[-2]), int(text[-1])
        if kind == "o":
            s.give(text[1], zz, k)
        else:
            s.item(kind, zz, k)

    def give(s, route, zz, k):
        c = s.c
        to, conds = dict(
            d=(c.dn, [lambda: c.hasdn]), u=(c.up, [lambda: c.hasup]), b=(c.bp, []), a=(c.ap, []), s=(c.sib, [])
        )[route]
        here = [lambda: c.z == zz]
        s.when(here, lambda: s.send(s.own.at[k], c.me, k, to, here, *conds))

    def item(s, kind, zz, k):
        c = s.c
        src = c.me + 8 * (zz - c.z)
        if kind in "ac":
            src = src + c.astep * (1 - 2 * c.abit)
        if kind in "bc":
            src = src + c.bstep * (1 - 2 * c.bbit)
        outer = [lambda: c.z != zz] if kind == "z" else []

        def body():
            s.wait(src, k)
            r = s.w.at[src, k]
            if kind == "z":
                if zz < 2:
                    s.send(r, src, k, c.up, outer, lambda: c.z > zz, lambda: c.hasup)
                if zz > 1:
                    s.send(r, src, k, c.dn, outer, lambda: c.z < zz, lambda: c.hasdn)
            if kind in "za":
                s.send(r, src, k, c.bp, outer)
            if kind == "z":
                s.send(r, src, k, c.ap, outer)
            s.send(r, src, k, c.sib, outer)

        s.when(outer, body)

    def wait(s, dev, k):
        r = s.w.at[dev, k]
        pltpu.make_async_copy(r, r, s.slot(dev, k)).wait()

    def keep(s):
        for k in range(s.K):
            pltpu.make_async_copy(s.own.at[k], s.w.at[s.c.me, k], s.lsem.at[k]).start()

    def kept(s, k):
        pltpu.make_async_copy(s.own.at[k], s.w.at[s.c.me, k], s.lsem.at[k]).wait()

    def sibling(s, first, last, ks):
        def one(i, _):
            for k in ks:
                s.wait(2 * i + 1 - s.c.core, k)
            return 0

        lax.fori_loop(first, last, one, 0)

    def sent(s):
        for i, conds in s.pend:
            r = s.w.at[0, 0]
            s.when(conds, pltpu.make_async_copy(r, r, s.ssem.at[i]).wait)


class Vector:
    def __init__(s, c, own, vec, sem):
        s.c, s.own, s.vec, s.sem = c, own, vec, sem
        s.n = 31

    def tell(s):
        bar = pltpu.get_barrier_semaphore()

        @pl.when(s.c.me != s.n)
        def _():
            pl.semaphore_signal(bar, inc=1, device_id=(s.n,), device_id_type=MESH)

    def copy(s, to):
        return pltpu.make_async_remote_copy(
            s.own, s.vec, s.sem.at[to], s.sem.at[s.n], device_id=(to,), device_id_type=MESH
        )

    def start(s):
        @pl.when(s.c.me == s.n)
        def _():
            s.vec[...] = s.own[...]

            def one(i, _):
                s.copy(i).start()
                return 0

            lax.fori_loop(0, s.n, one, 0)

    def wait(s):
        @pl.when(s.c.me != s.n)
        def _():
            pltpu.make_async_copy(s.vec, s.vec, s.sem.at[s.n]).wait()

    def sent(s):
        @pl.when(s.c.me == s.n)
        def _():
            def one(i, _):
                s.copy(i).wait_send()
                return 0

            lax.fori_loop(0, s.n, one, 0)

class Reduce:
    K = 3

    @staticmethod
    def scratch(lo, hi, stage):
        nz = hi - lo + 1
        pieces = lambda n: pltpu.VMEM((n, 128, D), BF)
        dma = lambda n: pltpu.SemaphoreType.DMA((n,))
        sizes = [12 * nz, 6 * nz, 3 * nz, 3 * nz + 3]
        return (
            [pieces(n) for n in sizes]
            + [pieces(stage)]
            + [dma(12 * nz)]
            + [dma(n) for n in sizes]
            + [dma(12 * nz), dma(stage)]
        )

    def __init__(s, c, lo, hi, parts, out, scr, scale, order, direct=False, auto=True):
        s.auto = auto
        s.c, s.lo, s.hi, s.parts, s.out, s.scale, s.order, s.direct = c, lo, hi, parts, out, scale, order, direct
        s.S, s.B, s.A, s.Z, s.stage, s.sent_s, s.got_s, s.got_b, s.got_a, s.got_z, s.sent, s.loaded = scr
        s.nst = s.stage.shape[0]
        s.nz = hi - lo + 1
        s.later = []
        s.waits = []
        s.steps = [functools.partial(s.item, i) for i in range(len(order))]

    def owner(s, zz, fb, fa, core):
        c = s.c
        astep = 2 + 2 * core
        bstep = 4 - 2 * core
        abit = c.x + (c.y - c.x) * core
        bbit = c.y + (c.x - c.y) * core
        return zz * 8 + core + bstep * (bbit + fb * (1 - 2 * bbit)) + astep * (abit + fa * (1 - 2 * abit))

    def source(s, p, fn):
        if len(s.parts) == 1:
            lo, hi, ref = s.parts[0]
            fn(ref.at[p - lo])
            return
        for lo, hi, ref in s.parts:

            @pl.when(jnp.logical_and(p >= lo, p < hi))
            def _():
                fn(ref.at[jnp.clip(p - lo, 0, hi - lo - 1)])

    def slot(s, zz, fb, fa, k):
        return (((zz - s.lo) * 2 + fb) * 2 + fa) * s.K + k

    def places(s, order=None):
        for kind, zz, fa, k in order or s.order:
            if kind != "f":
                yield zz, 1 if kind == "b" else 0, fa, k

    def zero(s):
        c = s.c

        def clear(n):
            s.Z[n] = jnp.zeros((128, D), BF)

        for n in range(3 * s.nz + 3):
            at_zero = n < 3 * s.nz
            at_three = n >= 3 * s.nz or s.lo + n // 3 < 3
            if at_zero:
                pl.when(c.z == 0)(functools.partial(clear, n))
            if at_three:
                pl.when(c.z == 3)(functools.partial(clear, n))

    def to_sibling(s, order=None):
        c = s.c
        for zz, fb, fa, k in s.places(order):
            n = s.slot(zz, fb, fa, k)

            def go(r, n=n):
                pltpu.make_async_remote_copy(
                    r, s.S.at[n], s.sent_s.at[n], s.got_s.at[n], device_id=(c.sib,), device_id_type=MESH
                ).start()

            s.source(s.owner(zz, fb, fa, 1 - c.core) * s.K + k, go)

    def load(s, i):
        if s.direct or i >= len(s.order):
            return
        kind, zz, fa, k = s.order[i]
        n = i % s.nst

        def go(r):
            pltpu.make_async_copy(r, s.stage.at[n], s.loaded.at[n]).start()

        s.source(s.owner(zz, 1 if kind == "b" else 0, fa, s.c.core) * s.K + k, go)

    def prefetch(s):
        for i in range(s.nst - 1):
            s.load(i)

    def flush(s):
        for f in s.later:
            f()
        s.later = []

    @staticmethod
    def wait(ref, sem):
        pltpu.make_async_copy(ref, ref, sem).wait()

    @staticmethod
    def sum(srcs, dst, scale=None):
        def rows(r, _):
            rr = pl.ds(pl.multiple_of(r * 16, 16), 16)
            t = srcs[0][rr, :].astype(F32)
            for q in srcs[1:]:
                t = t + q[rr, :].astype(F32)
            if scale is not None:
                t = t * scale
            dst[rr, :] = t.astype(dst.dtype)
            return 0

        lax.fori_loop(0, 8, rows, 0)

    def item(s, i):
        c, K = s.c, s.K
        kind, zz, fa, k = s.order[i]
        fb = 1 if kind == "b" else 0
        if s.direct:
            lo, hi, ref = s.parts[0]
            own = ref.at[s.owner(zz, fb, fa, c.core) * K + k - lo]
        else:
            own = s.stage.at[i % s.nst]
            s.wait(own, s.loaded.at[i % s.nst])
        s.flush()
        n = s.slot(zz, fb, fa, k)
        out = s.S.at[n]
        bi = ((zz - s.lo) * 2 + fa) * K + k
        zi = (zz - s.lo) * K + k
        z2 = s.nz * K + k

        def gather(kinds):
            srcs = [own]
            if "S" in kinds:
                srcs.append((out, s.got_s.at[n]))
            if "B" in kinds:
                srcs.append((s.B.at[bi], s.got_b.at[bi]))
            if "A" in kinds:
                srcs.append((s.A.at[zi], s.got_a.at[zi]))
            for pair in srcs[1:]:
                s.wait(*pair)
            return srcs[:1] + [ref for ref, _ in srcs[1:]]

        def send(dst, sem, to):
            return pltpu.make_async_remote_copy(
                out, dst, s.sent.at[n], sem, device_id=(to,), device_id_type=MESH
            )

        if kind == "b":
            s.sum(gather("S"), out)
            s.later.append(send(s.B.at[bi], s.got_b.at[bi], c.bp).start)
            s.waits.append((n, None))
        elif kind == "a":
            s.sum(gather("SB"), out)
            s.later.append(send(s.A.at[zi], s.got_a.at[zi], c.ap).start)
            s.waits.append((n, None))
        elif kind == "z":

            @pl.when(c.z != zz)
            def _():
                srcs = gather("SBA")
                comes = jnp.where(c.z <= zz, c.z, 3 - c.z)
                pl.when(comes > 0)(functools.partial(s.wait, s.Z.at[zi], s.got_z.at[zi]))
                s.sum(srcs + [s.Z.at[zi]], out)

            def on():
                @pl.when(c.z < zz)
                def _():
                    send(s.Z.at[zi], s.got_z.at[zi], c.up).start()

                to = jnp.where(c.z == zz + 1, z2, zi)

                @pl.when(c.z > zz)
                def _():
                    send(s.Z.at[to], s.got_z.at[to], c.dn).start()

            s.later.append(on)
            s.waits.append((n, zz))
        else:

            @pl.when(c.z == zz)
            def _():
                srcs = gather("SBA")
                pl.when(c.hasdn)(functools.partial(s.wait, s.Z.at[zi], s.got_z.at[zi]))
                pl.when(c.hasup)(functools.partial(s.wait, s.Z.at[z2], s.got_z.at[z2]))
                s.sum(srcs + [s.Z.at[zi], s.Z.at[z2]], s.out.at[k], s.scale)

        if s.auto:
            s.load(i + s.nst - 1)

    def finish(s):
        s.flush()
        for n, zz in s.waits:
            w = functools.partial(s.wait, s.S.at[0], s.sent.at[n])
            if zz is None:
                w()
            else:
                pl.when(s.c.z != zz)(w)

        for place in s.places():
            s.wait(s.S.at[0], s.sent_s.at[s.slot(*place)])


BACK_STEPS = (
    ("b301", "b211", "b310", "b212",),
    ("b312", "b300", "b210",),
    ("b311", "b110", "a211", "b100", "b201",),
    (),
    (),
    ("b302",),
    ("a311",),
    ("a310",),
    ("z301", "a312", "a210",),
    ("z300", "b200", "a110", "b202",),
    ("a212", "b111", "z302", "z201",),
    (),
    ("z200", "b112",),
    ("b101", "a111", "z100",),
    ("b102", "z202", "f302", "a112", "f301", "f300", "z101",),
    ("f101", "f201", "f100", "f202", "z102",),
    ("f102", "f200",),
)
TAIL_STEPS = (
    (),
    (),
    ("b000", "b010",),
    ("b011", "b001",),
    ("a010", "a011", "b012", "b002",),
    ("z000",),
    ("a012", "f000", "z001",),
    ("f001", "z002",),
    ("f002",),
)


def reduce_order(groups):
    order = [(t[0], int(t[1]), int(t[2]), int(t[3])) for g in groups for t in g]
    ends = [sum(len(g) for g in groups[: i + 1]) for i in range(len(groups))]
    return order, [list(range(e - len(g), e)) for e, g in zip(ends, groups)]


def qkv_kernel(x_ref, vec_ref, w_ref, out_ref, n_ref):
    j = pl.program_id(0)

    @pl.when(j == 0)
    def _():
        for i in range(2):

            def block(rows, dst):
                v = x_ref[i, rows, :].astype(F32)
                c = v - jnp.mean(v, axis=1, keepdims=True)
                rc = lax.rsqrt(jnp.mean(c * c, axis=1, keepdims=True) + EPS)
                return (c * rc * (1.0 + vec_ref[8:9, :]) + vec_ref[9:10, :]).astype(BF)

            def one(c, _):
                n_ref[i, rows_at(c), :] = block(rows_at(c), None)
                return 0

            lax.fori_loop(0, 18, one, 0)
            last = block(slice(576, 577), None).astype(F32)
            n_ref[i, 576:592, :] = jnp.concatenate([last, jnp.zeros((15, D), F32)], axis=0).astype(BF)

    w = w_ref[...].reshape(D, D)
    bias = jnp.where(j == 0, vec_ref[0:1, :], jnp.where(j == 2, vec_ref[1:2, :], 0.0))
    for i in range(2):
        out_ref[0, i] = (nn(n_ref[i], w) + bias).astype(BF)


def qkv(x, vec, w):
    return pl.pallas_call(
        qkv_kernel,
        grid=(3,),
        in_specs=[full((2, S, D)), full((16, D)), pl.BlockSpec((8, 1, 128, D), lambda j: (0, j, 0, 0))],
        out_specs=[pl.BlockSpec((1, 2, SQ, D), lambda j: (j, 0, 0, 0)), full((2, SQ, D))],
        out_shape=[jax.ShapeDtypeStruct((3, 2, SQ, D), BF), jax.ShapeDtypeStruct((2, SQ, D), BF)],
        compiler_params=pltpu.CompilerParams(vmem_limit_bytes=VMEM_ALL),
        name="qkv",
    )(x, vec, w.reshape(32, 3, 128, D))


def padded(v):
    return jnp.concatenate([v, jnp.zeros((640 - SQ, 128), v.dtype)], axis=0)


def attend_pair(q, k, v):
    lane = lax.broadcasted_iota(jnp.int32, (1, 128), 1)
    k = padded(k)
    v = padded(v)
    outs = []
    for h in range(2):
        mine = lane < 64 if h == 0 else lane >= 64
        s = nt(jnp.where(mine, q, jnp.zeros_like(q)), k)
        s = jnp.concatenate([s[:, :512], jnp.where(lane < S - 512, s[:, 512:], -1e30)], axis=1)
        top = jnp.max(s, axis=1, keepdims=True)
        p = jnp.exp2((s - top) * SCORE)
        total = jnp.sum(p, axis=1, keepdims=True)
        outs.append(nn(p.astype(BF), v) * (1.0 / total))
    return jnp.where(lane < 64, outs[0], outs[1]).astype(BF)


def attend_kernel(q_ref, k_ref, v_ref, o_ref):
    half = SQ // 2
    for r in range(2):
        rows = slice(r * half, (r + 1) * half)
        o_ref[0, rows, :] = attend_pair(q_ref[0, 0, rows, :], k_ref[0, 0], v_ref[0, 0])


def attend(z):
    spec = lambda j: pl.BlockSpec((1, 1, SQ, 128), lambda i, h: (j, i, 0, h))
    return pl.pallas_call(
        attend_kernel,
        grid=(2, 8),
        in_specs=[spec(0), spec(1), spec(2)],
        out_specs=pl.BlockSpec((1, SQ, 128), lambda i, h: (i, 0, h)),
        out_shape=jax.ShapeDtypeStruct((2, SQ, D), BF),
        compiler_params=pltpu.CompilerParams(vmem_limit_bytes=VMEM_ALL),
        name="attend",
    )(z, z, z)


def norm_block(v, vec_ref):
    v = v.astype(F32)
    ce = v - jnp.mean(v, axis=1, keepdims=True)
    rc = lax.rsqrt(jnp.mean(ce * ce, axis=1, keepdims=True) + EPS)
    return (ce * rc * (1.0 + vec_ref[8:9, :]) + vec_ref[9:10, :]).astype(BF)


def norm_one(x_ref, vec_ref, n_ref):
    for i in range(2):

        def one(c, _):
            n_ref[i, rows_at(c), :] = norm_block(x_ref[i, rows_at(c), :], vec_ref)
            return 0

        lax.fori_loop(0, 18, one, 0)
        last = norm_block(x_ref[i, 576:577, :], vec_ref).astype(F32)
        n_ref[i, 576:592, :] = jnp.concatenate([last, jnp.zeros((15, D), F32)], axis=0).astype(BF)


FRONT_STEPS = (
    ("oa31", "oa30", "ou00", "oa01", "od11", "ob20", "os21", "os00", "os31", "ob31", "ob30", "ou31", "ob00", "oa32", "ou01", "ob10", "oa20", "ob21", "od32", "oa10", "z00",),
    ("od10", "os01", "ob01", "od31", "b00", "ou32", "oa00", "z01", "ou02", "ob02", "od20", "od12", "a00", "os12", "z02", "os30", "a01", "os02", "oa02", "ob32", "b02", "od30", "a02", "od21", "os32", "oa21", "os20", "os11", "oa11", "ou20", "ob22", "oa22", "ob12", "z10", "c00", "z11", "ou10", "c01", "os10", "od22", "ob11", "b01", "ou11",),
    ("z12", "z20", "os22", "z21", "ou21", "ou12", "oa12", "c02",),
    ("a11",),
    ("a10", "z22", "b10", "ou22",),
    ("b11", "a21", "a20",),
    ("ou30", "a12",),
    (),
    ("a22", "z31",),
    (),
    (),
    (),
    ("z30", "c10", "z32", "b20",),
    (),
    ("b31", "a30",),
    (),
    ("c20", "b30",),
    ("a31", "c21", "c12", "b22", "c11", "a32",),
    ("b21", "c30", "b32", "c22",),
    ("b12", "c31",),
    ("c32",),
)


def front_kernel(own, vec_own, x_ref, w, vec, z_ref, n_ref, mix_ref, vlow, wq, qsem, vsem, ssem, rsem, lsem):
    c = Ctx()
    g = Gather(c, own, w, ssem, rsem, lsem)
    vector = Vector(c, vec_own, vlow, vsem)
    vector.tell()
    c.barrier(jnp.where(c.me == 31, 31, 0))
    vector.start()
    g.keep()

    def take(n):
        for text in FRONT_STEPS[n]:
            g.step(text)

    take(0)
    vector.wait()
    vec[...] = vlow[...].astype(F32)
    norm_one(x_ref, vec, n_ref)
    for j in range(3):
        take(1 + j)
        g.kept(j)
        g.sibling(0, 4, (j,))
        load = pltpu.make_async_copy(w.at[0:8, j], wq.at[j % 2], qsem.at[j])
        load.start()
        load.wait()
        for i in range(2):
            r = nn(n_ref[i], wq[j % 2].reshape(D, D))
            if j != 1:
                r = r + vec[j // 2 : j // 2 + 1, :]
            z_ref[j, i] = r.astype(BF)

    def pair(t, _):
        for n in range(16):
            if FRONT_STEPS[4 + n]:

                @pl.when(t == n)
                def _():
                    take(4 + n)

        i = t // 8
        cols = pl.ds(pl.multiple_of((t % 8) * 128, 128), 128)
        half = SQ // 2
        k = z_ref[1, i, :, cols]
        v = z_ref[2, i, :, cols]
        for r in range(2):
            rows = slice(r * half, (r + 1) * half)
            mix_ref[i, rows, cols] = attend_pair(z_ref[0, i, rows, cols], k, v)
        return 0

    lax.fori_loop(0, 16, pair, 0)
    take(20)
    g.sibling(4, 16, (0, 1, 2))
    g.sent()
    vector.sent()


def front(own, vec_own, x):
    vm = pl.BlockSpec(memory_space=pltpu.VMEM)
    dma = lambda n: pltpu.SemaphoreType.DMA((n,))
    return pl.pallas_call(
        front_kernel,
        in_specs=[vm, vm, vm],
        out_specs=[pl.BlockSpec(memory_space=pl.ANY), vm, vm, vm, vm],
        out_shape=[
            jax.ShapeDtypeStruct((32, 3, 128, D), BF),
            jax.ShapeDtypeStruct((16, D), F32),
            jax.ShapeDtypeStruct((3, 2, SQ, D), BF),
            jax.ShapeDtypeStruct((2, SQ, D), BF),
            jax.ShapeDtypeStruct((2, SQ, D), BF),
        ],
        scratch_shapes=[pltpu.VMEM((16, D), BF), pltpu.VMEM((2, 8, 128, D), BF), dma(3), dma(32)]
        + [dma(240), dma(96), dma(3)],
        compiler_params=pltpu.CompilerParams(collective_id=1, has_side_effects=True, vmem_limit_bytes=VMEM_ALL),
        name="front",
    )(own, vec_own, x)


def attend_back_pair(q, k, v, do):
    lane = lax.broadcasted_iota(jnp.int32, (1, 128), 1)
    real = lax.broadcasted_iota(jnp.int32, (16, 1), 0) < S - 576
    q = padded(q)
    do = padded(do)
    dqs, dks, dvs = [], [], []
    for h in range(2):
        mine = lane < 64 if h == 0 else lane >= 64
        s = nt(jnp.where(mine, k, jnp.zeros_like(k)), q)
        s = jnp.concatenate([s[:576], jnp.where(real, s[576:], -1e30)], axis=0)
        top = jnp.max(s, axis=0, keepdims=True)
        p = jnp.exp2((s - top) * SCORE)
        p = p * (1.0 / jnp.sum(p, axis=0, keepdims=True))
        dvs.append(nn(p.astype(BF), do))
        dp = nt(jnp.where(mine, v, jnp.zeros_like(v)), do)
        ds = (p * (dp - jnp.sum(p * dp, axis=0, keepdims=True))).astype(BF)
        dks.append(nn(ds, q))
        dqs.append(tn(ds, k))
    pick = lambda pair, scale: (jnp.where(lane < 64, pair[0], pair[1]) * scale).astype(BF)
    return pick(dqs, 0.125)[:SQ], pick(dks, 0.125), pick(dvs, 1.0)


def attend_back_kernel(q_ref, k_ref, v_ref, do_ref, out_ref):
    dq, dk, dv = attend_back_pair(q_ref[0, 0], k_ref[0, 0], v_ref[0, 0], do_ref[0])
    out_ref[0, 0] = dq
    out_ref[1, 0] = dk
    out_ref[2, 0] = dv


def attend_back(z, do):
    spec = lambda j: pl.BlockSpec((1, 1, SQ, 128), lambda i, h: (j, i, 0, h))
    return pl.pallas_call(
        attend_back_kernel,
        grid=(2, 8),
        in_specs=[spec(0), spec(1), spec(2), pl.BlockSpec((1, SQ, 128), lambda i, h: (i, 0, h))],
        out_specs=pl.BlockSpec((3, 1, SQ, 128), lambda i, h: (0, i, 0, h)),
        out_shape=jax.ShapeDtypeStruct((3, 2, SQ, D), BF),
        compiler_params=pltpu.CompilerParams(vmem_limit_bytes=VMEM_ALL),
        name="attend_back",
    )(z, z, z, do)


def mlp_kernel(x_ref,g_ref,mix_ref,vec_ref,wo_ref,wu_ref,wd_ref,
               out_ref,gup_ref,gdn_ref,gout_ref,dmix_ref,dhid_ref,gvec_ref,
               n2,gs,acc,dn,stat,*,FB,NB):
    jb=pl.program_id(0)
    hid=dhid_ref
    @pl.when(jb==0)
    def _():
        wo=wo_ref[...].reshape(D,D)
        for i in range(2):
            hid[i*SQ:(i+1)*SQ,:]=nn(mix_ref[i],wo)
            gs[i*SQ:i*SQ+576,:]=g_ref[i,:576,:]
            gs[i*SQ+576:(i+1)*SQ,:]=jnp.concatenate([g_ref[i,576:577,:].astype(F32),jnp.zeros((15,D),F32)],axis=0).astype(BF)
            def addx(c,_):
                r=pl.multiple_of(c*CH,CH)
                hid[pl.ds(i*SQ+r,CH),:]+=x_ref[i,pl.ds(r,CH),:].astype(F32)+vec_ref[2:3,:]
                return 0
            lax.fori_loop(0,18,addx,0)
            hid[i*SQ+576:i*SQ+577,:]+=x_ref[i,576:577,:].astype(F32)+vec_ref[2:3,:]
        acc[...]=jnp.zeros_like(acc); dn[...]=jnp.zeros_like(dn)
        gvec_ref[...]=jnp.zeros_like(gvec_ref)
        def ln(c,_):
            r=pl.ds(pl.multiple_of(c*CH,CH),CH)
            h=hid[r,:]
            mu=jnp.mean(h,axis=1,keepdims=True)
            ce=h-mu
            rc=lax.rsqrt(jnp.mean(ce*ce,axis=1,keepdims=True)+EPS)
            n2[r,:]=(ce*rc*(1.0+vec_ref[10:11,:])+vec_ref[11:12,:]).astype(BF)
            stat[r,0:1]=mu; stat[r,1:2]=rc
            return 0
        lax.fori_loop(0,M//CH,ln,0)
        def gsum(c,a):
            r=pl.ds(pl.multiple_of(c*CH,CH),CH)
            return a+gs[r,:].astype(F32)
        t=lax.fori_loop(0,M//CH,gsum,jnp.zeros((CH,D),F32))
        gvec_ref[7:8,:]=jnp.sum(t,axis=0,keepdims=True)
    wu=wu_ref[...].reshape(D,FB); wd=wd_ref[...].reshape(FB,D)
    nper=D//FB
    row=vec_ref[pl.ds(3+jb//nper,1),:]
    bup=row[:,:FB]
    for t in range(1,nper): bup=jnp.where(jb%nper==t,row[:,t*FB:(t+1)*FB],bup)
    g=gs[...]; n=n2[...]
    acts=[];dps=[]
    pres=[nn(n[i*SQ:(i+1)*SQ],wu)+bup for i in range(2)]
    das=[nt(g[i*SQ:(i+1)*SQ],wd) for i in range(2)]
    for i in range(2):
        pre=pres[i]
        cdf=0.5*(1.0+lax.erf(pre*0.7071067811865476))
        act=(pre*cdf).astype(BF)
        slope=cdf+pre*0.3989422804014327*jnp.exp(-0.5*pre*pre)
        dp=(das[i]*slope).astype(BF)
        acc[i*SQ:(i+1)*SQ,:]+=nn(act,wd)
        dn[i*SQ:(i+1)*SQ,:]+=nt(dp,wu)
        acts.append(act);dps.append(dp)
    act=jnp.concatenate(acts,axis=0);dp=jnp.concatenate(dps,axis=0)
    gup_ref[...]=tn(n,dp).astype(BF).reshape(gup_ref.shape)
    gdn_ref[...]=tn(act,g).astype(BF).reshape(gdn_ref.shape)
    bsum=jnp.sum(dp.astype(F32),axis=0,keepdims=True)
    for t in range(nper):
        @pl.when(jb%nper==t)
        def _(): gvec_ref[pl.ds(3+jb//nper,1),t*FB:(t+1)*FB]=bsum
    @pl.when(jb==NB-1)
    def _():
        for i in range(2):
            def ob(c,_):
                r=pl.multiple_of(c*CH,CH)
                out_ref[i,pl.ds(r,CH),:]=(hid[pl.ds(i*SQ+r,CH),:]+(acc[pl.ds(i*SQ+r,CH),:]+vec_ref[7:8,:])).astype(BF)
                return 0
            lax.fori_loop(0,18,ob,0)
            out_ref[i,576:577,:]=(hid[i*SQ+576:i*SQ+577,:]+(acc[i*SQ+576:i*SQ+577,:]+vec_ref[7:8,:])).astype(BF)
        def bk(c,car):
            a,b,d=car
            r=pl.ds(pl.multiple_of(c*CH,CH),CH)
            mu=stat[r,0:1]; rc=stat[r,1:2]
            xh=(hid[r,:]-mu)*rc
            dd=dn[r,:]
            e=dd*(1.0+vec_ref[10:11,:])
            dh=gs[r,:].astype(F32)+rc*(e-jnp.mean(e,axis=1,keepdims=True)-xh*jnp.mean(e*xh,axis=1,keepdims=True))
            dhid_ref[r,:]=dh
            db=dh.astype(BF)
            n2[r,:]=db
            return (a+dd*xh,b+dd,d+db.astype(F32))
        zz=jnp.zeros((CH,D),F32)
        a,b,d=lax.fori_loop(0,M//CH,bk,(zz,zz,zz))
        gvec_ref[10:11,:]=jnp.sum(a,axis=0,keepdims=True)
        gvec_ref[11:12,:]=jnp.sum(b,axis=0,keepdims=True)
        gvec_ref[2:3,:]=jnp.sum(d,axis=0,keepdims=True)
        db=n2[...]
        wo=wo_ref[...].reshape(D,D)
        dmix_ref[...]=nt(db,wo).astype(BF).reshape(2,SQ,D)
        gout_ref[...]=tn(mix_ref[...].reshape(M,D),db).astype(BF).reshape(8,128,D)
def mlp(x,g,mix,vec,W,FB=512):
    NB=4096//FB; nper=D//FB
    W4=W.reshape(96,4,32,1024)
    return pl.pallas_call(functools.partial(mlp_kernel,FB=FB,NB=NB),grid=(NB,),
      in_specs=[full((2,S,D)),full((2,S,D)),full((2,SQ,D)),full((16,D)),
        pl.BlockSpec((8,128,D),lambda j:(3,0,0),pipeline_mode=pl.Buffered(1)),
        pl.BlockSpec((32,1,32,FB),lambda j:(1,j//nper,0,j%nper)),
        pl.BlockSpec((FB//128,128,D),lambda j:(64//(FB//128)+j,0,0))],
      out_specs=[full((2,S,D)),pl.BlockSpec((32,1,32,FB),lambda j:(0,j//nper,0,j%nper)),
        pl.BlockSpec((FB//128,128,D),lambda j:(j,0,0)),full((8,128,D)),full((2,SQ,D)),full((M,D)),full((16,D))],
      out_shape=[jax.ShapeDtypeStruct((2,S,D),BF),jax.ShapeDtypeStruct((32,4,32,D),BF),jax.ShapeDtypeStruct((32,128,D),BF),
        jax.ShapeDtypeStruct((8,128,D),BF),jax.ShapeDtypeStruct((2,SQ,D),BF),jax.ShapeDtypeStruct((M,D),F32),jax.ShapeDtypeStruct((16,D),F32)],
      scratch_shapes=[pltpu.VMEM((M,D),BF),pltpu.VMEM((M,D),BF),pltpu.VMEM((M,D),F32),pltpu.VMEM((M,D),F32),pltpu.VMEM((M,128),F32)],
      compiler_params=pltpu.CompilerParams(vmem_limit_bytes=67043328),name=f"mlp{FB}")(x,g,mix,vec,W,W4,W)


def tail_kernel(x_ref, dz_ref, n_ref, dhid_ref, vec_ref, w_ref, gvin_ref, gx_ref, gw_ref, gvec_ref, acc):
    j = pl.program_id(0)

    @pl.when(j == 0)
    def _():
        gvec_ref[...] = gvin_ref[...]
        acc[...] = jnp.zeros_like(acc)

    w = w_ref[...].reshape(D, D)
    dz = dz_ref[0].reshape(M, D)
    acc[...] += nt(dz, w)
    gw_ref[...] = tn(n_ref[...].reshape(M, D), dz).astype(BF).reshape(8, 1, 128, D)

    @pl.when(j != 1)
    def _():
        def add(c, t):
            return t + dz_ref[0, 0, pl.ds(c * 16, 16), :].astype(F32) + dz_ref[0, 1, pl.ds(c * 16, 16), :].astype(F32)

        t = lax.fori_loop(0, SQ // 16, add, jnp.zeros((16, D), F32))
        gvec_ref[pl.ds(j // 2, 1), :] = jnp.sum(t, axis=0, keepdims=True)

    @pl.when(j == 2)
    def _():
        def back(x, dd, dh):
            v = x.astype(F32)
            ce = v - jnp.mean(v, axis=1, keepdims=True)
            rc = lax.rsqrt(jnp.mean(ce * ce, axis=1, keepdims=True) + EPS)
            xh = ce * rc
            e = dd * (1.0 + vec_ref[8:9, :])
            g = dh + rc * (e - jnp.mean(e, axis=1, keepdims=True) - xh * jnp.mean(e * xh, axis=1, keepdims=True))
            return g.astype(BF), dd * xh, dd

        a = b = jnp.zeros((CH, D), F32)
        la = lb = jnp.zeros((1, D), F32)
        for i in range(2):

            def one(c, carry):
                r = rows_at(c)
                r2 = pl.ds(pl.multiple_of(i * SQ + c * CH, 16), CH)
                g, s1, s2 = back(x_ref[i, r, :], acc[r2, :], dhid_ref[r2, :])
                gx_ref[i, r, :] = g
                return carry[0] + s1, carry[1] + s2

            a, b = lax.fori_loop(0, 18, one, (a, b))
            r2 = slice(i * SQ + 576, i * SQ + 577)
            g, s1, s2 = back(x_ref[i, 576:577, :], acc[r2, :], dhid_ref[r2, :])
            gx_ref[i, 576:577, :] = g
            la, lb = la + s1, lb + s2
        gvec_ref[8:9, :] = jnp.sum(a, axis=0, keepdims=True) + la
        gvec_ref[9:10, :] = jnp.sum(b, axis=0, keepdims=True) + lb


def tail(x, dz, n1, dhid, vec, w, gvec):
    return pl.pallas_call(
        tail_kernel,
        grid=(3,),
        in_specs=[
            full((2, S, D)),
            pl.BlockSpec((1, 2, SQ, D), lambda j: (j, 0, 0, 0)),
            full((2, SQ, D)),
            full((M, D)),
            full((16, D)),
            pl.BlockSpec((8, 1, 128, D), lambda j: (0, j, 0, 0)),
            full((16, D)),
        ],
        out_specs=[full((2, S, D)), pl.BlockSpec((8, 1, 128, D), lambda j: (0, j, 0, 0)), full((16, D))],
        out_shape=[
            jax.ShapeDtypeStruct((2, S, D), BF),
            jax.ShapeDtypeStruct((8, 3, 128, D), BF),
            jax.ShapeDtypeStruct((16, D), F32),
        ],
        scratch_shapes=[pltpu.VMEM((M, D), F32)],
        compiler_params=pltpu.CompilerParams(vmem_limit_bytes=VMEM_ALL),
        name="tail",
    )(x, dz, n1, dhid, vec, w.reshape(32, 3, 128, D), gvec)

def back_kernel(z_ref, do_ref, *refs, lo, hi, ranges, scale):
    n = len(ranges)
    parts = [(a, b, r) for (a, b), r in zip(ranges, refs[:n])]
    dz_ref, chunk = refs[n : n + 2]
    c = Ctx()
    order, groups = reduce_order(BACK_STEPS)
    red = Reduce(c, lo, hi, parts, chunk, refs[n + 2 :], scale, order)
    red.zero()
    chunk[...] = jnp.zeros_like(chunk)
    c.barrier()
    red.to_sibling()
    red.prefetch()

    def pair(t, _):
        for m in range(16):
            if groups[m]:

                @pl.when(t == m)
                def _():
                    for i in groups[m]:
                        red.steps[i]()
                    red.flush()

        i = t // 8
        cols = pl.ds(pl.multiple_of((t % 8) * 128, 128), 128)
        dq, dk, dv = attend_back_pair(z_ref[0, i, :, cols], z_ref[1, i, :, cols], z_ref[2, i, :, cols], do_ref[i, :, cols])
        dz_ref[0, i, :, cols] = dq
        dz_ref[1, i, :, cols] = dk
        dz_ref[2, i, :, cols] = dv
        return 0

    lax.fori_loop(0, 16, pair, 0)
    for i in groups[16]:
        red.steps[i]()
    red.finish()


def back(z, do, parts, lo, hi, ranges, scale):
    vm = pl.BlockSpec(memory_space=pltpu.VMEM)
    return pl.pallas_call(
        functools.partial(back_kernel, lo=lo, hi=hi, ranges=ranges, scale=scale),
        in_specs=[vm, vm] + [pl.BlockSpec(memory_space=pl.ANY)] * len(parts),
        out_specs=[vm, vm],
        out_shape=[jax.ShapeDtypeStruct((3, 2, SQ, D), BF), jax.ShapeDtypeStruct((3, 128, D), F32)],
        scratch_shapes=Reduce.scratch(lo, hi, 4),
        compiler_params=pltpu.CompilerParams(collective_id=2, has_side_effects=True, vmem_limit_bytes=VMEM_ALL),
        name="back",
    )(z, do, *parts)


def back_norm(x, dd, dh, vec_ref):
    v = x.astype(F32)
    ce = v - jnp.mean(v, axis=1, keepdims=True)
    rc = lax.rsqrt(jnp.mean(ce * ce, axis=1, keepdims=True) + EPS)
    xh = ce * rc
    e = dd * (1.0 + vec_ref[8:9, :])
    g = dh + rc * (e - jnp.mean(e, axis=1, keepdims=True) - xh * jnp.mean(e * xh, axis=1, keepdims=True))
    return g.astype(BF), dd * xh


def tail_quick_kernel(
    x_ref, dz_ref, n_ref, dhid_ref, vec_ref, gvin_ref, w, gx_ref, chunk, gvec_ref, acc, gw, wq, qsem, *scr, scale
):
    c = Ctx()
    order, groups = reduce_order(TAIL_STEPS)
    red = Reduce(c, 0, 0, [(0, 24, gw)], chunk, scr, scale, order, direct=True)
    loads = [pltpu.make_async_copy(w.at[0:8, j], wq.at[j % 2], qsem.at[j]) for j in range(3)]
    loads[0].start()
    loads[1].start()
    red.zero()
    chunk[...] = jnp.zeros_like(chunk)
    gvec_ref[...] = gvin_ref[...]
    c.barrier()

    def take(n):
        for i in groups[n]:
            red.steps[i]()
        red.flush()

    def weights(j):
        g = tn(n_ref[...].reshape(M, D), dz_ref[j].reshape(M, D)).astype(BF)
        for d in range(8):
            gw[3 * d + j] = g[128 * d : 128 * (d + 1)]

    def colsum(j):
        def add(r, t):
            rr = pl.ds(pl.multiple_of(r * 16, 16), 16)
            return t + dz_ref[j, 0, rr, :].astype(F32) + dz_ref[j, 1, rr, :].astype(F32)

        t = lax.fori_loop(0, SQ // 16, add, jnp.zeros((16, D), F32))
        gvec_ref[j // 2 : j // 2 + 1, :] = jnp.sum(t, axis=0, keepdims=True)

    def inputs(j):
        loads[j].wait()
        wj = wq[j % 2].reshape(D, D)
        for i in range(2):
            r = nt(dz_ref[j, i], wj)
            rows = slice(i * SQ, (i + 1) * SQ)
            acc[rows, :] = r if j == 0 else acc[rows, :] + r

    some = lambda k: [o for o in order if o[3] == k]
    weights(0)
    colsum(0)
    red.to_sibling(some(0))
    weights(1)
    red.to_sibling(some(1))
    take(2)
    weights(2)
    colsum(2)
    red.to_sibling(some(2))
    take(3)
    for j in range(3):
        inputs(j)
        if j == 0:
            loads[2].start()
        take(4 + j)
    a = b = jnp.zeros((CH, D), F32)
    la = lb = jnp.zeros((1, D), F32)
    for i in range(2):

        def one(t, carry):
            r = rows_at(t)
            r2 = pl.ds(pl.multiple_of(i * SQ + t * CH, 16), CH)
            dd = acc[r2, :]
            g, s1 = back_norm(x_ref[i, r, :], dd, dhid_ref[r2, :], vec_ref)
            gx_ref[i, r, :] = g
            return carry[0] + s1, carry[1] + dd

        a, b = lax.fori_loop(0, 18, one, (a, b))
        r2 = slice(i * SQ + 576, i * SQ + 577)
        dd = acc[r2, :]
        g, s1 = back_norm(x_ref[i, 576:577, :], dd, dhid_ref[r2, :], vec_ref)
        gx_ref[i, 576:577, :] = g
        la, lb = la + s1, lb + dd
        take(7 + i)
    gvec_ref[8:9, :] = jnp.sum(a, axis=0, keepdims=True) + la
    gvec_ref[9:10, :] = jnp.sum(b, axis=0, keepdims=True) + lb
    red.finish()


def tail_quick(x, dz, n1, dhid, vec, gvec, w, scale):
    vm = pl.BlockSpec(memory_space=pltpu.VMEM)
    return pl.pallas_call(
        functools.partial(tail_quick_kernel, scale=scale),
        in_specs=[vm] * 6 + [pl.BlockSpec(memory_space=pl.ANY)],
        out_specs=[vm] * 3,
        out_shape=[
            jax.ShapeDtypeStruct((2, S, D), BF),
            jax.ShapeDtypeStruct((3, 128, D), F32),
            jax.ShapeDtypeStruct((16, D), F32),
        ],
        scratch_shapes=[
            pltpu.VMEM((M, D), F32),
            pltpu.VMEM((24, 128, D), BF),
            pltpu.VMEM((2, 8, 128, D), BF),
            pltpu.SemaphoreType.DMA((3,)),
        ]
        + Reduce.scratch(0, 0, 1),
        compiler_params=pltpu.CompilerParams(collective_id=3, has_side_effects=True, vmem_limit_bytes=VMEM_ALL),
        name="tail_quick",
    )(x, dz, n1, dhid, vec, gvec, w)


def close_kernel(chunk_a, chunk_b, gvec, wg, clip_ref, flat, e, es, ea, eb, ez, sem, *, scale):
    c = Ctx()
    me = c.me
    bar = pltpu.get_barrier_semaphore()
    others = [c.sib, c.ap, c.bp] + [lax.rem(me + 8 * i, 32) for i in (1, 2, 3)]
    for to in others:
        pl.semaphore_signal(bar, inc=1, device_id=(to,), device_id_type=MESH)
    first, last = me == 0, me == 31

    @pl.when(jnp.logical_not(first))
    def _():
        pl.semaphore_signal(bar, inc=1, device_id=(me - 1,), device_id_type=MESH)

    @pl.when(jnp.logical_not(last))
    def _():
        pl.semaphore_signal(bar, inc=1, device_id=(me + 1,), device_id_type=MESH)

    def unfold(src, k, kind):
        for t in range(8):
            cols = slice(128 * t, 128 * (t + 1))
            if kind == 0:
                flat[pl.ds(8 * k + t, 128, stride=24), :] = src[k, :, cols]
            elif kind == 1:
                flat[pl.ds(1024 * k + t, 128, stride=8), :] = src[k, :, cols]
            else:
                for j in range(4):
                    flat[pl.ds(1024 * k + 8 * j + t, 32, stride=32), :] = src[k, 32 * j : 32 * j + 32, cols]

    for k in range(3):
        p = 3 * me + k
        up = jnp.logical_and(p >= 32, p < 64)
        pl.when(c.z == 0)(functools.partial(unfold, chunk_b, k, 0))
        pl.when(up)(functools.partial(unfold, chunk_a, k, 2))
        pl.when(jnp.logical_and(c.z > 0, jnp.logical_not(up)))(functools.partial(unfold, chunk_a, k, 1))

    def square(i, t):
        v = flat[pl.ds(pl.multiple_of(i * 64, 64), 64), :]
        return t + v * v

    sq = jnp.sum(lax.fori_loop(0, 48, square, jnp.zeros((64, 128), F32)))
    e[0:12, :] = gvec[0:12, :]
    e[12:16, :] = jnp.full((4, D), sq, F32)
    pl.semaphore_wait(bar, 6 + jnp.where(first, 0, 1) + jnp.where(last, 0, 1))
    head = flat.at[0:96]
    room = flat.at[3072:3168]
    edge = pltpu.make_async_remote_copy(
        head, room, sem.at[14], sem.at[15], device_id=(jnp.maximum(me - 1, 0),), device_id_type=MESH
    )
    pl.when(jnp.logical_not(first))(edge.start)
    for n, (to, dst) in enumerate(((c.sib, es), (c.ap, ea), (c.bp, eb))):
        cp = pltpu.make_async_remote_copy(e, dst, sem.at[n], sem.at[3 + n], device_id=(to,), device_id_type=MESH)
        cp.start()
        cp.wait()
        e[...] = e[...] + dst[...]
    ez[c.z] = e[...]
    cps = []
    for i in (1, 2, 3):
        to = lax.rem(me + 8 * i, 32)
        cp = pltpu.make_async_remote_copy(
            e, ez.at[c.z], sem.at[6 + i], sem.at[9 + i], device_id=(to,), device_id_type=MESH
        )
        cp.start()
        cps.append(cp)
    for i in (1, 2, 3):
        cps[i - 1].wait_send()
        zz = lax.rem(c.z + 4 - i, 4)
        pltpu.make_async_copy(ez.at[zz], ez.at[zz], sem.at[9 + i]).wait()
    total = ((ez[0] + ez[1]) + ez[2]) + ez[3]
    vec = total[0:12, :]
    square_sum = (total[12:13, 0:128] + jnp.sum(vec * vec)) * (scale * scale)
    clip_ref[...] = jnp.broadcast_to(jnp.minimum(1.0, max_norm / (jnp.sqrt(square_sum) + 1e-06)), (8, 128))

    @pl.when(last)
    def _():
        for t in range(8):
            flat[pl.ds(3072 + t, 12, stride=8), :] = vec[:, 128 * t : 128 * (t + 1)]

    @pl.when(jnp.logical_not(last))
    def _():
        pltpu.make_async_copy(room, room, sem.at[15]).wait()

    pl.when(jnp.logical_not(first))(edge.wait_send)

    def block(i, _):
        wg[pl.ds(pl.multiple_of(i * 64, 64), 64), :] = flat[pl.ds(i * 64 + 3 * me, 64), :]
        return 0

    lax.fori_loop(0, 48, block, 0)
    wg[3072:3075, :] = flat[pl.ds(3072 + 3 * me, 3), :]


def close(chunk_a, chunk_b, gvec, scale):
    vm = pl.BlockSpec(memory_space=pltpu.VMEM)
    small = pltpu.VMEM((16, D), F32)
    return pl.pallas_call(
        functools.partial(close_kernel, scale=scale),
        in_specs=[vm] * 3,
        out_specs=[vm] * 2,
        out_shape=[jax.ShapeDtypeStruct((3075, 128), F32), jax.ShapeDtypeStruct((8, 128), F32)],
        scratch_shapes=[pltpu.VMEM((3168, 128), F32)]
        + [small] * 4
        + [pltpu.VMEM((4, 16, D), F32), pltpu.SemaphoreType.DMA((16,))],
        compiler_params=pltpu.CompilerParams(collective_id=4, has_side_effects=True, vmem_limit_bytes=VMEM_ALL),
        name="close",
    )(chunk_a, chunk_b, gvec)


def to_pieces(rows, first):
    n = rows.shape[0] // 128
    plain = rows.reshape(n, 128, D)
    three = rows.reshape(n // 3, 128, 3, D).transpose(0, 2, 1, 3).reshape(n, 128, D)
    four = rows.reshape(n, 32, 4, D).transpose(0, 2, 1, 3).reshape(n, 128, D)
    p = first + lax.broadcasted_iota(jnp.int32, (n, 1, 1), 0)
    return jnp.where(p < 24, three, jnp.where((p >= 32) & (p < 64), four, plain))


def from_pieces(pieces, first):
    n = pieces.shape[0]
    plain = pieces.reshape(n * 128, D)
    three = pieces.reshape(n // 3, 3, 128, D).transpose(0, 2, 1, 3).reshape(n * 128, D)
    four = pieces.reshape(n, 4, 32, D).transpose(0, 2, 1, 3).reshape(n * 128, D)
    p = first + lax.broadcasted_iota(jnp.int32, (n * 128, 1), 0) // 128
    return jnp.where(p < 24, three, jnp.where((p >= 32) & (p < 64), four, plain))


def update(params, moment_one, moment_two, weight_grad, clip_factor):
    clipped = clip_factor * weight_grad
    moment_one_new = beta_one * moment_one + (1.0 - beta_one) * clipped
    moment_two_new = beta_two * moment_two + (1.0 - beta_two) * clipped * clipped
    correct_one = 1.0 - beta_one**STEP
    correct_two = 1.0 - beta_two**STEP
    params_new = params - learn_rate * (
        moment_one_new / correct_one / (jnp.sqrt(moment_two_new / correct_two) + adam_eps) + decay_rate * params
    )
    return params_new, moment_one_new, moment_two_new


def shards(tokens, cotangent, params, moment_one, moment_two):
    n = lax.axis_size("dp")
    me = lax.axis_index("dp")
    shard_len = params.shape[0]
    images_all = tokens.shape[0] * n
    mats = PIECES * 128 * D
    scale = 1.0 / images_all
    if n == 32:
        unit = 128
        extra = 12 * D // unit
        own_units = shard_len // unit
        gap = extra // n
        low = params.reshape(own_units, unit)
        before = lax.ppermute(low[own_units - extra :].astype(BF), "dp", [(i, (i + 1) % n) for i in range(n)])
        joined = jnp.concatenate([before.astype(F32), low], axis=0)
        aligned = lax.dynamic_slice(joined, (extra - gap * me, 0), (own_units - gap, unit))
        own = to_pieces(aligned.reshape(-1, D), 3 * me).astype(BF)
        vec_own = jnp.pad(low[own_units - extra :].reshape(12, D), ((0, 4), (0, 0))).astype(BF)
        w, vec, z, n1, mixed = front(own, vec_own, tokens)
        flat_w = w.reshape(PIECES, 128, D)
        outputs, gup, gdn, gout, dmix, dhid, gvec = mlp(tokens, cotangent, mixed, vec, flat_w)
        parts = [gout, gup.reshape(32, 128, D), gdn]
        dz, chunk_a = back(z, dmix, parts, 1, 3, [(24, 32), (32, 64), (64, 96)], None)
        grad_tokens, chunk_b, gvec = tail_quick(tokens, dz, n1, dhid, vec, gvec, w, None)
        sums, clip = close(chunk_a, chunk_b, gvec, scale)
        weight_grad = sums.reshape(shard_len) * scale
        news = update(params, moment_one, moment_two, weight_grad, clip[0, 0])
        return (outputs, grad_tokens, weight_grad, *news)
    flat = lax.all_gather(params.astype(BF), "dp", axis=0, tiled=True)
    w = to_pieces(flat[:mats].reshape(-1, D), 0)
    vec = jnp.pad(flat[mats:].reshape(12, D).astype(F32), ((0, 4), (0, 0)))
    z, n1 = qkv(tokens, vec, w)
    mixed = attend(z)
    outputs, gup, gdn, gout, dmix, dhid, gvec = mlp(tokens, cotangent, mixed, vec, w)
    dz = attend_back(z, dmix)
    grad_tokens, gqkv, gvec = tail(tokens, dz, n1, dhid, vec, w, gvec)
    parts = [gqkv.reshape(24, 128, D), gout, gup.reshape(32, 128, D), gdn]
    flat = jnp.concatenate([from_pieces(jnp.concatenate(parts, axis=0), 0).reshape(-1), gvec[:12].reshape(-1).astype(BF)])
    arrived = lax.all_to_all(flat.reshape(n, shard_len), "dp", split_axis=0, concat_axis=0, tiled=True)
    weight_grad = jnp.sum(arrived.astype(F32), axis=0) * scale
    square_sum = lax.psum(jnp.sum(weight_grad * weight_grad), "dp")
    clip = jnp.minimum(1.0, max_norm / (jnp.sqrt(square_sum) + 1e-06))
    news = update(params, moment_one, moment_two, weight_grad, clip)
    return (outputs, grad_tokens, weight_grad, *news)


def solution(mesh):
    in_specs = (P("dp", None, None), P("dp", None, None), P("dp"), P("dp"), P("dp"))
    out_specs = (P("dp", None, None), P("dp", None, None), P("dp"), P("dp"), P("dp"), P("dp"))
    return jax.shard_map(shards, mesh=mesh, in_specs=in_specs, out_specs=out_specs, check_vma=False)
```

```python
import functools

import jax
import jax.numpy as jnp
from jax import lax
from jax.experimental import pallas as pl
from jax.experimental.pallas import tpu as pltpu
from jax.sharding import PartitionSpec as P

D = 1024
FF = 4096
S = 577
SQ = 592
M = 2 * SQ
CH = 32
PIECES = 96
STEP = 4
BF = jnp.bfloat16
F32 = jnp.float32
MESH = pl.DeviceIdType.MESH
VMEM_ALL = 67043328

EPS = 1e-06
max_norm = 1.0
beta_one = 0.9
beta_two = 0.95
learn_rate = 0.02
decay_rate = 0.05
adam_eps = 1e-08
SCORE = 0.125 * 1.4426950408889634


def nt(a, b):
    return lax.dot_general(a, b, (((1,), (1,)), ((), ())), preferred_element_type=F32)


def nn(a, b):
    return jnp.dot(a, b, preferred_element_type=F32)


def tn(a, b):
    return lax.dot_general(a, b, (((0,), (0,)), ((), ())), preferred_element_type=F32)


def rows_at(c):
    return pl.ds(pl.multiple_of(c * CH, CH), CH)


def full(shape):
    return pl.BlockSpec(shape, lambda *_: (0,) * len(shape), pipeline_mode=pl.Buffered(1))


class Ctx:
    def __init__(s):
        me=lax.axis_index("dp"); s.me=me
        s.core=me%2; s.x=(me//2)%2; s.y=(me//4)%2; s.z=me//8
        s.sib=me+1-2*s.core
        xp=me+2*(1-2*s.x); yp=me+4*(1-2*s.y)
        s.ap=xp+(yp-xp)*s.core
        s.bp=yp+(xp-yp)*s.core
        s.astep=2+2*s.core; s.bstep=4-2*s.core
        s.abit=s.x+(s.y-s.x)*s.core; s.bbit=s.y+(s.x-s.y)*s.core
        s.up=me+8; s.dn=me-8
        s.hasup=s.z<3; s.hasdn=s.z>0
    def barrier(s,extra=None):
        bar=pltpu.get_barrier_semaphore()
        for p in (s.sib,s.ap,s.bp): pl.semaphore_signal(bar,inc=1,device_id=(p,),device_id_type=MESH)
        @pl.when(s.hasup)
        def _(): pl.semaphore_signal(bar,inc=1,device_id=(s.up,),device_id_type=MESH)
        @pl.when(s.hasdn)
        def _(): pl.semaphore_signal(bar,inc=1,device_id=(s.dn,),device_id_type=MESH)
        more=0 if extra is None else extra
        pl.semaphore_wait(bar,3+jnp.where(s.hasup,1,0)+jnp.where(s.hasdn,1,0)+more)
class Gather:
    K = 3

    def __init__(s, c, own, w, ssem, rsem, lsem):
        s.c, s.own, s.w, s.ssem, s.rsem, s.lsem = c, own, w, ssem, rsem, lsem
        s.ns = 0
        s.pend = []

    def slot(s, dev, k):
        return s.rsem.at[dev * s.K + k]

    @staticmethod
    def when(conds, fn):
        if conds:
            pl.when(functools.reduce(jnp.logical_and, [f() for f in conds]))(fn)
        else:
            fn()

    def send(s, src, dev, k, to, outer, *conds):
        i = s.ns
        s.ns += 1
        cp = pltpu.make_async_remote_copy(
            src, s.w.at[dev, k], s.ssem.at[i], s.slot(dev, k), device_id=(to,), device_id_type=MESH
        )
        s.pend.append((i, outer + list(conds)))
        s.when(list(conds), cp.start)

    def step(s, text):
        kind = text[0]
        zz, k = int(text[-2]), int(text[-1])
        if kind == "o":
            s.give(text[1], zz, k)
        else:
            s.item(kind, zz, k)

    def give(s, route, zz, k):
        c = s.c
        to, conds = dict(
            d=(c.dn, [lambda: c.hasdn]), u=(c.up, [lambda: c.hasup]), b=(c.bp, []), a=(c.ap, []), s=(c.sib, [])
        )[route]
        here = [lambda: c.z == zz]
        s.when(here, lambda: s.send(s.own.at[k], c.me, k, to, here, *conds))

    def item(s, kind, zz, k):
        c = s.c
        src = c.me + 8 * (zz - c.z)
        if kind in "ac":
            src = src + c.astep * (1 - 2 * c.abit)
        if kind in "bc":
            src = src + c.bstep * (1 - 2 * c.bbit)
        outer = [lambda: c.z != zz] if kind == "z" else []

        def body():
            s.wait(src, k)
            r = s.w.at[src, k]
            if kind == "z":
                if zz < 2:
                    s.send(r, src, k, c.up, outer, lambda: c.z > zz, lambda: c.hasup)
                if zz > 1:
                    s.send(r, src, k, c.dn, outer, lambda: c.z < zz, lambda: c.hasdn)
            if kind in "za":
                s.send(r, src, k, c.bp, outer)
            if kind == "z":
                s.send(r, src, k, c.ap, outer)
            s.send(r, src, k, c.sib, outer)

        s.when(outer, body)

    def wait(s, dev, k):
        r = s.w.at[dev, k]
        pltpu.make_async_copy(r, r, s.slot(dev, k)).wait()

    def keep(s):
        for k in range(s.K):
            pltpu.make_async_copy(s.own.at[k], s.w.at[s.c.me, k], s.lsem.at[k]).start()

    def kept(s, k):
        pltpu.make_async_copy(s.own.at[k], s.w.at[s.c.me, k], s.lsem.at[k]).wait()

    def sibling(s, first, last, ks):
        def one(i, _):
            for k in ks:
                s.wait(2 * i + 1 - s.c.core, k)
            return 0

        lax.fori_loop(first, last, one, 0)

    def sent(s):
        for i, conds in s.pend:
            r = s.w.at[0, 0]
            s.when(conds, pltpu.make_async_copy(r, r, s.ssem.at[i]).wait)


class Vector:
    def __init__(s, c, own, vec, sem):
        s.c, s.own, s.vec, s.sem = c, own, vec, sem
        s.n = 31

    def tell(s):
        bar = pltpu.get_barrier_semaphore()

        @pl.when(s.c.me != s.n)
        def _():
            pl.semaphore_signal(bar, inc=1, device_id=(s.n,), device_id_type=MESH)

    def copy(s, to):
        return pltpu.make_async_remote_copy(
            s.own, s.vec, s.sem.at[to], s.sem.at[s.n], device_id=(to,), device_id_type=MESH
        )

    def start(s):
        @pl.when(s.c.me == s.n)
        def _():
            s.vec[...] = s.own[...]

            def one(i, _):
                s.copy(i).start()
                return 0

            lax.fori_loop(0, s.n, one, 0)

    def wait(s):
        @pl.when(s.c.me != s.n)
        def _():
            pltpu.make_async_copy(s.vec, s.vec, s.sem.at[s.n]).wait()

    def sent(s):
        @pl.when(s.c.me == s.n)
        def _():
            def one(i, _):
                s.copy(i).wait_send()
                return 0

            lax.fori_loop(0, s.n, one, 0)

class Reduce:
    K = 3

    @staticmethod
    def scratch(lo, hi, stage):
        nz = hi - lo + 1
        pieces = lambda n: pltpu.VMEM((n, 128, D), BF)
        dma = lambda n: pltpu.SemaphoreType.DMA((n,))
        sizes = [12 * nz, 6 * nz, 3 * nz, 3 * nz + 3]
        return (
            [pieces(n) for n in sizes]
            + [pieces(stage)]
            + [dma(12 * nz)]
            + [dma(n) for n in sizes]
            + [dma(12 * nz), dma(stage)]
        )

    def __init__(s, c, lo, hi, parts, out, scr, scale, order, direct=False, auto=True):
        s.auto = auto
        s.c, s.lo, s.hi, s.parts, s.out, s.scale, s.order, s.direct = c, lo, hi, parts, out, scale, order, direct
        s.S, s.B, s.A, s.Z, s.stage, s.sent_s, s.got_s, s.got_b, s.got_a, s.got_z, s.sent, s.loaded = scr
        s.nst = s.stage.shape[0]
        s.nz = hi - lo + 1
        s.later = []
        s.waits = []
        s.steps = [functools.partial(s.item, i) for i in range(len(order))]

    def owner(s, zz, fb, fa, core):
        c = s.c
        astep = 2 + 2 * core
        bstep = 4 - 2 * core
        abit = c.x + (c.y - c.x) * core
        bbit = c.y + (c.x - c.y) * core
        return zz * 8 + core + bstep * (bbit + fb * (1 - 2 * bbit)) + astep * (abit + fa * (1 - 2 * abit))

    def source(s, p, fn):
        if len(s.parts) == 1:
            lo, hi, ref = s.parts[0]
            fn(ref.at[p - lo])
            return
        for lo, hi, ref in s.parts:

            @pl.when(jnp.logical_and(p >= lo, p < hi))
            def _():
                fn(ref.at[jnp.clip(p - lo, 0, hi - lo - 1)])

    def slot(s, zz, fb, fa, k):
        return (((zz - s.lo) * 2 + fb) * 2 + fa) * s.K + k

    def places(s, order=None):
        for kind, zz, fa, k in order or s.order:
            if kind != "f":
                yield zz, 1 if kind == "b" else 0, fa, k

    def zero(s):
        c = s.c

        def clear(n):
            s.Z[n] = jnp.zeros((128, D), BF)

        for n in range(3 * s.nz + 3):
            at_zero = n < 3 * s.nz
            at_three = n >= 3 * s.nz or s.lo + n // 3 < 3
            if at_zero:
                pl.when(c.z == 0)(functools.partial(clear, n))
            if at_three:
                pl.when(c.z == 3)(functools.partial(clear, n))

    def to_sibling(s, order=None):
        c = s.c
        for zz, fb, fa, k in s.places(order):
            n = s.slot(zz, fb, fa, k)

            def go(r, n=n):
                pltpu.make_async_remote_copy(
                    r, s.S.at[n], s.sent_s.at[n], s.got_s.at[n], device_id=(c.sib,), device_id_type=MESH
                ).start()

            s.source(s.owner(zz, fb, fa, 1 - c.core) * s.K + k, go)

    def load(s, i):
        if s.direct or i >= len(s.order):
            return
        kind, zz, fa, k = s.order[i]
        n = i % s.nst

        def go(r):
            pltpu.make_async_copy(r, s.stage.at[n], s.loaded.at[n]).start()

        s.source(s.owner(zz, 1 if kind == "b" else 0, fa, s.c.core) * s.K + k, go)

    def prefetch(s):
        for i in range(s.nst - 1):
            s.load(i)

    def flush(s):
        for f in s.later:
            f()
        s.later = []

    @staticmethod
    def wait(ref, sem):
        pltpu.make_async_copy(ref, ref, sem).wait()

    @staticmethod
    def sum(srcs, dst, scale=None):
        def rows(r, _):
            rr = pl.ds(pl.multiple_of(r * 16, 16), 16)
            t = srcs[0][rr, :].astype(F32)
            for q in srcs[1:]:
                t = t + q[rr, :].astype(F32)
            if scale is not None:
                t = t * scale
            dst[rr, :] = t.astype(dst.dtype)
            return 0

        lax.fori_loop(0, 8, rows, 0)

    def item(s, i):
        c, K = s.c, s.K
        kind, zz, fa, k = s.order[i]
        fb = 1 if kind == "b" else 0
        if s.direct:
            lo, hi, ref = s.parts[0]
            own = ref.at[s.owner(zz, fb, fa, c.core) * K + k - lo]
        else:
            own = s.stage.at[i % s.nst]
            s.wait(own, s.loaded.at[i % s.nst])
        s.flush()
        n = s.slot(zz, fb, fa, k)
        out = s.S.at[n]
        bi = ((zz - s.lo) * 2 + fa) * K + k
        zi = (zz - s.lo) * K + k
        z2 = s.nz * K + k

        def gather(kinds):
            srcs = [own]
            if "S" in kinds:
                srcs.append((out, s.got_s.at[n]))
            if "B" in kinds:
                srcs.append((s.B.at[bi], s.got_b.at[bi]))
            if "A" in kinds:
                srcs.append((s.A.at[zi], s.got_a.at[zi]))
            for pair in srcs[1:]:
                s.wait(*pair)
            return srcs[:1] + [ref for ref, _ in srcs[1:]]

        def send(dst, sem, to):
            return pltpu.make_async_remote_copy(
                out, dst, s.sent.at[n], sem, device_id=(to,), device_id_type=MESH
            )

        if kind == "b":
            s.sum(gather("S"), out)
            s.later.append(send(s.B.at[bi], s.got_b.at[bi], c.bp).start)
            s.waits.append((n, None))
        elif kind == "a":
            s.sum(gather("SB"), out)
            s.later.append(send(s.A.at[zi], s.got_a.at[zi], c.ap).start)
            s.waits.append((n, None))
        elif kind == "z":

            @pl.when(c.z != zz)
            def _():
                srcs = gather("SBA")
                comes = jnp.where(c.z <= zz, c.z, 3 - c.z)
                pl.when(comes > 0)(functools.partial(s.wait, s.Z.at[zi], s.got_z.at[zi]))
                s.sum(srcs + [s.Z.at[zi]], out)

            def on():
                @pl.when(c.z < zz)
                def _():
                    send(s.Z.at[zi], s.got_z.at[zi], c.up).start()

                to = jnp.where(c.z == zz + 1, z2, zi)

                @pl.when(c.z > zz)
                def _():
                    send(s.Z.at[to], s.got_z.at[to], c.dn).start()

            s.later.append(on)
            s.waits.append((n, zz))
        else:

            @pl.when(c.z == zz)
            def _():
                srcs = gather("SBA")
                pl.when(c.hasdn)(functools.partial(s.wait, s.Z.at[zi], s.got_z.at[zi]))
                pl.when(c.hasup)(functools.partial(s.wait, s.Z.at[z2], s.got_z.at[z2]))
                s.sum(srcs + [s.Z.at[zi], s.Z.at[z2]], s.out.at[k], s.scale)

        if s.auto:
            s.load(i + s.nst - 1)

    def finish(s):
        s.flush()
        for n, zz in s.waits:
            w = functools.partial(s.wait, s.S.at[0], s.sent.at[n])
            if zz is None:
                w()
            else:
                pl.when(s.c.z != zz)(w)

        for place in s.places():
            s.wait(s.S.at[0], s.sent_s.at[s.slot(*place)])


BACK_STEPS = (
    ("b301", "b211", "b310", "b212",),
    ("b312", "b300", "b210",),
    ("b311", "b110", "a211", "b100", "b201",),
    (),
    (),
    ("b302",),
    ("a311",),
    ("a310",),
    ("z301", "a312", "a210",),
    ("z300", "b200", "a110", "b202",),
    ("a212", "b111", "z302", "z201",),
    (),
    ("z200", "b112",),
    ("b101", "a111", "z100",),
    ("b102", "z202", "f302", "a112", "f301", "f300", "z101",),
    ("f101", "f201", "f100", "f202", "z102",),
    ("f102", "f200",),
)
TAIL_STEPS = (
    (),
    (),
    ("b000", "b010",),
    ("b011", "b001",),
    ("a010", "a011", "b012", "b002",),
    ("z000",),
    ("a012", "f000", "z001",),
    ("f001", "z002",),
    ("f002",),
)


def reduce_order(groups):
    order = [(t[0], int(t[1]), int(t[2]), int(t[3])) for g in groups for t in g]
    ends = [sum(len(g) for g in groups[: i + 1]) for i in range(len(groups))]
    return order, [list(range(e - len(g), e)) for e, g in zip(ends, groups)]


def qkv_kernel(x_ref, vec_ref, w_ref, out_ref, n_ref):
    j = pl.program_id(0)

    @pl.when(j == 0)
    def _():
        for i in range(2):

            def block(rows, dst):
                v = x_ref[i, rows, :].astype(F32)
                c = v - jnp.mean(v, axis=1, keepdims=True)
                rc = lax.rsqrt(jnp.mean(c * c, axis=1, keepdims=True) + EPS)
                return (c * rc * (1.0 + vec_ref[8:9, :]) + vec_ref[9:10, :]).astype(BF)

            def one(c, _):
                n_ref[i, rows_at(c), :] = block(rows_at(c), None)
                return 0

            lax.fori_loop(0, 18, one, 0)
            last = block(slice(576, 577), None).astype(F32)
            n_ref[i, 576:592, :] = jnp.concatenate([last, jnp.zeros((15, D), F32)], axis=0).astype(BF)

    w = w_ref[...].reshape(D, D)
    bias = jnp.where(j == 0, vec_ref[0:1, :], jnp.where(j == 2, vec_ref[1:2, :], 0.0))
    for i in range(2):
        out_ref[0, i] = (nn(n_ref[i], w) + bias).astype(BF)


def qkv(x, vec, w):
    return pl.pallas_call(
        qkv_kernel,
        grid=(3,),
        in_specs=[full((2, S, D)), full((16, D)), pl.BlockSpec((8, 1, 128, D), lambda j: (0, j, 0, 0))],
        out_specs=[pl.BlockSpec((1, 2, SQ, D), lambda j: (j, 0, 0, 0)), full((2, SQ, D))],
        out_shape=[jax.ShapeDtypeStruct((3, 2, SQ, D), BF), jax.ShapeDtypeStruct((2, SQ, D), BF)],
        compiler_params=pltpu.CompilerParams(vmem_limit_bytes=VMEM_ALL),
        name="qkv",
    )(x, vec, w.reshape(32, 3, 128, D))


def padded(v):
    return jnp.concatenate([v, jnp.zeros((640 - SQ, 128), v.dtype)], axis=0)


def attend_pair(q, k, v):
    lane = lax.broadcasted_iota(jnp.int32, (1, 128), 1)
    k = padded(k)
    v = padded(v)
    outs = []
    for h in range(2):
        mine = lane < 64 if h == 0 else lane >= 64
        s = nt(jnp.where(mine, q, jnp.zeros_like(q)), k)
        s = jnp.concatenate([s[:, :512], jnp.where(lane < S - 512, s[:, 512:], -1e30)], axis=1)
        top = jnp.max(s, axis=1, keepdims=True)
        p = jnp.exp2((s - top) * SCORE)
        total = jnp.sum(p, axis=1, keepdims=True)
        outs.append(nn(p.astype(BF), v) * (1.0 / total))
    return jnp.where(lane < 64, outs[0], outs[1]).astype(BF)


def attend_kernel(q_ref, k_ref, v_ref, o_ref):
    half = SQ // 2
    for r in range(2):
        rows = slice(r * half, (r + 1) * half)
        o_ref[0, rows, :] = attend_pair(q_ref[0, 0, rows, :], k_ref[0, 0], v_ref[0, 0])


def attend(z):
    spec = lambda j: pl.BlockSpec((1, 1, SQ, 128), lambda i, h: (j, i, 0, h))
    return pl.pallas_call(
        attend_kernel,
        grid=(2, 8),
        in_specs=[spec(0), spec(1), spec(2)],
        out_specs=pl.BlockSpec((1, SQ, 128), lambda i, h: (i, 0, h)),
        out_shape=jax.ShapeDtypeStruct((2, SQ, D), BF),
        compiler_params=pltpu.CompilerParams(vmem_limit_bytes=VMEM_ALL),
        name="attend",
    )(z, z, z)


def norm_block(v, vec_ref):
    v = v.astype(F32)
    ce = v - jnp.mean(v, axis=1, keepdims=True)
    rc = lax.rsqrt(jnp.mean(ce * ce, axis=1, keepdims=True) + EPS)
    return (ce * rc * (1.0 + vec_ref[8:9, :]) + vec_ref[9:10, :]).astype(BF)


def norm_one(x_ref, vec_ref, n_ref):
    for i in range(2):

        def one(c, _):
            n_ref[i, rows_at(c), :] = norm_block(x_ref[i, rows_at(c), :], vec_ref)
            return 0

        lax.fori_loop(0, 18, one, 0)
        last = norm_block(x_ref[i, 576:577, :], vec_ref).astype(F32)
        n_ref[i, 576:592, :] = jnp.concatenate([last, jnp.zeros((15, D), F32)], axis=0).astype(BF)


FRONT_STEPS = (
    ("oa31", "oa30", "ou00", "oa01", "od11", "ob20", "os21", "os00", "os31", "ob31", "ob30", "ou31", "ob00", "oa32", "ou01", "ob10", "oa20", "ob21", "od32", "oa10", "z00",),
    ("od10", "os01", "ob01", "od31", "b00", "ou32", "oa00", "z01", "ou02", "ob02", "od20", "od12", "a00", "os12", "z02", "os30", "a01", "os02", "oa02", "ob32", "b02", "od30", "a02", "od21", "os32", "oa21", "os20", "os11", "oa11", "ou20", "ob22", "oa22", "ob12", "z10", "c00", "z11", "ou10", "c01", "os10", "od22", "ob11", "b01", "ou11",),
    ("z12", "z20", "os22", "z21", "ou21", "ou12", "oa12", "c02",),
    ("a11",),
    ("a10", "z22", "b10", "ou22",),
    ("b11", "a21", "a20",),
    ("ou30", "a12",),
    (),
    ("a22", "z31",),
    (),
    (),
    (),
    ("z30", "c10", "z32", "b20",),
    (),
    ("b31", "a30",),
    (),
    ("c20", "b30",),
    ("a31", "c21", "c12", "b22", "c11", "a32",),
    ("b21", "c30", "b32", "c22",),
    ("b12", "c31",),
    ("c32",),
)


def front_kernel(
    own, vec_own, x_ref, w, vec, z_out, n_out, mix_out, z_ref, n_ref, mix_ref, osem, vlow, wq, qsem, vsem, ssem, rsem, lsem
):
    c = Ctx()
    g = Gather(c, own, w, ssem, rsem, lsem)
    vector = Vector(c, vec_own, vlow, vsem)
    vector.tell()
    c.barrier(jnp.where(c.me == 31, 31, 0))
    vector.start()
    g.keep()

    def take(n):
        for text in FRONT_STEPS[n]:
            g.step(text)

    take(0)
    vector.wait()
    vec[...] = vlow[...].astype(F32)
    norm_one(x_ref, vec, n_ref)
    leave = [pltpu.make_async_copy(n_ref, n_out, osem.at[0])]
    leave[0].start()
    for j in range(3):
        take(1 + j)
        g.kept(j)
        g.sibling(0, 4, (j,))
        load = pltpu.make_async_copy(w.at[0:8, j], wq.at[j % 2], qsem.at[j])
        load.start()
        load.wait()
        for i in range(2):
            r = nn(n_ref[i], wq[j % 2].reshape(D, D))
            if j != 1:
                r = r + vec[j // 2 : j // 2 + 1, :]
            z_ref[j, i] = r.astype(BF)
    leave.append(pltpu.make_async_copy(z_ref, z_out, osem.at[1]))
    leave[1].start()

    def pair(t, _):
        for n in range(16):
            if FRONT_STEPS[4 + n]:

                @pl.when(t == n)
                def _():
                    take(4 + n)

        i = t // 8
        cols = pl.ds(pl.multiple_of((t % 8) * 128, 128), 128)
        half = SQ // 2
        k = z_ref[1, i, :, cols]
        v = z_ref[2, i, :, cols]
        for r in range(2):
            rows = slice(r * half, (r + 1) * half)
            mix_ref[i, rows, cols] = attend_pair(z_ref[0, i, rows, cols], k, v)
        return 0

    lax.fori_loop(0, 16, pair, 0)
    leave.append(pltpu.make_async_copy(mix_ref, mix_out, osem.at[2]))
    leave[2].start()
    take(20)
    g.sibling(4, 16, (0, 1, 2))
    g.sent()
    vector.sent()
    for cp in leave:
        cp.wait()


def front(own, vec_own, x):
    vm = pl.BlockSpec(memory_space=pltpu.VMEM)
    far = pl.BlockSpec(memory_space=pl.ANY)
    dma = lambda n: pltpu.SemaphoreType.DMA((n,))
    return pl.pallas_call(
        front_kernel,
        in_specs=[vm, vm, vm],
        out_specs=[far, vm, far, far, far],
        out_shape=[
            jax.ShapeDtypeStruct((32, 3, 128, D), BF),
            jax.ShapeDtypeStruct((16, D), F32),
            jax.ShapeDtypeStruct((3, 2, SQ, D), BF),
            jax.ShapeDtypeStruct((2, SQ, D), BF),
            jax.ShapeDtypeStruct((2, SQ, D), BF),
        ],
        scratch_shapes=[pltpu.VMEM((3, 2, SQ, D), BF), pltpu.VMEM((2, SQ, D), BF), pltpu.VMEM((2, SQ, D), BF), dma(3)]
        + [pltpu.VMEM((16, D), BF), pltpu.VMEM((2, 8, 128, D), BF), dma(3), dma(32)]
        + [dma(240), dma(96), dma(3)],
        compiler_params=pltpu.CompilerParams(collective_id=1, has_side_effects=True, vmem_limit_bytes=VMEM_ALL),
        name="front",
    )(own, vec_own, x)


def attend_back_pair(q, k, v, do):
    lane = lax.broadcasted_iota(jnp.int32, (1, 128), 1)
    real = lax.broadcasted_iota(jnp.int32, (16, 1), 0) < S - 576
    q = padded(q)
    do = padded(do)
    dqs, dks, dvs = [], [], []
    for h in range(2):
        mine = lane < 64 if h == 0 else lane >= 64
        s = nt(jnp.where(mine, k, jnp.zeros_like(k)), q)
        s = jnp.concatenate([s[:576], jnp.where(real, s[576:], -1e30)], axis=0)
        top = jnp.max(s, axis=0, keepdims=True)
        p = jnp.exp2((s - top) * SCORE)
        p = p * (1.0 / jnp.sum(p, axis=0, keepdims=True))
        dvs.append(nn(p.astype(BF), do))
        dp = nt(jnp.where(mine, v, jnp.zeros_like(v)), do)
        ds = (p * (dp - jnp.sum(p * dp, axis=0, keepdims=True))).astype(BF)
        dks.append(nn(ds, q))
        dqs.append(tn(ds, k))
    pick = lambda pair, scale: (jnp.where(lane < 64, pair[0], pair[1]) * scale).astype(BF)
    return pick(dqs, 0.125)[:SQ], pick(dks, 0.125), pick(dvs, 1.0)


def attend_back_kernel(q_ref, k_ref, v_ref, do_ref, out_ref):
    dq, dk, dv = attend_back_pair(q_ref[0, 0], k_ref[0, 0], v_ref[0, 0], do_ref[0])
    out_ref[0, 0] = dq
    out_ref[1, 0] = dk
    out_ref[2, 0] = dv


def attend_back(z, do):
    spec = lambda j: pl.BlockSpec((1, 1, SQ, 128), lambda i, h: (j, i, 0, h))
    return pl.pallas_call(
        attend_back_kernel,
        grid=(2, 8),
        in_specs=[spec(0), spec(1), spec(2), pl.BlockSpec((1, SQ, 128), lambda i, h: (i, 0, h))],
        out_specs=pl.BlockSpec((3, 1, SQ, 128), lambda i, h: (0, i, 0, h)),
        out_shape=jax.ShapeDtypeStruct((3, 2, SQ, D), BF),
        compiler_params=pltpu.CompilerParams(vmem_limit_bytes=VMEM_ALL),
        name="attend_back",
    )(z, z, z, do)


def mlp_kernel(x_ref,g_ref,mix_ref,vec_ref,wo_ref,wu_ref,wd_ref,
               out_ref,gup_ref,gdn_ref,gout_ref,dmix_ref,dhid_ref,gvec_ref,
               n2,gs,acc,dn,stat,*,FB,NB):
    jb=pl.program_id(0)
    hid=dhid_ref
    @pl.when(jb==0)
    def _():
        wo=wo_ref[...].reshape(D,D)
        for i in range(2):
            hid[i*SQ:(i+1)*SQ,:]=nn(mix_ref[i],wo)
            gs[i*SQ:i*SQ+576,:]=g_ref[i,:576,:]
            gs[i*SQ+576:(i+1)*SQ,:]=jnp.concatenate([g_ref[i,576:577,:].astype(F32),jnp.zeros((15,D),F32)],axis=0).astype(BF)
            def addx(c,_):
                r=pl.multiple_of(c*CH,CH)
                hid[pl.ds(i*SQ+r,CH),:]+=x_ref[i,pl.ds(r,CH),:].astype(F32)+vec_ref[2:3,:]
                return 0
            lax.fori_loop(0,18,addx,0)
            hid[i*SQ+576:i*SQ+577,:]+=x_ref[i,576:577,:].astype(F32)+vec_ref[2:3,:]
        acc[...]=jnp.zeros_like(acc); dn[...]=jnp.zeros_like(dn)
        gvec_ref[...]=jnp.zeros_like(gvec_ref)
        def ln(c,_):
            r=pl.ds(pl.multiple_of(c*CH,CH),CH)
            h=hid[r,:]
            mu=jnp.mean(h,axis=1,keepdims=True)
            ce=h-mu
            rc=lax.rsqrt(jnp.mean(ce*ce,axis=1,keepdims=True)+EPS)
            n2[r,:]=(ce*rc*(1.0+vec_ref[10:11,:])+vec_ref[11:12,:]).astype(BF)
            stat[r,0:1]=mu; stat[r,1:2]=rc
            return 0
        lax.fori_loop(0,M//CH,ln,0)
        def gsum(c,a):
            r=pl.ds(pl.multiple_of(c*CH,CH),CH)
            return a+gs[r,:].astype(F32)
        t=lax.fori_loop(0,M//CH,gsum,jnp.zeros((CH,D),F32))
        gvec_ref[7:8,:]=jnp.sum(t,axis=0,keepdims=True)
    wu=wu_ref[...].reshape(D,FB); wd=wd_ref[...].reshape(FB,D)
    nper=D//FB
    row=vec_ref[pl.ds(3+jb//nper,1),:]
    bup=row[:,:FB]
    for t in range(1,nper): bup=jnp.where(jb%nper==t,row[:,t*FB:(t+1)*FB],bup)
    g=gs[...]; n=n2[...]
    acts=[];dps=[]
    pres=[nn(n[i*SQ:(i+1)*SQ],wu)+bup for i in range(2)]
    das=[nt(g[i*SQ:(i+1)*SQ],wd) for i in range(2)]
    for i in range(2):
        pre=pres[i]
        cdf=0.5*(1.0+lax.erf(pre*0.7071067811865476))
        act=(pre*cdf).astype(BF)
        slope=cdf+pre*0.3989422804014327*jnp.exp(-0.5*pre*pre)
        dp=(das[i]*slope).astype(BF)
        acc[i*SQ:(i+1)*SQ,:]+=nn(act,wd)
        dn[i*SQ:(i+1)*SQ,:]+=nt(dp,wu)
        acts.append(act);dps.append(dp)
    act=jnp.concatenate(acts,axis=0);dp=jnp.concatenate(dps,axis=0)
    gup_ref[...]=tn(n,dp).astype(BF).reshape(gup_ref.shape)
    gdn_ref[...]=tn(act,g).astype(BF).reshape(gdn_ref.shape)
    bsum=jnp.sum(dp.astype(F32),axis=0,keepdims=True)
    for t in range(nper):
        @pl.when(jb%nper==t)
        def _(): gvec_ref[pl.ds(3+jb//nper,1),t*FB:(t+1)*FB]=bsum
    @pl.when(jb==NB-1)
    def _():
        for i in range(2):
            def ob(c,_):
                r=pl.multiple_of(c*CH,CH)
                out_ref[i,pl.ds(r,CH),:]=(hid[pl.ds(i*SQ+r,CH),:]+(acc[pl.ds(i*SQ+r,CH),:]+vec_ref[7:8,:])).astype(BF)
                return 0
            lax.fori_loop(0,18,ob,0)
            out_ref[i,576:577,:]=(hid[i*SQ+576:i*SQ+577,:]+(acc[i*SQ+576:i*SQ+577,:]+vec_ref[7:8,:])).astype(BF)
        def bk(c,car):
            a,b,d=car
            r=pl.ds(pl.multiple_of(c*CH,CH),CH)
            mu=stat[r,0:1]; rc=stat[r,1:2]
            xh=(hid[r,:]-mu)*rc
            dd=dn[r,:]
            e=dd*(1.0+vec_ref[10:11,:])
            dh=gs[r,:].astype(F32)+rc*(e-jnp.mean(e,axis=1,keepdims=True)-xh*jnp.mean(e*xh,axis=1,keepdims=True))
            dhid_ref[r,:]=dh
            db=dh.astype(BF)
            n2[r,:]=db
            return (a+dd*xh,b+dd,d+db.astype(F32))
        zz=jnp.zeros((CH,D),F32)
        a,b,d=lax.fori_loop(0,M//CH,bk,(zz,zz,zz))
        gvec_ref[10:11,:]=jnp.sum(a,axis=0,keepdims=True)
        gvec_ref[11:12,:]=jnp.sum(b,axis=0,keepdims=True)
        gvec_ref[2:3,:]=jnp.sum(d,axis=0,keepdims=True)
        db=n2[...]
        wo=wo_ref[...].reshape(D,D)
        dmix_ref[...]=nt(db,wo).astype(BF).reshape(2,SQ,D)
        gout_ref[...]=tn(mix_ref[...].reshape(M,D),db).astype(BF).reshape(8,128,D)
def mlp(x,g,mix,vec,W,FB=512):
    NB=4096//FB; nper=D//FB
    W4=W.reshape(96,4,32,1024)
    return pl.pallas_call(functools.partial(mlp_kernel,FB=FB,NB=NB),grid=(NB,),
      in_specs=[full((2,S,D)),full((2,S,D)),full((2,SQ,D)),full((16,D)),
        pl.BlockSpec((8,128,D),lambda j:(3,0,0),pipeline_mode=pl.Buffered(1)),
        pl.BlockSpec((32,1,32,FB),lambda j:(1,j//nper,0,j%nper)),
        pl.BlockSpec((FB//128,128,D),lambda j:(64//(FB//128)+j,0,0))],
      out_specs=[full((2,S,D)),pl.BlockSpec((32,1,32,FB),lambda j:(0,j//nper,0,j%nper)),
        pl.BlockSpec((FB//128,128,D),lambda j:(j,0,0)),full((8,128,D)),full((2,SQ,D)),full((M,D)),full((16,D))],
      out_shape=[jax.ShapeDtypeStruct((2,S,D),BF),jax.ShapeDtypeStruct((32,4,32,D),BF),jax.ShapeDtypeStruct((32,128,D),BF),
        jax.ShapeDtypeStruct((8,128,D),BF),jax.ShapeDtypeStruct((2,SQ,D),BF),jax.ShapeDtypeStruct((M,D),F32),jax.ShapeDtypeStruct((16,D),F32)],
      scratch_shapes=[pltpu.VMEM((M,D),BF),pltpu.VMEM((M,D),BF),pltpu.VMEM((M,D),F32),pltpu.VMEM((M,D),F32),pltpu.VMEM((M,128),F32)],
      compiler_params=pltpu.CompilerParams(vmem_limit_bytes=67043328),name=f"mlp{FB}")(x,g,mix,vec,W,W4,W)


def tail_kernel(x_ref, dz_ref, n_ref, dhid_ref, vec_ref, w_ref, gvin_ref, gx_ref, gw_ref, gvec_ref, acc):
    j = pl.program_id(0)

    @pl.when(j == 0)
    def _():
        gvec_ref[...] = gvin_ref[...]
        acc[...] = jnp.zeros_like(acc)

    w = w_ref[...].reshape(D, D)
    dz = dz_ref[0].reshape(M, D)
    acc[...] += nt(dz, w)
    gw_ref[...] = tn(n_ref[...].reshape(M, D), dz).astype(BF).reshape(8, 1, 128, D)

    @pl.when(j != 1)
    def _():
        def add(c, t):
            return t + dz_ref[0, 0, pl.ds(c * 16, 16), :].astype(F32) + dz_ref[0, 1, pl.ds(c * 16, 16), :].astype(F32)

        t = lax.fori_loop(0, SQ // 16, add, jnp.zeros((16, D), F32))
        gvec_ref[pl.ds(j // 2, 1), :] = jnp.sum(t, axis=0, keepdims=True)

    @pl.when(j == 2)
    def _():
        def back(x, dd, dh):
            v = x.astype(F32)
            ce = v - jnp.mean(v, axis=1, keepdims=True)
            rc = lax.rsqrt(jnp.mean(ce * ce, axis=1, keepdims=True) + EPS)
            xh = ce * rc
            e = dd * (1.0 + vec_ref[8:9, :])
            g = dh + rc * (e - jnp.mean(e, axis=1, keepdims=True) - xh * jnp.mean(e * xh, axis=1, keepdims=True))
            return g.astype(BF), dd * xh, dd

        a = b = jnp.zeros((CH, D), F32)
        la = lb = jnp.zeros((1, D), F32)
        for i in range(2):

            def one(c, carry):
                r = rows_at(c)
                r2 = pl.ds(pl.multiple_of(i * SQ + c * CH, 16), CH)
                g, s1, s2 = back(x_ref[i, r, :], acc[r2, :], dhid_ref[r2, :])
                gx_ref[i, r, :] = g
                return carry[0] + s1, carry[1] + s2

            a, b = lax.fori_loop(0, 18, one, (a, b))
            r2 = slice(i * SQ + 576, i * SQ + 577)
            g, s1, s2 = back(x_ref[i, 576:577, :], acc[r2, :], dhid_ref[r2, :])
            gx_ref[i, 576:577, :] = g
            la, lb = la + s1, lb + s2
        gvec_ref[8:9, :] = jnp.sum(a, axis=0, keepdims=True) + la
        gvec_ref[9:10, :] = jnp.sum(b, axis=0, keepdims=True) + lb


def tail(x, dz, n1, dhid, vec, w, gvec):
    return pl.pallas_call(
        tail_kernel,
        grid=(3,),
        in_specs=[
            full((2, S, D)),
            pl.BlockSpec((1, 2, SQ, D), lambda j: (j, 0, 0, 0)),
            full((2, SQ, D)),
            full((M, D)),
            full((16, D)),
            pl.BlockSpec((8, 1, 128, D), lambda j: (0, j, 0, 0)),
            full((16, D)),
        ],
        out_specs=[full((2, S, D)), pl.BlockSpec((8, 1, 128, D), lambda j: (0, j, 0, 0)), full((16, D))],
        out_shape=[
            jax.ShapeDtypeStruct((2, S, D), BF),
            jax.ShapeDtypeStruct((8, 3, 128, D), BF),
            jax.ShapeDtypeStruct((16, D), F32),
        ],
        scratch_shapes=[pltpu.VMEM((M, D), F32)],
        compiler_params=pltpu.CompilerParams(vmem_limit_bytes=VMEM_ALL),
        name="tail",
    )(x, dz, n1, dhid, vec, w.reshape(32, 3, 128, D), gvec)

def back_kernel(z_in, do_in, *refs, lo, hi, ranges, scale):
    n = len(ranges)
    parts = [(a, b, r) for (a, b), r in zip(ranges, refs[:n])]
    dz_out, chunk, z_ref, do_ref, dz_ref, iosem = refs[n : n + 6]
    c = Ctx()
    loads = [pltpu.make_async_copy(z_in.at[j], z_ref.at[j], iosem.at[j]) for j in range(3)]
    loads.append(pltpu.make_async_copy(do_in, do_ref, iosem.at[3]))
    for cp in loads:
        cp.start()
    order, groups = reduce_order(BACK_STEPS)
    red = Reduce(c, lo, hi, parts, chunk, refs[n + 6 :], scale, order)
    red.zero()
    chunk[...] = jnp.zeros_like(chunk)
    c.barrier()
    red.to_sibling()
    red.prefetch()
    for cp in loads:
        cp.wait()

    def pair(t, _):
        for m in range(16):
            if groups[m]:

                @pl.when(t == m)
                def _():
                    for i in groups[m]:
                        red.steps[i]()
                    red.flush()

        i = t // 8
        cols = pl.ds(pl.multiple_of((t % 8) * 128, 128), 128)
        dq, dk, dv = attend_back_pair(z_ref[0, i, :, cols], z_ref[1, i, :, cols], z_ref[2, i, :, cols], do_ref[i, :, cols])
        dz_ref[0, i, :, cols] = dq
        dz_ref[1, i, :, cols] = dk
        dz_ref[2, i, :, cols] = dv
        return 0

    lax.fori_loop(0, 16, pair, 0)
    leave = pltpu.make_async_copy(dz_ref, dz_out, iosem.at[4])
    leave.start()
    for i in groups[16]:
        red.steps[i]()
    red.finish()
    leave.wait()


def back(z, do, parts, lo, hi, ranges, scale):
    vm = pl.BlockSpec(memory_space=pltpu.VMEM)
    return pl.pallas_call(
        functools.partial(back_kernel, lo=lo, hi=hi, ranges=ranges, scale=scale),
        in_specs=[pl.BlockSpec(memory_space=pl.ANY)] * (2 + len(parts)),
        out_specs=[pl.BlockSpec(memory_space=pl.ANY), vm],
        out_shape=[jax.ShapeDtypeStruct((3, 2, SQ, D), BF), jax.ShapeDtypeStruct((3, 128, D), F32)],
        scratch_shapes=[
            pltpu.VMEM((3, 2, SQ, D), BF),
            pltpu.VMEM((2, SQ, D), BF),
            pltpu.VMEM((3, 2, SQ, D), BF),
            pltpu.SemaphoreType.DMA((5,)),
        ]
        + Reduce.scratch(lo, hi, 4),
        compiler_params=pltpu.CompilerParams(collective_id=2, has_side_effects=True, vmem_limit_bytes=VMEM_ALL),
        name="back",
    )(z, do, *parts)


def back_norm(x, dd, dh, vec_ref):
    v = x.astype(F32)
    ce = v - jnp.mean(v, axis=1, keepdims=True)
    rc = lax.rsqrt(jnp.mean(ce * ce, axis=1, keepdims=True) + EPS)
    xh = ce * rc
    e = dd * (1.0 + vec_ref[8:9, :])
    g = dh + rc * (e - jnp.mean(e, axis=1, keepdims=True) - xh * jnp.mean(e * xh, axis=1, keepdims=True))
    return g.astype(BF), dd * xh


def tail_quick_kernel(
    x_in, dz_ref, n_ref, dhid_in, vec_ref, gvin_ref, w, gx_ref, chunk, gvec_ref,
    x_ref, dhid_ref, xsem, acc, gw, wq, qsem, *scr, scale
):
    c = Ctx()
    order, groups = reduce_order(TAIL_STEPS)
    red = Reduce(c, 0, 0, [(0, 24, gw)], chunk, scr, scale, order, direct=True)
    loads = [pltpu.make_async_copy(w.at[0:8, j], wq.at[j % 2], qsem.at[j]) for j in range(3)]
    loads[0].start()
    loads[1].start()
    late = [pltpu.make_async_copy(x_in, x_ref, xsem.at[0]), pltpu.make_async_copy(dhid_in, dhid_ref, xsem.at[1])]
    for cp in late:
        cp.start()
    red.zero()
    chunk[...] = jnp.zeros_like(chunk)
    gvec_ref[...] = gvin_ref[...]
    c.barrier()

    def take(n):
        for i in groups[n]:
            red.steps[i]()
        red.flush()

    def weights(j):
        g = tn(n_ref[...].reshape(M, D), dz_ref[j].reshape(M, D)).astype(BF)
        for d in range(8):
            gw[3 * d + j] = g[128 * d : 128 * (d + 1)]

    def colsum(j):
        def add(r, t):
            rr = pl.ds(pl.multiple_of(r * 16, 16), 16)
            return t + dz_ref[j, 0, rr, :].astype(F32) + dz_ref[j, 1, rr, :].astype(F32)

        t = lax.fori_loop(0, SQ // 16, add, jnp.zeros((16, D), F32))
        gvec_ref[j // 2 : j // 2 + 1, :] = jnp.sum(t, axis=0, keepdims=True)

    def inputs(j):
        loads[j].wait()
        wj = wq[j % 2].reshape(D, D)
        for i in range(2):
            r = nt(dz_ref[j, i], wj)
            rows = slice(i * SQ, (i + 1) * SQ)
            acc[rows, :] = r if j == 0 else acc[rows, :] + r

    some = lambda k: [o for o in order if o[3] == k]
    weights(0)
    colsum(0)
    red.to_sibling(some(0))
    weights(1)
    red.to_sibling(some(1))
    take(2)
    weights(2)
    colsum(2)
    red.to_sibling(some(2))
    take(3)
    for j in range(3):
        inputs(j)
        if j == 0:
            loads[2].start()
        take(4 + j)
    for cp in late:
        cp.wait()
    a = b = jnp.zeros((CH, D), F32)
    la = lb = jnp.zeros((1, D), F32)
    for i in range(2):

        def one(t, carry):
            r = rows_at(t)
            r2 = pl.ds(pl.multiple_of(i * SQ + t * CH, 16), CH)
            dd = acc[r2, :]
            g, s1 = back_norm(x_ref[i, r, :], dd, dhid_ref[r2, :], vec_ref)
            gx_ref[i, r, :] = g
            return carry[0] + s1, carry[1] + dd

        a, b = lax.fori_loop(0, 18, one, (a, b))
        r2 = slice(i * SQ + 576, i * SQ + 577)
        dd = acc[r2, :]
        g, s1 = back_norm(x_ref[i, 576:577, :], dd, dhid_ref[r2, :], vec_ref)
        gx_ref[i, 576:577, :] = g
        la, lb = la + s1, lb + dd
        take(7 + i)
    gvec_ref[8:9, :] = jnp.sum(a, axis=0, keepdims=True) + la
    gvec_ref[9:10, :] = jnp.sum(b, axis=0, keepdims=True) + lb
    red.finish()


def tail_quick(x, dz, n1, dhid, vec, gvec, w, scale):
    vm = pl.BlockSpec(memory_space=pltpu.VMEM)
    far = pl.BlockSpec(memory_space=pl.ANY)
    return pl.pallas_call(
        functools.partial(tail_quick_kernel, scale=scale),
        in_specs=[far, vm, vm, far, vm, vm, far],
        out_specs=[vm] * 3,
        out_shape=[
            jax.ShapeDtypeStruct((2, S, D), BF),
            jax.ShapeDtypeStruct((3, 128, D), F32),
            jax.ShapeDtypeStruct((16, D), F32),
        ],
        scratch_shapes=[
            pltpu.VMEM((2, S, D), BF),
            pltpu.VMEM((M, D), F32),
            pltpu.SemaphoreType.DMA((2,)),
            pltpu.VMEM((M, D), F32),
            pltpu.VMEM((24, 128, D), BF),
            pltpu.VMEM((2, 8, 128, D), BF),
            pltpu.SemaphoreType.DMA((3,)),
        ]
        + Reduce.scratch(0, 0, 1),
        compiler_params=pltpu.CompilerParams(collective_id=3, has_side_effects=True, vmem_limit_bytes=VMEM_ALL),
        name="tail_quick",
    )(x, dz, n1, dhid, vec, gvec, w)


def close_kernel(chunk_a, chunk_b, gvec, wg, clip_ref, flat, e, es, ea, eb, ez, sem, *, scale):
    c = Ctx()
    me = c.me
    bar = pltpu.get_barrier_semaphore()
    others = [c.sib, c.ap, c.bp] + [lax.rem(me + 8 * i, 32) for i in (1, 2, 3)]
    for to in others:
        pl.semaphore_signal(bar, inc=1, device_id=(to,), device_id_type=MESH)
    first, last = me == 0, me == 31

    @pl.when(jnp.logical_not(first))
    def _():
        pl.semaphore_signal(bar, inc=1, device_id=(me - 1,), device_id_type=MESH)

    @pl.when(jnp.logical_not(last))
    def _():
        pl.semaphore_signal(bar, inc=1, device_id=(me + 1,), device_id_type=MESH)

    def unfold(src, k, kind):
        for t in range(8):
            cols = slice(128 * t, 128 * (t + 1))
            if kind == 0:
                flat[pl.ds(8 * k + t, 128, stride=24), :] = src[k, :, cols]
            elif kind == 1:
                flat[pl.ds(1024 * k + t, 128, stride=8), :] = src[k, :, cols]
            else:
                for j in range(4):
                    flat[pl.ds(1024 * k + 8 * j + t, 32, stride=32), :] = src[k, 32 * j : 32 * j + 32, cols]

    for k in range(3):
        p = 3 * me + k
        up = jnp.logical_and(p >= 32, p < 64)
        pl.when(c.z == 0)(functools.partial(unfold, chunk_b, k, 0))
        pl.when(up)(functools.partial(unfold, chunk_a, k, 2))
        pl.when(jnp.logical_and(c.z > 0, jnp.logical_not(up)))(functools.partial(unfold, chunk_a, k, 1))

    def square(i, t):
        v = flat[pl.ds(pl.multiple_of(i * 64, 64), 64), :]
        return t + v * v

    sq = jnp.sum(lax.fori_loop(0, 48, square, jnp.zeros((64, 128), F32)))
    e[0:12, :] = gvec[0:12, :]
    e[12:16, :] = jnp.full((4, D), sq, F32)
    pl.semaphore_wait(bar, 6 + jnp.where(first, 0, 1) + jnp.where(last, 0, 1))
    head = flat.at[0:96]
    room = flat.at[3072:3168]
    edge = pltpu.make_async_remote_copy(
        head, room, sem.at[14], sem.at[15], device_id=(jnp.maximum(me - 1, 0),), device_id_type=MESH
    )
    pl.when(jnp.logical_not(first))(edge.start)
    for n, (to, dst) in enumerate(((c.sib, es), (c.ap, ea), (c.bp, eb))):
        cp = pltpu.make_async_remote_copy(e, dst, sem.at[n], sem.at[3 + n], device_id=(to,), device_id_type=MESH)
        cp.start()
        cp.wait()
        e[...] = e[...] + dst[...]
    ez[c.z] = e[...]
    cps = []
    for i in (1, 2, 3):
        to = lax.rem(me + 8 * i, 32)
        cp = pltpu.make_async_remote_copy(
            e, ez.at[c.z], sem.at[6 + i], sem.at[9 + i], device_id=(to,), device_id_type=MESH
        )
        cp.start()
        cps.append(cp)
    for i in (1, 2, 3):
        cps[i - 1].wait_send()
        zz = lax.rem(c.z + 4 - i, 4)
        pltpu.make_async_copy(ez.at[zz], ez.at[zz], sem.at[9 + i]).wait()
    total = ((ez[0] + ez[1]) + ez[2]) + ez[3]
    vec = total[0:12, :]
    square_sum = (total[12:13, 0:128] + jnp.sum(vec * vec)) * (scale * scale)
    clip_ref[...] = jnp.broadcast_to(jnp.minimum(1.0, max_norm / (jnp.sqrt(square_sum) + 1e-06)), (8, 128))

    @pl.when(last)
    def _():
        for t in range(8):
            flat[pl.ds(3072 + t, 12, stride=8), :] = vec[:, 128 * t : 128 * (t + 1)]

    @pl.when(jnp.logical_not(last))
    def _():
        pltpu.make_async_copy(room, room, sem.at[15]).wait()

    pl.when(jnp.logical_not(first))(edge.wait_send)

    def block(i, _):
        wg[pl.ds(pl.multiple_of(i * 64, 64), 64), :] = flat[pl.ds(i * 64 + 3 * me, 64), :]
        return 0

    lax.fori_loop(0, 48, block, 0)
    wg[3072:3075, :] = flat[pl.ds(3072 + 3 * me, 3), :]


def close(chunk_a, chunk_b, gvec, scale):
    vm = pl.BlockSpec(memory_space=pltpu.VMEM)
    small = pltpu.VMEM((16, D), F32)
    return pl.pallas_call(
        functools.partial(close_kernel, scale=scale),
        in_specs=[vm] * 3,
        out_specs=[vm] * 2,
        out_shape=[jax.ShapeDtypeStruct((3075, 128), F32), jax.ShapeDtypeStruct((8, 128), F32)],
        scratch_shapes=[pltpu.VMEM((3168, 128), F32)]
        + [small] * 4
        + [pltpu.VMEM((4, 16, D), F32), pltpu.SemaphoreType.DMA((16,))],
        compiler_params=pltpu.CompilerParams(collective_id=4, has_side_effects=True, vmem_limit_bytes=VMEM_ALL),
        name="close",
    )(chunk_a, chunk_b, gvec)


def to_pieces(rows, first):
    n = rows.shape[0] // 128
    plain = rows.reshape(n, 128, D)
    three = rows.reshape(n // 3, 128, 3, D).transpose(0, 2, 1, 3).reshape(n, 128, D)
    four = rows.reshape(n, 32, 4, D).transpose(0, 2, 1, 3).reshape(n, 128, D)
    p = first + lax.broadcasted_iota(jnp.int32, (n, 1, 1), 0)
    return jnp.where(p < 24, three, jnp.where((p >= 32) & (p < 64), four, plain))


def from_pieces(pieces, first):
    n = pieces.shape[0]
    plain = pieces.reshape(n * 128, D)
    three = pieces.reshape(n // 3, 3, 128, D).transpose(0, 2, 1, 3).reshape(n * 128, D)
    four = pieces.reshape(n, 4, 32, D).transpose(0, 2, 1, 3).reshape(n * 128, D)
    p = first + lax.broadcasted_iota(jnp.int32, (n * 128, 1), 0) // 128
    return jnp.where(p < 24, three, jnp.where((p >= 32) & (p < 64), four, plain))


def update(params, moment_one, moment_two, weight_grad, clip_factor):
    clipped = clip_factor * weight_grad
    moment_one_new = beta_one * moment_one + (1.0 - beta_one) * clipped
    moment_two_new = beta_two * moment_two + (1.0 - beta_two) * clipped * clipped
    correct_one = 1.0 - beta_one**STEP
    correct_two = 1.0 - beta_two**STEP
    params_new = params - learn_rate * (
        moment_one_new / correct_one / (jnp.sqrt(moment_two_new / correct_two) + adam_eps) + decay_rate * params
    )
    return params_new, moment_one_new, moment_two_new


def shards(tokens, cotangent, params, moment_one, moment_two):
    n = lax.axis_size("dp")
    me = lax.axis_index("dp")
    shard_len = params.shape[0]
    images_all = tokens.shape[0] * n
    mats = PIECES * 128 * D
    scale = 1.0 / images_all
    if n == 32:
        unit = 128
        extra = 12 * D // unit
        own_units = shard_len // unit
        gap = extra // n
        low = params.reshape(own_units, unit)
        before = lax.ppermute(low[own_units - extra :].astype(BF), "dp", [(i, (i + 1) % n) for i in range(n)])
        joined = jnp.concatenate([before.astype(F32), low], axis=0)
        aligned = lax.dynamic_slice(joined, (extra - gap * me, 0), (own_units - gap, unit))
        own = to_pieces(aligned.reshape(-1, D), 3 * me).astype(BF)
        vec_own = jnp.pad(low[own_units - extra :].reshape(12, D), ((0, 4), (0, 0))).astype(BF)
        w, vec, z, n1, mixed = front(own, vec_own, tokens)
        flat_w = w.reshape(PIECES, 128, D)
        outputs, gup, gdn, gout, dmix, dhid, gvec = mlp(tokens, cotangent, mixed, vec, flat_w)
        parts = [gout, gup.reshape(32, 128, D), gdn]
        dz, chunk_a = back(z, dmix, parts, 1, 3, [(24, 32), (32, 64), (64, 96)], None)
        grad_tokens, chunk_b, gvec = tail_quick(tokens, dz, n1, dhid, vec, gvec, w, None)
        sums, clip = close(chunk_a, chunk_b, gvec, scale)
        weight_grad = sums.reshape(shard_len) * scale
        news = update(params, moment_one, moment_two, weight_grad, clip[0, 0])
        return (outputs, grad_tokens, weight_grad, *news)
    flat = lax.all_gather(params.astype(BF), "dp", axis=0, tiled=True)
    w = to_pieces(flat[:mats].reshape(-1, D), 0)
    vec = jnp.pad(flat[mats:].reshape(12, D).astype(F32), ((0, 4), (0, 0)))
    z, n1 = qkv(tokens, vec, w)
    mixed = attend(z)
    outputs, gup, gdn, gout, dmix, dhid, gvec = mlp(tokens, cotangent, mixed, vec, w)
    dz = attend_back(z, dmix)
    grad_tokens, gqkv, gvec = tail(tokens, dz, n1, dhid, vec, w, gvec)
    parts = [gqkv.reshape(24, 128, D), gout, gup.reshape(32, 128, D), gdn]
    flat = jnp.concatenate([from_pieces(jnp.concatenate(parts, axis=0), 0).reshape(-1), gvec[:12].reshape(-1).astype(BF)])
    arrived = lax.all_to_all(flat.reshape(n, shard_len), "dp", split_axis=0, concat_axis=0, tiled=True)
    weight_grad = jnp.sum(arrived.astype(F32), axis=0) * scale
    square_sum = lax.psum(jnp.sum(weight_grad * weight_grad), "dp")
    clip = jnp.minimum(1.0, max_norm / (jnp.sqrt(square_sum) + 1e-06))
    news = update(params, moment_one, moment_two, weight_grad, clip)
    return (outputs, grad_tokens, weight_grad, *news)


def solution(mesh):
    in_specs = (P("dp", None, None), P("dp", None, None), P("dp"), P("dp"), P("dp"))
    out_specs = (P("dp", None, None), P("dp", None, None), P("dp"), P("dp"), P("dp"), P("dp"))
    return jax.shard_map(shards, mesh=mesh, in_specs=in_specs, out_specs=out_specs, check_vma=False)
```

```python
import functools

import jax
import jax.numpy as jnp
from jax import lax
from jax.experimental import pallas as pl
from jax.experimental.pallas import tpu as pltpu
from jax.sharding import PartitionSpec as P

D = 1024
FF = 4096
S = 577
SQ = 592
M = 2 * SQ
CH = 32
PIECES = 96
STEP = 4
BF = jnp.bfloat16
F32 = jnp.float32
MESH = pl.DeviceIdType.MESH
VMEM_ALL = 67043328

EPS = 1e-06
max_norm = 1.0
beta_one = 0.9
beta_two = 0.95
learn_rate = 0.02
decay_rate = 0.05
adam_eps = 1e-08
SCORE = 0.125 * 1.4426950408889634


def nt(a, b):
    return lax.dot_general(a, b, (((1,), (1,)), ((), ())), preferred_element_type=F32)


def nn(a, b):
    return jnp.dot(a, b, preferred_element_type=F32)


def tn(a, b):
    return lax.dot_general(a, b, (((0,), (0,)), ((), ())), preferred_element_type=F32)


def rows_at(c):
    return pl.ds(pl.multiple_of(c * CH, CH), CH)


def full(shape):
    return pl.BlockSpec(shape, lambda *_: (0,) * len(shape), pipeline_mode=pl.Buffered(1))


class Ctx:
    def __init__(s):
        me=lax.axis_index("dp"); s.me=me
        s.core=me%2; s.x=(me//2)%2; s.y=(me//4)%2; s.z=me//8
        s.sib=me+1-2*s.core
        xp=me+2*(1-2*s.x); yp=me+4*(1-2*s.y)
        s.ap=xp+(yp-xp)*s.core
        s.bp=yp+(xp-yp)*s.core
        s.astep=2+2*s.core; s.bstep=4-2*s.core
        s.abit=s.x+(s.y-s.x)*s.core; s.bbit=s.y+(s.x-s.y)*s.core
        s.up=me+8; s.dn=me-8
        s.hasup=s.z<3; s.hasdn=s.z>0
    def barrier(s,extra=None):
        bar=pltpu.get_barrier_semaphore()
        for p in (s.sib,s.ap,s.bp): pl.semaphore_signal(bar,inc=1,device_id=(p,),device_id_type=MESH)
        @pl.when(s.hasup)
        def _(): pl.semaphore_signal(bar,inc=1,device_id=(s.up,),device_id_type=MESH)
        @pl.when(s.hasdn)
        def _(): pl.semaphore_signal(bar,inc=1,device_id=(s.dn,),device_id_type=MESH)
        more=0 if extra is None else extra
        pl.semaphore_wait(bar,3+jnp.where(s.hasup,1,0)+jnp.where(s.hasdn,1,0)+more)
class Gather:
    K = 3

    def __init__(s, c, own, w, ssem, rsem, lsem):
        s.c, s.own, s.w, s.ssem, s.rsem, s.lsem = c, own, w, ssem, rsem, lsem
        s.ns = 0
        s.pend = []

    def slot(s, dev, k):
        return s.rsem.at[dev * s.K + k]

    @staticmethod
    def when(conds, fn):
        if conds:
            pl.when(functools.reduce(jnp.logical_and, [f() for f in conds]))(fn)
        else:
            fn()

    def send(s, src, dev, k, to, outer, *conds):
        i = s.ns
        s.ns += 1
        cp = pltpu.make_async_remote_copy(
            src, s.w.at[dev, k], s.ssem.at[i], s.slot(dev, k), device_id=(to,), device_id_type=MESH
        )
        s.pend.append((i, outer + list(conds)))
        s.when(list(conds), cp.start)

    def step(s, text):
        kind = text[0]
        zz, k = int(text[-2]), int(text[-1])
        if kind == "o":
            s.give(text[1], zz, k)
        else:
            s.item(kind, zz, k)

    def give(s, route, zz, k):
        c = s.c
        to, conds = dict(
            d=(c.dn, [lambda: c.hasdn]), u=(c.up, [lambda: c.hasup]), b=(c.bp, []), a=(c.ap, []), s=(c.sib, [])
        )[route]
        here = [lambda: c.z == zz]
        s.when(here, lambda: s.send(s.own.at[k], c.me, k, to, here, *conds))

    def item(s, kind, zz, k):
        c = s.c
        src = c.me + 8 * (zz - c.z)
        if kind in "ac":
            src = src + c.astep * (1 - 2 * c.abit)
        if kind in "bc":
            src = src + c.bstep * (1 - 2 * c.bbit)
        outer = [lambda: c.z != zz] if kind == "z" else []

        def body():
            s.wait(src, k)
            r = s.w.at[src, k]
            cross = (zz, k) in CROSS_FIRST
            if kind == "z" or (cross and kind == "a"):
                s.send(r, src, k, c.up, outer, lambda: c.z >= zz, lambda: c.hasup)
                s.send(r, src, k, c.dn, outer, lambda: c.z <= zz, lambda: c.hasdn)
            if kind in "za":
                s.send(r, src, k, c.bp, outer)
            if kind == "z" and not cross:
                s.send(r, src, k, c.ap, outer)
            s.send(r, src, k, c.sib, outer)

        s.when(outer, body)

    def wait(s, dev, k):
        r = s.w.at[dev, k]
        pltpu.make_async_copy(r, r, s.slot(dev, k)).wait()

    def keep(s):
        for k in range(s.K):
            pltpu.make_async_copy(s.own.at[k], s.w.at[s.c.me, k], s.lsem.at[k]).start()

    def kept(s, k):
        pltpu.make_async_copy(s.own.at[k], s.w.at[s.c.me, k], s.lsem.at[k]).wait()

    def sibling(s, first, last, ks):
        def one(i, _):
            for k in ks:
                s.wait(2 * i + 1 - s.c.core, k)
            return 0

        lax.fori_loop(first, last, one, 0)

    def sent(s):
        for i, conds in s.pend:
            r = s.w.at[0, 0]
            s.when(conds, pltpu.make_async_copy(r, r, s.ssem.at[i]).wait)


class Vector:
    def __init__(s, c, own, vec, sem):
        s.c, s.own, s.vec, s.sem = c, own, vec, sem
        s.n = 31

    def tell(s):
        bar = pltpu.get_barrier_semaphore()

        @pl.when(s.c.me != s.n)
        def _():
            pl.semaphore_signal(bar, inc=1, device_id=(s.n,), device_id_type=MESH)

    def copy(s, to):
        return pltpu.make_async_remote_copy(
            s.own, s.vec, s.sem.at[to], s.sem.at[s.n], device_id=(to,), device_id_type=MESH
        )

    def start(s):
        @pl.when(s.c.me == s.n)
        def _():
            s.vec[...] = s.own[...]

            def one(i, _):
                s.copy(i).start()
                return 0

            lax.fori_loop(0, s.n, one, 0)

    def wait(s):
        @pl.when(s.c.me != s.n)
        def _():
            pltpu.make_async_copy(s.vec, s.vec, s.sem.at[s.n]).wait()

    def sent(s):
        @pl.when(s.c.me == s.n)
        def _():
            def one(i, _):
                s.copy(i).wait_send()
                return 0

            lax.fori_loop(0, s.n, one, 0)

class Reduce:
    K = 3

    @staticmethod
    def scratch(lo, hi, stage):
        nz = hi - lo + 1
        pieces = lambda n: pltpu.VMEM((n, 128, D), BF)
        dma = lambda n: pltpu.SemaphoreType.DMA((n,))
        sizes = [12 * nz, 6 * nz, 3 * nz, 3 * nz + 3]
        return (
            [pieces(n) for n in sizes]
            + [pieces(stage)]
            + [dma(12 * nz)]
            + [dma(n) for n in sizes]
            + [dma(12 * nz), dma(stage)]
        )

    def __init__(s, c, lo, hi, parts, out, scr, scale, order, direct=False, auto=True):
        s.auto = auto
        s.c, s.lo, s.hi, s.parts, s.out, s.scale, s.order, s.direct = c, lo, hi, parts, out, scale, order, direct
        s.S, s.B, s.A, s.Z, s.stage, s.sent_s, s.got_s, s.got_b, s.got_a, s.got_z, s.sent, s.loaded = scr
        s.nst = s.stage.shape[0]
        s.nz = hi - lo + 1
        s.later = []
        s.waits = []
        s.steps = [functools.partial(s.item, i) for i in range(len(order))]

    def owner(s, zz, fb, fa, core):
        c = s.c
        astep = 2 + 2 * core
        bstep = 4 - 2 * core
        abit = c.x + (c.y - c.x) * core
        bbit = c.y + (c.x - c.y) * core
        return zz * 8 + core + bstep * (bbit + fb * (1 - 2 * bbit)) + astep * (abit + fa * (1 - 2 * abit))

    def source(s, p, fn):
        if len(s.parts) == 1:
            lo, hi, ref = s.parts[0]
            fn(ref.at[p - lo])
            return
        for lo, hi, ref in s.parts:

            @pl.when(jnp.logical_and(p >= lo, p < hi))
            def _():
                fn(ref.at[jnp.clip(p - lo, 0, hi - lo - 1)])

    def slot(s, zz, fb, fa, k):
        return (((zz - s.lo) * 2 + fb) * 2 + fa) * s.K + k

    def places(s, order=None):
        for kind, zz, fa, k in order or s.order:
            if kind != "f":
                yield zz, 1 if kind == "b" else 0, fa, k

    def zero(s):
        c = s.c

        def clear(n):
            s.Z[n] = jnp.zeros((128, D), BF)

        for n in range(3 * s.nz + 3):
            at_zero = n < 3 * s.nz
            at_three = n >= 3 * s.nz or s.lo + n // 3 < 3
            if at_zero:
                pl.when(c.z == 0)(functools.partial(clear, n))
            if at_three:
                pl.when(c.z == 3)(functools.partial(clear, n))

    def to_sibling(s, order=None):
        c = s.c
        for zz, fb, fa, k in s.places(order):
            n = s.slot(zz, fb, fa, k)

            def go(r, n=n):
                pltpu.make_async_remote_copy(
                    r, s.S.at[n], s.sent_s.at[n], s.got_s.at[n], device_id=(c.sib,), device_id_type=MESH
                ).start()

            s.source(s.owner(zz, fb, fa, 1 - c.core) * s.K + k, go)

    def load(s, i):
        if s.direct or i >= len(s.order):
            return
        kind, zz, fa, k = s.order[i]
        n = i % s.nst

        def go(r):
            pltpu.make_async_copy(r, s.stage.at[n], s.loaded.at[n]).start()

        s.source(s.owner(zz, 1 if kind == "b" else 0, fa, s.c.core) * s.K + k, go)

    def prefetch(s):
        for i in range(s.nst - 1):
            s.load(i)

    def flush(s):
        for f in s.later:
            f()
        s.later = []

    @staticmethod
    def wait(ref, sem):
        pltpu.make_async_copy(ref, ref, sem).wait()

    @staticmethod
    def sum(srcs, dst, scale=None):
        def rows(r, _):
            rr = pl.ds(pl.multiple_of(r * 16, 16), 16)
            t = srcs[0][rr, :].astype(F32)
            for q in srcs[1:]:
                t = t + q[rr, :].astype(F32)
            if scale is not None:
                t = t * scale
            dst[rr, :] = t.astype(dst.dtype)
            return 0

        lax.fori_loop(0, 8, rows, 0)

    def item(s, i):
        c, K = s.c, s.K
        kind, zz, fa, k = s.order[i]
        fb = 1 if kind == "b" else 0
        if s.direct:
            lo, hi, ref = s.parts[0]
            own = ref.at[s.owner(zz, fb, fa, c.core) * K + k - lo]
        else:
            own = s.stage.at[i % s.nst]
            s.wait(own, s.loaded.at[i % s.nst])
        s.flush()
        n = s.slot(zz, fb, fa, k)
        out = s.S.at[n]
        bi = ((zz - s.lo) * 2 + fa) * K + k
        zi = (zz - s.lo) * K + k
        z2 = s.nz * K + k

        def gather(kinds):
            srcs = [own]
            if "S" in kinds:
                srcs.append((out, s.got_s.at[n]))
            if "B" in kinds:
                srcs.append((s.B.at[bi], s.got_b.at[bi]))
            if "A" in kinds:
                srcs.append((s.A.at[zi], s.got_a.at[zi]))
            for pair in srcs[1:]:
                s.wait(*pair)
            return srcs[:1] + [ref for ref, _ in srcs[1:]]

        def send(dst, sem, to):
            return pltpu.make_async_remote_copy(
                out, dst, s.sent.at[n], sem, device_id=(to,), device_id_type=MESH
            )

        if kind == "b":
            s.sum(gather("S"), out)
            s.later.append(send(s.B.at[bi], s.got_b.at[bi], c.bp).start)
            s.waits.append((n, None))
        elif kind == "a":
            s.sum(gather("SB"), out)
            s.later.append(send(s.A.at[zi], s.got_a.at[zi], c.ap).start)
            s.waits.append((n, None))
        elif kind == "z":

            @pl.when(c.z != zz)
            def _():
                srcs = gather("SBA")
                comes = jnp.where(c.z <= zz, c.z, 3 - c.z)
                pl.when(comes > 0)(functools.partial(s.wait, s.Z.at[zi], s.got_z.at[zi]))
                s.sum(srcs + [s.Z.at[zi]], out)

            def on():
                @pl.when(c.z < zz)
                def _():
                    send(s.Z.at[zi], s.got_z.at[zi], c.up).start()

                to = jnp.where(c.z == zz + 1, z2, zi)

                @pl.when(c.z > zz)
                def _():
                    send(s.Z.at[to], s.got_z.at[to], c.dn).start()

            s.later.append(on)
            s.waits.append((n, zz))
        else:

            @pl.when(c.z == zz)
            def _():
                srcs = gather("SBA")
                pl.when(c.hasdn)(functools.partial(s.wait, s.Z.at[zi], s.got_z.at[zi]))
                pl.when(c.hasup)(functools.partial(s.wait, s.Z.at[z2], s.got_z.at[z2]))
                s.sum(srcs + [s.Z.at[zi], s.Z.at[z2]], s.out.at[k], s.scale)

        if s.auto:
            s.load(i + s.nst - 1)

    def finish(s):
        s.flush()
        for n, zz in s.waits:
            w = functools.partial(s.wait, s.S.at[0], s.sent.at[n])
            if zz is None:
                w()
            else:
                pl.when(s.c.z != zz)(w)

        for place in s.places():
            s.wait(s.S.at[0], s.sent_s.at[s.slot(*place)])


BACK_STEPS = (
    ("b301", "b211", "b310", "b212",),
    ("b312", "b300", "b210",),
    ("b311", "b110", "a211", "b100", "b201",),
    (),
    (),
    ("b302",),
    ("a311",),
    ("a310",),
    ("z301", "a312", "a210",),
    ("z300", "b200", "a110", "b202",),
    ("a212", "b111", "z302", "z201",),
    (),
    ("z200", "b112",),
    ("b101", "a111", "z100",),
    ("b102", "z202", "f302", "a112", "f301", "f300", "z101",),
    ("f101", "f201", "f100", "f202", "z102",),
    ("f102", "f200",),
)
TAIL_STEPS = (
    (),
    (),
    ("b000", "b010",),
    ("b011", "b001",),
    ("a010", "a011", "b012", "b002",),
    ("z000",),
    ("a012", "f000", "z001",),
    ("f001", "z002",),
    ("f002",),
)


def reduce_order(groups):
    order = [(t[0], int(t[1]), int(t[2]), int(t[3])) for g in groups for t in g]
    ends = [sum(len(g) for g in groups[: i + 1]) for i in range(len(groups))]
    return order, [list(range(e - len(g), e)) for e, g in zip(ends, groups)]


def qkv_kernel(x_ref, vec_ref, w_ref, out_ref, n_ref):
    j = pl.program_id(0)

    @pl.when(j == 0)
    def _():
        for i in range(2):

            def block(rows, dst):
                v = x_ref[i, rows, :].astype(F32)
                c = v - jnp.mean(v, axis=1, keepdims=True)
                rc = lax.rsqrt(jnp.mean(c * c, axis=1, keepdims=True) + EPS)
                return (c * rc * (1.0 + vec_ref[8:9, :]) + vec_ref[9:10, :]).astype(BF)

            def one(c, _):
                n_ref[i, rows_at(c), :] = block(rows_at(c), None)
                return 0

            lax.fori_loop(0, 18, one, 0)
            last = block(slice(576, 577), None).astype(F32)
            n_ref[i, 576:592, :] = jnp.concatenate([last, jnp.zeros((15, D), F32)], axis=0).astype(BF)

    w = w_ref[...].reshape(D, D)
    bias = jnp.where(j == 0, vec_ref[0:1, :], jnp.where(j == 2, vec_ref[1:2, :], 0.0))
    for i in range(2):
        out_ref[0, i] = (nn(n_ref[i], w) + bias).astype(BF)


def qkv(x, vec, w):
    return pl.pallas_call(
        qkv_kernel,
        grid=(3,),
        in_specs=[full((2, S, D)), full((16, D)), pl.BlockSpec((8, 1, 128, D), lambda j: (0, j, 0, 0))],
        out_specs=[pl.BlockSpec((1, 2, SQ, D), lambda j: (j, 0, 0, 0)), full((2, SQ, D))],
        out_shape=[jax.ShapeDtypeStruct((3, 2, SQ, D), BF), jax.ShapeDtypeStruct((2, SQ, D), BF)],
        compiler_params=pltpu.CompilerParams(vmem_limit_bytes=VMEM_ALL),
        name="qkv",
    )(x, vec, w.reshape(32, 3, 128, D))


def padded(v):
    return jnp.concatenate([v, jnp.zeros((640 - SQ, 128), v.dtype)], axis=0)


def attend_pair(q, k, v):
    lane = lax.broadcasted_iota(jnp.int32, (1, 128), 1)
    k = padded(k)
    v = padded(v)
    outs = []
    for h in range(2):
        mine = lane < 64 if h == 0 else lane >= 64
        s = nt(jnp.where(mine, q, jnp.zeros_like(q)), k)
        s = jnp.concatenate([s[:, :512], jnp.where(lane < S - 512, s[:, 512:], -1e30)], axis=1)
        top = jnp.max(s, axis=1, keepdims=True)
        p = jnp.exp2((s - top) * SCORE)
        total = jnp.sum(p, axis=1, keepdims=True)
        outs.append(nn(p.astype(BF), v) * (1.0 / total))
    return jnp.where(lane < 64, outs[0], outs[1]).astype(BF)


def attend_kernel(q_ref, k_ref, v_ref, o_ref):
    half = SQ // 2
    for r in range(2):
        rows = slice(r * half, (r + 1) * half)
        o_ref[0, rows, :] = attend_pair(q_ref[0, 0, rows, :], k_ref[0, 0], v_ref[0, 0])


def attend(z):
    spec = lambda j: pl.BlockSpec((1, 1, SQ, 128), lambda i, h: (j, i, 0, h))
    return pl.pallas_call(
        attend_kernel,
        grid=(2, 8),
        in_specs=[spec(0), spec(1), spec(2)],
        out_specs=pl.BlockSpec((1, SQ, 128), lambda i, h: (i, 0, h)),
        out_shape=jax.ShapeDtypeStruct((2, SQ, D), BF),
        compiler_params=pltpu.CompilerParams(vmem_limit_bytes=VMEM_ALL),
        name="attend",
    )(z, z, z)


def norm_block(v, vec_ref):
    v = v.astype(F32)
    ce = v - jnp.mean(v, axis=1, keepdims=True)
    rc = lax.rsqrt(jnp.mean(ce * ce, axis=1, keepdims=True) + EPS)
    return (ce * rc * (1.0 + vec_ref[8:9, :]) + vec_ref[9:10, :]).astype(BF)


def norm_one(x_ref, vec_ref, n_ref):
    for i in range(2):

        def one(c, _):
            n_ref[i, rows_at(c), :] = norm_block(x_ref[i, rows_at(c), :], vec_ref)
            return 0

        lax.fori_loop(0, 18, one, 0)
        last = norm_block(x_ref[i, 576:577, :], vec_ref).astype(F32)
        n_ref[i, 576:592, :] = jnp.concatenate([last, jnp.zeros((15, D), F32)], axis=0).astype(BF)


FRONT_STEPS = (
    ("ob30", "os11", "os32", "ob00", "oa32", "ou00", "ou20", "ob21", "oa20", "ou21", "od12", "oa31", "oa00", "os10", "od10", "os00", "oa10", "os02", "ob32", "os22", "od31", "od32", "ob10", "ob20", "od22", "ob22", "od11", "ou10", "oa02", "oa30", "z00", "a00", "b00", "os21", "ob01", "oa01", "z01", "z02", "ou01", "ob31", "ou11", "ob02", "od20",),
    ("os20", "ou02", "a01", "ou12", "os12", "ou22", "c00", "a02", "z22", "z10", "z12", "os01", "z20", "b01", "c01", "os30", "ob12", "b02", "od30", "z11", "od21", "oa11", "ou31",),
    ("oa12", "c02", "oa21", "a10", "b10", "ou30", "ou32", "ob11",),
    ("a11",),
    (),
    ("z21",),
    ("a12", "z30",),
    (),
    ("z31", "c10", "b12",),
    ("os31", "z32", "a30",),
    ("b21",),
    ("a20", "a21",),
    (),
    ("oa22", "a31", "c11",),
    (),
    ("b20", "a22", "b31", "b32", "b22", "c21", "a32",),
    ("c30", "c12", "c20",),
    ("c31", "b11",),
    (),
    ("b30", "c22",),
    ("c32",),
)
CROSS_FIRST = ((1, 1), (2, 1), (1, 2), (2, 2), (1, 0))


def front_kernel(
    own, vec_own, x_ref, w, vec, z_out, n_out, mix_out, z_ref, n_ref, mix_ref, osem, vlow, wq, qsem, vsem, ssem, rsem, lsem
):
    c = Ctx()
    g = Gather(c, own, w, ssem, rsem, lsem)
    vector = Vector(c, vec_own, vlow, vsem)
    vector.tell()
    c.barrier(jnp.where(c.me == 31, 31, 0))
    vector.start()
    g.keep()

    def take(n):
        for text in FRONT_STEPS[n]:
            g.step(text)

    take(0)
    vector.wait()
    vec[...] = vlow[...].astype(F32)
    norm_one(x_ref, vec, n_ref)
    leave = [pltpu.make_async_copy(n_ref, n_out, osem.at[0])]
    leave[0].start()
    for j in range(3):
        take(1 + j)
        g.kept(j)
        g.sibling(0, 4, (j,))
        load = pltpu.make_async_copy(w.at[0:8, j], wq.at[j % 2], qsem.at[j])
        load.start()
        load.wait()
        for i in range(2):
            r = nn(n_ref[i], wq[j % 2].reshape(D, D))
            if j != 1:
                r = r + vec[j // 2 : j // 2 + 1, :]
            z_ref[j, i] = r.astype(BF)
    leave.append(pltpu.make_async_copy(z_ref, z_out, osem.at[1]))
    leave[1].start()

    def pair(t, _):
        for n in range(16):
            if FRONT_STEPS[4 + n]:

                @pl.when(t == n)
                def _():
                    take(4 + n)

        i = t // 8
        cols = pl.ds(pl.multiple_of((t % 8) * 128, 128), 128)
        half = SQ // 2
        k = z_ref[1, i, :, cols]
        v = z_ref[2, i, :, cols]
        for r in range(2):
            rows = slice(r * half, (r + 1) * half)
            mix_ref[i, rows, cols] = attend_pair(z_ref[0, i, rows, cols], k, v)
        return 0

    lax.fori_loop(0, 16, pair, 0)
    leave.append(pltpu.make_async_copy(mix_ref, mix_out, osem.at[2]))
    leave[2].start()
    take(20)
    g.sibling(4, 16, (0, 1, 2))
    g.sent()
    vector.sent()
    for cp in leave:
        cp.wait()


def front(own, vec_own, x):
    vm = pl.BlockSpec(memory_space=pltpu.VMEM)
    far = pl.BlockSpec(memory_space=pl.ANY)
    dma = lambda n: pltpu.SemaphoreType.DMA((n,))
    return pl.pallas_call(
        front_kernel,
        in_specs=[vm, vm, vm],
        out_specs=[far, vm, far, far, far],
        out_shape=[
            jax.ShapeDtypeStruct((32, 3, 128, D), BF),
            jax.ShapeDtypeStruct((16, D), F32),
            jax.ShapeDtypeStruct((3, 2, SQ, D), BF),
            jax.ShapeDtypeStruct((2, SQ, D), BF),
            jax.ShapeDtypeStruct((2, SQ, D), BF),
        ],
        scratch_shapes=[pltpu.VMEM((3, 2, SQ, D), BF), pltpu.VMEM((2, SQ, D), BF), pltpu.VMEM((2, SQ, D), BF), dma(3)]
        + [pltpu.VMEM((16, D), BF), pltpu.VMEM((2, 8, 128, D), BF), dma(3), dma(32)]
        + [dma(300), dma(96), dma(3)],
        compiler_params=pltpu.CompilerParams(collective_id=1, has_side_effects=True, vmem_limit_bytes=VMEM_ALL),
        name="front",
    )(own, vec_own, x)


def attend_back_pair(q, k, v, do):
    lane = lax.broadcasted_iota(jnp.int32, (1, 128), 1)
    real = lax.broadcasted_iota(jnp.int32, (16, 1), 0) < S - 576
    q = padded(q)
    do = padded(do)
    dqs, dks, dvs = [], [], []
    for h in range(2):
        mine = lane < 64 if h == 0 else lane >= 64
        s = nt(jnp.where(mine, k, jnp.zeros_like(k)), q)
        s = jnp.concatenate([s[:576], jnp.where(real, s[576:], -1e30)], axis=0)
        top = jnp.max(s, axis=0, keepdims=True)
        p = jnp.exp2((s - top) * SCORE)
        p = p * (1.0 / jnp.sum(p, axis=0, keepdims=True))
        dvs.append(nn(p.astype(BF), do))
        dp = nt(jnp.where(mine, v, jnp.zeros_like(v)), do)
        ds = (p * (dp - jnp.sum(p * dp, axis=0, keepdims=True))).astype(BF)
        dks.append(nn(ds, q))
        dqs.append(tn(ds, k))
    pick = lambda pair, scale: (jnp.where(lane < 64, pair[0], pair[1]) * scale).astype(BF)
    return pick(dqs, 0.125)[:SQ], pick(dks, 0.125), pick(dvs, 1.0)


def attend_back_kernel(q_ref, k_ref, v_ref, do_ref, out_ref):
    dq, dk, dv = attend_back_pair(q_ref[0, 0], k_ref[0, 0], v_ref[0, 0], do_ref[0])
    out_ref[0, 0] = dq
    out_ref[1, 0] = dk
    out_ref[2, 0] = dv


def attend_back(z, do):
    spec = lambda j: pl.BlockSpec((1, 1, SQ, 128), lambda i, h: (j, i, 0, h))
    return pl.pallas_call(
        attend_back_kernel,
        grid=(2, 8),
        in_specs=[spec(0), spec(1), spec(2), pl.BlockSpec((1, SQ, 128), lambda i, h: (i, 0, h))],
        out_specs=pl.BlockSpec((3, 1, SQ, 128), lambda i, h: (0, i, 0, h)),
        out_shape=jax.ShapeDtypeStruct((3, 2, SQ, D), BF),
        compiler_params=pltpu.CompilerParams(vmem_limit_bytes=VMEM_ALL),
        name="attend_back",
    )(z, z, z, do)


def mlp_kernel(x_ref,g_ref,mix_ref,vec_ref,wo_ref,wu_ref,wd_ref,
               out_ref,gup_ref,gdn_ref,gout_ref,dmix_ref,dhid_ref,gvec_ref,
               n2,gs,acc,dn,stat,*,FB,NB):
    jb=pl.program_id(0)
    hid=dhid_ref
    @pl.when(jb==0)
    def _():
        wo=wo_ref[...].reshape(D,D)
        for i in range(2):
            hid[i*SQ:(i+1)*SQ,:]=nn(mix_ref[i],wo)
            gs[i*SQ:i*SQ+576,:]=g_ref[i,:576,:]
            gs[i*SQ+576:(i+1)*SQ,:]=jnp.concatenate([g_ref[i,576:577,:].astype(F32),jnp.zeros((15,D),F32)],axis=0).astype(BF)
            def addx(c,_):
                r=pl.multiple_of(c*CH,CH)
                hid[pl.ds(i*SQ+r,CH),:]+=x_ref[i,pl.ds(r,CH),:].astype(F32)+vec_ref[2:3,:]
                return 0
            lax.fori_loop(0,18,addx,0)
            hid[i*SQ+576:i*SQ+577,:]+=x_ref[i,576:577,:].astype(F32)+vec_ref[2:3,:]
        acc[...]=jnp.zeros_like(acc); dn[...]=jnp.zeros_like(dn)
        gvec_ref[...]=jnp.zeros_like(gvec_ref)
        def ln(c,_):
            r=pl.ds(pl.multiple_of(c*CH,CH),CH)
            h=hid[r,:]
            mu=jnp.mean(h,axis=1,keepdims=True)
            ce=h-mu
            rc=lax.rsqrt(jnp.mean(ce*ce,axis=1,keepdims=True)+EPS)
            n2[r,:]=(ce*rc*(1.0+vec_ref[10:11,:])+vec_ref[11:12,:]).astype(BF)
            stat[r,0:1]=mu; stat[r,1:2]=rc
            return 0
        lax.fori_loop(0,M//CH,ln,0)
        def gsum(c,a):
            r=pl.ds(pl.multiple_of(c*CH,CH),CH)
            return a+gs[r,:].astype(F32)
        t=lax.fori_loop(0,M//CH,gsum,jnp.zeros((CH,D),F32))
        gvec_ref[7:8,:]=jnp.sum(t,axis=0,keepdims=True)
    wu=wu_ref[...].reshape(D,FB); wd=wd_ref[...].reshape(FB,D)
    nper=D//FB
    row=vec_ref[pl.ds(3+jb//nper,1),:]
    bup=row[:,:FB]
    for t in range(1,nper): bup=jnp.where(jb%nper==t,row[:,t*FB:(t+1)*FB],bup)
    g=gs[...]; n=n2[...]
    acts=[];dps=[]
    pres=[nn(n[i*SQ:(i+1)*SQ],wu)+bup for i in range(2)]
    das=[nt(g[i*SQ:(i+1)*SQ],wd) for i in range(2)]
    for i in range(2):
        pre=pres[i]
        cdf=0.5*(1.0+lax.erf(pre*0.7071067811865476))
        act=(pre*cdf).astype(BF)
        slope=cdf+pre*0.3989422804014327*jnp.exp(-0.5*pre*pre)
        dp=(das[i]*slope).astype(BF)
        acc[i*SQ:(i+1)*SQ,:]+=nn(act,wd)
        dn[i*SQ:(i+1)*SQ,:]+=nt(dp,wu)
        acts.append(act);dps.append(dp)
    act=jnp.concatenate(acts,axis=0);dp=jnp.concatenate(dps,axis=0)
    gup_ref[...]=tn(n,dp).astype(BF).reshape(gup_ref.shape)
    gdn_ref[...]=tn(act,g).astype(BF).reshape(gdn_ref.shape)
    bsum=jnp.sum(dp.astype(F32),axis=0,keepdims=True)
    for t in range(nper):
        @pl.when(jb%nper==t)
        def _(): gvec_ref[pl.ds(3+jb//nper,1),t*FB:(t+1)*FB]=bsum
    @pl.when(jb==NB-1)
    def _():
        for i in range(2):
            def ob(c,_):
                r=pl.multiple_of(c*CH,CH)
                out_ref[i,pl.ds(r,CH),:]=(hid[pl.ds(i*SQ+r,CH),:]+(acc[pl.ds(i*SQ+r,CH),:]+vec_ref[7:8,:])).astype(BF)
                return 0
            lax.fori_loop(0,18,ob,0)
            out_ref[i,576:577,:]=(hid[i*SQ+576:i*SQ+577,:]+(acc[i*SQ+576:i*SQ+577,:]+vec_ref[7:8,:])).astype(BF)
        def bk(c,car):
            a,b,d=car
            r=pl.ds(pl.multiple_of(c*CH,CH),CH)
            mu=stat[r,0:1]; rc=stat[r,1:2]
            xh=(hid[r,:]-mu)*rc
            dd=dn[r,:]
            e=dd*(1.0+vec_ref[10:11,:])
            dh=gs[r,:].astype(F32)+rc*(e-jnp.mean(e,axis=1,keepdims=True)-xh*jnp.mean(e*xh,axis=1,keepdims=True))
            dhid_ref[r,:]=dh
            db=dh.astype(BF)
            n2[r,:]=db
            return (a+dd*xh,b+dd,d+db.astype(F32))
        zz=jnp.zeros((CH,D),F32)
        a,b,d=lax.fori_loop(0,M//CH,bk,(zz,zz,zz))
        gvec_ref[10:11,:]=jnp.sum(a,axis=0,keepdims=True)
        gvec_ref[11:12,:]=jnp.sum(b,axis=0,keepdims=True)
        gvec_ref[2:3,:]=jnp.sum(d,axis=0,keepdims=True)
        db=n2[...]
        wo=wo_ref[...].reshape(D,D)
        dmix_ref[...]=nt(db,wo).astype(BF).reshape(2,SQ,D)
        gout_ref[...]=tn(mix_ref[...].reshape(M,D),db).astype(BF).reshape(8,128,D)
def mlp(x,g,mix,vec,W,FB=512):
    NB=4096//FB; nper=D//FB
    W4=W.reshape(96,4,32,1024)
    return pl.pallas_call(functools.partial(mlp_kernel,FB=FB,NB=NB),grid=(NB,),
      in_specs=[full((2,S,D)),full((2,S,D)),full((2,SQ,D)),full((16,D)),
        pl.BlockSpec((8,128,D),lambda j:(3,0,0),pipeline_mode=pl.Buffered(1)),
        pl.BlockSpec((32,1,32,FB),lambda j:(1,j//nper,0,j%nper)),
        pl.BlockSpec((FB//128,128,D),lambda j:(64//(FB//128)+j,0,0))],
      out_specs=[full((2,S,D)),pl.BlockSpec((32,1,32,FB),lambda j:(0,j//nper,0,j%nper)),
        pl.BlockSpec((FB//128,128,D),lambda j:(j,0,0)),full((8,128,D)),full((2,SQ,D)),full((M,D)),full((16,D))],
      out_shape=[jax.ShapeDtypeStruct((2,S,D),BF),jax.ShapeDtypeStruct((32,4,32,D),BF),jax.ShapeDtypeStruct((32,128,D),BF),
        jax.ShapeDtypeStruct((8,128,D),BF),jax.ShapeDtypeStruct((2,SQ,D),BF),jax.ShapeDtypeStruct((M,D),F32),jax.ShapeDtypeStruct((16,D),F32)],
      scratch_shapes=[pltpu.VMEM((M,D),BF),pltpu.VMEM((M,D),BF),pltpu.VMEM((M,D),F32),pltpu.VMEM((M,D),F32),pltpu.VMEM((M,128),F32)],
      compiler_params=pltpu.CompilerParams(vmem_limit_bytes=67043328),name=f"mlp{FB}")(x,g,mix,vec,W,W4,W)


def tail_kernel(x_ref, dz_ref, n_ref, dhid_ref, vec_ref, w_ref, gvin_ref, gx_ref, gw_ref, gvec_ref, acc):
    j = pl.program_id(0)

    @pl.when(j == 0)
    def _():
        gvec_ref[...] = gvin_ref[...]
        acc[...] = jnp.zeros_like(acc)

    w = w_ref[...].reshape(D, D)
    dz = dz_ref[0].reshape(M, D)
    acc[...] += nt(dz, w)
    gw_ref[...] = tn(n_ref[...].reshape(M, D), dz).astype(BF).reshape(8, 1, 128, D)

    @pl.when(j != 1)
    def _():
        def add(c, t):
            return t + dz_ref[0, 0, pl.ds(c * 16, 16), :].astype(F32) + dz_ref[0, 1, pl.ds(c * 16, 16), :].astype(F32)

        t = lax.fori_loop(0, SQ // 16, add, jnp.zeros((16, D), F32))
        gvec_ref[pl.ds(j // 2, 1), :] = jnp.sum(t, axis=0, keepdims=True)

    @pl.when(j == 2)
    def _():
        def back(x, dd, dh):
            v = x.astype(F32)
            ce = v - jnp.mean(v, axis=1, keepdims=True)
            rc = lax.rsqrt(jnp.mean(ce * ce, axis=1, keepdims=True) + EPS)
            xh = ce * rc
            e = dd * (1.0 + vec_ref[8:9, :])
            g = dh + rc * (e - jnp.mean(e, axis=1, keepdims=True) - xh * jnp.mean(e * xh, axis=1, keepdims=True))
            return g.astype(BF), dd * xh, dd

        a = b = jnp.zeros((CH, D), F32)
        la = lb = jnp.zeros((1, D), F32)
        for i in range(2):

            def one(c, carry):
                r = rows_at(c)
                r2 = pl.ds(pl.multiple_of(i * SQ + c * CH, 16), CH)
                g, s1, s2 = back(x_ref[i, r, :], acc[r2, :], dhid_ref[r2, :])
                gx_ref[i, r, :] = g
                return carry[0] + s1, carry[1] + s2

            a, b = lax.fori_loop(0, 18, one, (a, b))
            r2 = slice(i * SQ + 576, i * SQ + 577)
            g, s1, s2 = back(x_ref[i, 576:577, :], acc[r2, :], dhid_ref[r2, :])
            gx_ref[i, 576:577, :] = g
            la, lb = la + s1, lb + s2
        gvec_ref[8:9, :] = jnp.sum(a, axis=0, keepdims=True) + la
        gvec_ref[9:10, :] = jnp.sum(b, axis=0, keepdims=True) + lb


def tail(x, dz, n1, dhid, vec, w, gvec):
    return pl.pallas_call(
        tail_kernel,
        grid=(3,),
        in_specs=[
            full((2, S, D)),
            pl.BlockSpec((1, 2, SQ, D), lambda j: (j, 0, 0, 0)),
            full((2, SQ, D)),
            full((M, D)),
            full((16, D)),
            pl.BlockSpec((8, 1, 128, D), lambda j: (0, j, 0, 0)),
            full((16, D)),
        ],
        out_specs=[full((2, S, D)), pl.BlockSpec((8, 1, 128, D), lambda j: (0, j, 0, 0)), full((16, D))],
        out_shape=[
            jax.ShapeDtypeStruct((2, S, D), BF),
            jax.ShapeDtypeStruct((8, 3, 128, D), BF),
            jax.ShapeDtypeStruct((16, D), F32),
        ],
        scratch_shapes=[pltpu.VMEM((M, D), F32)],
        compiler_params=pltpu.CompilerParams(vmem_limit_bytes=VMEM_ALL),
        name="tail",
    )(x, dz, n1, dhid, vec, w.reshape(32, 3, 128, D), gvec)

def back_kernel(z_in, do_in, *refs, lo, hi, ranges, scale):
    n = len(ranges)
    parts = [(a, b, r) for (a, b), r in zip(ranges, refs[:n])]
    dz_out, chunk, z_ref, do_ref, dz_ref, iosem = refs[n : n + 6]
    c = Ctx()
    loads = [pltpu.make_async_copy(z_in.at[j], z_ref.at[j], iosem.at[j]) for j in range(3)]
    loads.append(pltpu.make_async_copy(do_in, do_ref, iosem.at[3]))
    for cp in loads:
        cp.start()
    order, groups = reduce_order(BACK_STEPS)
    red = Reduce(c, lo, hi, parts, chunk, refs[n + 6 :], scale, order)
    red.zero()
    chunk[...] = jnp.zeros_like(chunk)
    c.barrier()
    red.to_sibling()
    red.prefetch()
    for cp in loads:
        cp.wait()

    def pair(t, _):
        for m in range(16):
            if groups[m]:

                @pl.when(t == m)
                def _():
                    for i in groups[m]:
                        red.steps[i]()
                    red.flush()

        i = t // 8
        cols = pl.ds(pl.multiple_of((t % 8) * 128, 128), 128)
        dq, dk, dv = attend_back_pair(z_ref[0, i, :, cols], z_ref[1, i, :, cols], z_ref[2, i, :, cols], do_ref[i, :, cols])
        dz_ref[0, i, :, cols] = dq
        dz_ref[1, i, :, cols] = dk
        dz_ref[2, i, :, cols] = dv
        return 0

    lax.fori_loop(0, 16, pair, 0)
    leave = pltpu.make_async_copy(dz_ref, dz_out, iosem.at[4])
    leave.start()
    for i in groups[16]:
        red.steps[i]()
    red.finish()
    leave.wait()


def back(z, do, parts, lo, hi, ranges, scale):
    vm = pl.BlockSpec(memory_space=pltpu.VMEM)
    return pl.pallas_call(
        functools.partial(back_kernel, lo=lo, hi=hi, ranges=ranges, scale=scale),
        in_specs=[pl.BlockSpec(memory_space=pl.ANY)] * (2 + len(parts)),
        out_specs=[pl.BlockSpec(memory_space=pl.ANY), vm],
        out_shape=[jax.ShapeDtypeStruct((3, 2, SQ, D), BF), jax.ShapeDtypeStruct((3, 128, D), F32)],
        scratch_shapes=[
            pltpu.VMEM((3, 2, SQ, D), BF),
            pltpu.VMEM((2, SQ, D), BF),
            pltpu.VMEM((3, 2, SQ, D), BF),
            pltpu.SemaphoreType.DMA((5,)),
        ]
        + Reduce.scratch(lo, hi, 4),
        compiler_params=pltpu.CompilerParams(collective_id=2, has_side_effects=True, vmem_limit_bytes=VMEM_ALL),
        name="back",
    )(z, do, *parts)


def back_norm(x, dd, dh, vec_ref):
    v = x.astype(F32)
    ce = v - jnp.mean(v, axis=1, keepdims=True)
    rc = lax.rsqrt(jnp.mean(ce * ce, axis=1, keepdims=True) + EPS)
    xh = ce * rc
    e = dd * (1.0 + vec_ref[8:9, :])
    g = dh + rc * (e - jnp.mean(e, axis=1, keepdims=True) - xh * jnp.mean(e * xh, axis=1, keepdims=True))
    return g.astype(BF), dd * xh


def tail_quick_kernel(
    x_in, dz_ref, n_ref, dhid_in, vec_ref, gvin_ref, w, gx_ref, chunk, gvec_ref,
    x_ref, dhid_ref, xsem, acc, gw, wq, qsem, *scr, scale
):
    c = Ctx()
    order, groups = reduce_order(TAIL_STEPS)
    red = Reduce(c, 0, 0, [(0, 24, gw)], chunk, scr, scale, order, direct=True)
    loads = [pltpu.make_async_copy(w.at[0:8, j], wq.at[j % 2], qsem.at[j]) for j in range(3)]
    loads[0].start()
    loads[1].start()
    late = [pltpu.make_async_copy(x_in, x_ref, xsem.at[0]), pltpu.make_async_copy(dhid_in, dhid_ref, xsem.at[1])]
    for cp in late:
        cp.start()
    red.zero()
    chunk[...] = jnp.zeros_like(chunk)
    gvec_ref[...] = gvin_ref[...]
    c.barrier()

    def take(n):
        for i in groups[n]:
            red.steps[i]()
        red.flush()

    def weights(j):
        g = tn(n_ref[...].reshape(M, D), dz_ref[j].reshape(M, D)).astype(BF)
        for d in range(8):
            gw[3 * d + j] = g[128 * d : 128 * (d + 1)]

    def colsum(j):
        def add(r, t):
            rr = pl.ds(pl.multiple_of(r * 16, 16), 16)
            return t + dz_ref[j, 0, rr, :].astype(F32) + dz_ref[j, 1, rr, :].astype(F32)

        t = lax.fori_loop(0, SQ // 16, add, jnp.zeros((16, D), F32))
        gvec_ref[j // 2 : j // 2 + 1, :] = jnp.sum(t, axis=0, keepdims=True)

    def inputs(j):
        loads[j].wait()
        wj = wq[j % 2].reshape(D, D)
        for i in range(2):
            r = nt(dz_ref[j, i], wj)
            rows = slice(i * SQ, (i + 1) * SQ)
            acc[rows, :] = r if j == 0 else acc[rows, :] + r

    some = lambda k: [o for o in order if o[3] == k]
    weights(0)
    colsum(0)
    red.to_sibling(some(0))
    weights(1)
    red.to_sibling(some(1))
    take(2)
    weights(2)
    colsum(2)
    red.to_sibling(some(2))
    take(3)
    for j in range(3):
        inputs(j)
        if j == 0:
            loads[2].start()
        take(4 + j)
    for cp in late:
        cp.wait()
    a = b = jnp.zeros((CH, D), F32)
    la = lb = jnp.zeros((1, D), F32)
    for i in range(2):

        def one(t, carry):
            r = rows_at(t)
            r2 = pl.ds(pl.multiple_of(i * SQ + t * CH, 16), CH)
            dd = acc[r2, :]
            g, s1 = back_norm(x_ref[i, r, :], dd, dhid_ref[r2, :], vec_ref)
            gx_ref[i, r, :] = g
            return carry[0] + s1, carry[1] + dd

        a, b = lax.fori_loop(0, 18, one, (a, b))
        r2 = slice(i * SQ + 576, i * SQ + 577)
        dd = acc[r2, :]
        g, s1 = back_norm(x_ref[i, 576:577, :], dd, dhid_ref[r2, :], vec_ref)
        gx_ref[i, 576:577, :] = g
        la, lb = la + s1, lb + dd
        take(7 + i)
    gvec_ref[8:9, :] = jnp.sum(a, axis=0, keepdims=True) + la
    gvec_ref[9:10, :] = jnp.sum(b, axis=0, keepdims=True) + lb
    red.finish()


def tail_quick(x, dz, n1, dhid, vec, gvec, w, scale):
    vm = pl.BlockSpec(memory_space=pltpu.VMEM)
    far = pl.BlockSpec(memory_space=pl.ANY)
    return pl.pallas_call(
        functools.partial(tail_quick_kernel, scale=scale),
        in_specs=[far, vm, vm, far, vm, vm, far],
        out_specs=[vm] * 3,
        out_shape=[
            jax.ShapeDtypeStruct((2, S, D), BF),
            jax.ShapeDtypeStruct((3, 128, D), F32),
            jax.ShapeDtypeStruct((16, D), F32),
        ],
        scratch_shapes=[
            pltpu.VMEM((2, S, D), BF),
            pltpu.VMEM((M, D), F32),
            pltpu.SemaphoreType.DMA((2,)),
            pltpu.VMEM((M, D), F32),
            pltpu.VMEM((24, 128, D), BF),
            pltpu.VMEM((2, 8, 128, D), BF),
            pltpu.SemaphoreType.DMA((3,)),
        ]
        + Reduce.scratch(0, 0, 1),
        compiler_params=pltpu.CompilerParams(collective_id=3, has_side_effects=True, vmem_limit_bytes=VMEM_ALL),
        name="tail_quick",
    )(x, dz, n1, dhid, vec, gvec, w)


def close_kernel(chunk_a, chunk_b, gvec, wg, clip_ref, flat, e, es, ea, eb, ez, sem, *, scale):
    c = Ctx()
    me = c.me
    bar = pltpu.get_barrier_semaphore()
    others = [c.sib, c.ap, c.bp] + [lax.rem(me + 8 * i, 32) for i in (1, 2, 3)]
    for to in others:
        pl.semaphore_signal(bar, inc=1, device_id=(to,), device_id_type=MESH)
    first, last = me == 0, me == 31

    @pl.when(jnp.logical_not(first))
    def _():
        pl.semaphore_signal(bar, inc=1, device_id=(me - 1,), device_id_type=MESH)

    @pl.when(jnp.logical_not(last))
    def _():
        pl.semaphore_signal(bar, inc=1, device_id=(me + 1,), device_id_type=MESH)

    def unfold(src, k, kind):
        for t in range(8):
            cols = slice(128 * t, 128 * (t + 1))
            if kind == 0:
                flat[pl.ds(8 * k + t, 128, stride=24), :] = src[k, :, cols]
            elif kind == 1:
                flat[pl.ds(1024 * k + t, 128, stride=8), :] = src[k, :, cols]
            else:
                for j in range(4):
                    flat[pl.ds(1024 * k + 8 * j + t, 32, stride=32), :] = src[k, 32 * j : 32 * j + 32, cols]

    for k in range(3):
        p = 3 * me + k
        up = jnp.logical_and(p >= 32, p < 64)
        pl.when(c.z == 0)(functools.partial(unfold, chunk_b, k, 0))
        pl.when(up)(functools.partial(unfold, chunk_a, k, 2))
        pl.when(jnp.logical_and(c.z > 0, jnp.logical_not(up)))(functools.partial(unfold, chunk_a, k, 1))

    def square(i, t):
        v = flat[pl.ds(pl.multiple_of(i * 64, 64), 64), :]
        return t + v * v

    sq = jnp.sum(lax.fori_loop(0, 48, square, jnp.zeros((64, 128), F32)))
    e[0:12, :] = gvec[0:12, :]
    e[12:16, :] = jnp.full((4, D), sq, F32)
    pl.semaphore_wait(bar, 6 + jnp.where(first, 0, 1) + jnp.where(last, 0, 1))
    head = flat.at[0:96]
    room = flat.at[3072:3168]
    edge = pltpu.make_async_remote_copy(
        head, room, sem.at[14], sem.at[15], device_id=(jnp.maximum(me - 1, 0),), device_id_type=MESH
    )
    pl.when(jnp.logical_not(first))(edge.start)
    for n, (to, dst) in enumerate(((c.sib, es), (c.ap, ea), (c.bp, eb))):
        cp = pltpu.make_async_remote_copy(e, dst, sem.at[n], sem.at[3 + n], device_id=(to,), device_id_type=MESH)
        cp.start()
        cp.wait()
        e[...] = e[...] + dst[...]
    ez[c.z] = e[...]
    cps = []
    for i in (1, 2, 3):
        to = lax.rem(me + 8 * i, 32)
        cp = pltpu.make_async_remote_copy(
            e, ez.at[c.z], sem.at[6 + i], sem.at[9 + i], device_id=(to,), device_id_type=MESH
        )
        cp.start()
        cps.append(cp)
    for i in (1, 2, 3):
        cps[i - 1].wait_send()
        zz = lax.rem(c.z + 4 - i, 4)
        pltpu.make_async_copy(ez.at[zz], ez.at[zz], sem.at[9 + i]).wait()
    total = ((ez[0] + ez[1]) + ez[2]) + ez[3]
    vec = total[0:12, :]
    square_sum = (total[12:13, 0:128] + jnp.sum(vec * vec)) * (scale * scale)
    clip_ref[...] = jnp.broadcast_to(jnp.minimum(1.0, max_norm / (jnp.sqrt(square_sum) + 1e-06)), (8, 128))

    @pl.when(last)
    def _():
        for t in range(8):
            flat[pl.ds(3072 + t, 12, stride=8), :] = vec[:, 128 * t : 128 * (t + 1)]

    @pl.when(jnp.logical_not(last))
    def _():
        pltpu.make_async_copy(room, room, sem.at[15]).wait()

    pl.when(jnp.logical_not(first))(edge.wait_send)

    def block(i, _):
        wg[pl.ds(pl.multiple_of(i * 64, 64), 64), :] = flat[pl.ds(i * 64 + 3 * me, 64), :]
        return 0

    lax.fori_loop(0, 48, block, 0)
    wg[3072:3075, :] = flat[pl.ds(3072 + 3 * me, 3), :]


def close(chunk_a, chunk_b, gvec, scale):
    vm = pl.BlockSpec(memory_space=pltpu.VMEM)
    small = pltpu.VMEM((16, D), F32)
    return pl.pallas_call(
        functools.partial(close_kernel, scale=scale),
        in_specs=[vm] * 3,
        out_specs=[vm] * 2,
        out_shape=[jax.ShapeDtypeStruct((3075, 128), F32), jax.ShapeDtypeStruct((8, 128), F32)],
        scratch_shapes=[pltpu.VMEM((3168, 128), F32)]
        + [small] * 4
        + [pltpu.VMEM((4, 16, D), F32), pltpu.SemaphoreType.DMA((16,))],
        compiler_params=pltpu.CompilerParams(collective_id=4, has_side_effects=True, vmem_limit_bytes=VMEM_ALL),
        name="close",
    )(chunk_a, chunk_b, gvec)


def to_pieces(rows, first):
    n = rows.shape[0] // 128
    plain = rows.reshape(n, 128, D)
    three = rows.reshape(n // 3, 128, 3, D).transpose(0, 2, 1, 3).reshape(n, 128, D)
    four = rows.reshape(n, 32, 4, D).transpose(0, 2, 1, 3).reshape(n, 128, D)
    p = first + lax.broadcasted_iota(jnp.int32, (n, 1, 1), 0)
    return jnp.where(p < 24, three, jnp.where((p >= 32) & (p < 64), four, plain))


def from_pieces(pieces, first):
    n = pieces.shape[0]
    plain = pieces.reshape(n * 128, D)
    three = pieces.reshape(n // 3, 3, 128, D).transpose(0, 2, 1, 3).reshape(n * 128, D)
    four = pieces.reshape(n, 4, 32, D).transpose(0, 2, 1, 3).reshape(n * 128, D)
    p = first + lax.broadcasted_iota(jnp.int32, (n * 128, 1), 0) // 128
    return jnp.where(p < 24, three, jnp.where((p >= 32) & (p < 64), four, plain))


def update(params, moment_one, moment_two, weight_grad, clip_factor):
    clipped = clip_factor * weight_grad
    moment_one_new = beta_one * moment_one + (1.0 - beta_one) * clipped
    moment_two_new = beta_two * moment_two + (1.0 - beta_two) * clipped * clipped
    correct_one = 1.0 - beta_one**STEP
    correct_two = 1.0 - beta_two**STEP
    params_new = params - learn_rate * (
        moment_one_new / correct_one / (jnp.sqrt(moment_two_new / correct_two) + adam_eps) + decay_rate * params
    )
    return params_new, moment_one_new, moment_two_new


def shards(tokens, cotangent, params, moment_one, moment_two):
    n = lax.axis_size("dp")
    me = lax.axis_index("dp")
    shard_len = params.shape[0]
    images_all = tokens.shape[0] * n
    mats = PIECES * 128 * D
    scale = 1.0 / images_all
    if n == 32:
        unit = 128
        extra = 12 * D // unit
        own_units = shard_len // unit
        gap = extra // n
        low = params.reshape(own_units, unit)
        before = lax.ppermute(low[own_units - extra :].astype(BF), "dp", [(i, (i + 1) % n) for i in range(n)])
        joined = jnp.concatenate([before.astype(F32), low], axis=0)
        aligned = lax.dynamic_slice(joined, (extra - gap * me, 0), (own_units - gap, unit))
        own = to_pieces(aligned.reshape(-1, D), 3 * me).astype(BF)
        vec_own = jnp.pad(low[own_units - extra :].reshape(12, D), ((0, 4), (0, 0))).astype(BF)
        w, vec, z, n1, mixed = front(own, vec_own, tokens)
        flat_w = w.reshape(PIECES, 128, D)
        outputs, gup, gdn, gout, dmix, dhid, gvec = mlp(tokens, cotangent, mixed, vec, flat_w)
        parts = [gout, gup.reshape(32, 128, D), gdn]
        dz, chunk_a = back(z, dmix, parts, 1, 3, [(24, 32), (32, 64), (64, 96)], None)
        grad_tokens, chunk_b, gvec = tail_quick(tokens, dz, n1, dhid, vec, gvec, w, None)
        sums, clip = close(chunk_a, chunk_b, gvec, scale)
        weight_grad = sums.reshape(shard_len) * scale
        news = update(params, moment_one, moment_two, weight_grad, clip[0, 0])
        return (outputs, grad_tokens, weight_grad, *news)
    flat = lax.all_gather(params.astype(BF), "dp", axis=0, tiled=True)
    w = to_pieces(flat[:mats].reshape(-1, D), 0)
    vec = jnp.pad(flat[mats:].reshape(12, D).astype(F32), ((0, 4), (0, 0)))
    z, n1 = qkv(tokens, vec, w)
    mixed = attend(z)
    outputs, gup, gdn, gout, dmix, dhid, gvec = mlp(tokens, cotangent, mixed, vec, w)
    dz = attend_back(z, dmix)
    grad_tokens, gqkv, gvec = tail(tokens, dz, n1, dhid, vec, w, gvec)
    parts = [gqkv.reshape(24, 128, D), gout, gup.reshape(32, 128, D), gdn]
    flat = jnp.concatenate([from_pieces(jnp.concatenate(parts, axis=0), 0).reshape(-1), gvec[:12].reshape(-1).astype(BF)])
    arrived = lax.all_to_all(flat.reshape(n, shard_len), "dp", split_axis=0, concat_axis=0, tiled=True)
    weight_grad = jnp.sum(arrived.astype(F32), axis=0) * scale
    square_sum = lax.psum(jnp.sum(weight_grad * weight_grad), "dp")
    clip = jnp.minimum(1.0, max_norm / (jnp.sqrt(square_sum) + 1e-06))
    news = update(params, moment_one, moment_two, weight_grad, clip)
    return (outputs, grad_tokens, weight_grad, *news)


def solution(mesh):
    in_specs = (P("dp", None, None), P("dp", None, None), P("dp"), P("dp"), P("dp"))
    out_specs = (P("dp", None, None), P("dp", None, None), P("dp"), P("dp"), P("dp"), P("dp"))
    return jax.shard_map(shards, mesh=mesh, in_specs=in_specs, out_specs=out_specs, check_vma=False)
```

```python
import functools

import jax
import jax.numpy as jnp
from jax import lax
from jax.experimental import pallas as pl
from jax.experimental.pallas import tpu as pltpu
from jax.sharding import PartitionSpec as P

D = 1024
FF = 4096
S = 577
SQ = 592
M = 2 * SQ
CH = 32
PIECES = 96
STEP = 4
BF = jnp.bfloat16
F32 = jnp.float32
MESH = pl.DeviceIdType.MESH
VMEM_ALL = 67043328

EPS = 1e-06
max_norm = 1.0
beta_one = 0.9
beta_two = 0.95
learn_rate = 0.02
decay_rate = 0.05
adam_eps = 1e-08
SCORE = 0.125 * 1.4426950408889634


def nt(a, b):
    return lax.dot_general(a, b, (((1,), (1,)), ((), ())), preferred_element_type=F32)


def nn(a, b):
    return jnp.dot(a, b, preferred_element_type=F32)


def tn(a, b):
    return lax.dot_general(a, b, (((0,), (0,)), ((), ())), preferred_element_type=F32)


def rows_at(c):
    return pl.ds(pl.multiple_of(c * CH, CH), CH)


def full(shape):
    return pl.BlockSpec(shape, lambda *_: (0,) * len(shape), pipeline_mode=pl.Buffered(1))


class Ctx:
    def __init__(s):
        me=lax.axis_index("dp"); s.me=me
        s.core=me%2; s.x=(me//2)%2; s.y=(me//4)%2; s.z=me//8
        s.sib=me+1-2*s.core
        xp=me+2*(1-2*s.x); yp=me+4*(1-2*s.y)
        s.ap=xp+(yp-xp)*s.core
        s.bp=yp+(xp-yp)*s.core
        s.astep=2+2*s.core; s.bstep=4-2*s.core
        s.abit=s.x+(s.y-s.x)*s.core; s.bbit=s.y+(s.x-s.y)*s.core
        s.up=me+8; s.dn=me-8
        s.hasup=s.z<3; s.hasdn=s.z>0
    def barrier(s,extra=None):
        bar=pltpu.get_barrier_semaphore()
        for p in (s.sib,s.ap,s.bp): pl.semaphore_signal(bar,inc=1,device_id=(p,),device_id_type=MESH)
        @pl.when(s.hasup)
        def _(): pl.semaphore_signal(bar,inc=1,device_id=(s.up,),device_id_type=MESH)
        @pl.when(s.hasdn)
        def _(): pl.semaphore_signal(bar,inc=1,device_id=(s.dn,),device_id_type=MESH)
        more=0 if extra is None else extra
        pl.semaphore_wait(bar,3+jnp.where(s.hasup,1,0)+jnp.where(s.hasdn,1,0)+more)
class Gather:
    K = 3

    def __init__(s, c, own, w, ssem, rsem, lsem):
        s.c, s.own, s.w, s.ssem, s.rsem, s.lsem = c, own, w, ssem, rsem, lsem
        s.ns = 0
        s.pend = []

    def slot(s, dev, k):
        return s.rsem.at[dev * s.K + k]

    @staticmethod
    def when(conds, fn):
        if conds:
            pl.when(functools.reduce(jnp.logical_and, [f() for f in conds]))(fn)
        else:
            fn()

    def send(s, src, dev, k, to, outer, *conds):
        i = s.ns
        s.ns += 1
        cp = pltpu.make_async_remote_copy(
            src, s.w.at[dev, k], s.ssem.at[i], s.slot(dev, k), device_id=(to,), device_id_type=MESH
        )
        s.pend.append((i, outer + list(conds)))
        s.when(list(conds), cp.start)

    def step(s, text):
        kind = text[0]
        zz, k = int(text[-2]), int(text[-1])
        if kind == "o":
            s.give(text[1], zz, k)
        else:
            s.item(kind, zz, k)

    def give(s, route, zz, k):
        c = s.c
        to, conds = dict(
            d=(c.dn, [lambda: c.hasdn]), u=(c.up, [lambda: c.hasup]), b=(c.bp, []), a=(c.ap, []), s=(c.sib, [])
        )[route]
        here = [lambda: c.z == zz]
        s.when(here, lambda: s.send(s.own.at[k], c.me, k, to, here, *conds))

    def item(s, kind, zz, k):
        c = s.c
        src = c.me + 8 * (zz - c.z)
        if kind in "ac":
            src = src + c.astep * (1 - 2 * c.abit)
        if kind in "bc":
            src = src + c.bstep * (1 - 2 * c.bbit)
        outer = [lambda: c.z != zz] if kind == "z" else []

        def body():
            s.wait(src, k)
            r = s.w.at[src, k]
            cross = (zz, k) in CROSS_FIRST
            if kind == "z" or (cross and kind == "a"):
                s.send(r, src, k, c.up, outer, lambda: c.z >= zz, lambda: c.hasup)
                s.send(r, src, k, c.dn, outer, lambda: c.z <= zz, lambda: c.hasdn)
            if kind in "za":
                s.send(r, src, k, c.bp, outer)
            if kind == "z" and not cross:
                s.send(r, src, k, c.ap, outer)
            s.send(r, src, k, c.sib, outer)

        s.when(outer, body)

    def wait(s, dev, k):
        r = s.w.at[dev, k]
        pltpu.make_async_copy(r, r, s.slot(dev, k)).wait()

    def keep(s):
        for k in range(s.K):
            pltpu.make_async_copy(s.own.at[k], s.w.at[s.c.me, k], s.lsem.at[k]).start()

    def kept(s, k):
        pltpu.make_async_copy(s.own.at[k], s.w.at[s.c.me, k], s.lsem.at[k]).wait()

    def sibling(s, first, last, ks):
        def one(i, _):
            for k in ks:
                s.wait(2 * i + 1 - s.c.core, k)
            return 0

        lax.fori_loop(first, last, one, 0)

    def sent(s):
        for i, conds in s.pend:
            r = s.w.at[0, 0]
            s.when(conds, pltpu.make_async_copy(r, r, s.ssem.at[i]).wait)


class Vector:
    def __init__(s, c, own, vec, sem):
        s.c, s.own, s.vec, s.sem = c, own, vec, sem
        s.n = 31

    def tell(s):
        bar = pltpu.get_barrier_semaphore()

        @pl.when(s.c.me != s.n)
        def _():
            pl.semaphore_signal(bar, inc=1, device_id=(s.n,), device_id_type=MESH)

    def copy(s, to):
        return pltpu.make_async_remote_copy(
            s.own, s.vec, s.sem.at[to], s.sem.at[s.n], device_id=(to,), device_id_type=MESH
        )

    def start(s):
        @pl.when(s.c.me == s.n)
        def _():
            s.vec[...] = s.own[...]

            def one(i, _):
                s.copy(i).start()
                return 0

            lax.fori_loop(0, s.n, one, 0)

    def wait(s):
        @pl.when(s.c.me != s.n)
        def _():
            pltpu.make_async_copy(s.vec, s.vec, s.sem.at[s.n]).wait()

    def sent(s):
        @pl.when(s.c.me == s.n)
        def _():
            def one(i, _):
                s.copy(i).wait_send()
                return 0

            lax.fori_loop(0, s.n, one, 0)

class Reduce:
    K = 3

    @staticmethod
    def scratch(lo, hi, stage):
        nz = hi - lo + 1
        pieces = lambda n: pltpu.VMEM((n, 128, D), BF)
        dma = lambda n: pltpu.SemaphoreType.DMA((n,))
        sizes = [12 * nz, 6 * nz, 3 * nz, 3 * nz + 3]
        return (
            [pieces(n) for n in sizes]
            + [pieces(stage)]
            + [dma(12 * nz)]
            + [dma(n) for n in sizes]
            + [dma(12 * nz), dma(stage)]
        )

    def __init__(s, c, lo, hi, parts, out, scr, scale, order, direct=False, auto=True):
        s.auto = auto
        s.c, s.lo, s.hi, s.parts, s.out, s.scale, s.order, s.direct = c, lo, hi, parts, out, scale, order, direct
        s.S, s.B, s.A, s.Z, s.stage, s.sent_s, s.got_s, s.got_b, s.got_a, s.got_z, s.sent, s.loaded = scr
        s.nst = s.stage.shape[0]
        s.nz = hi - lo + 1
        s.later = []
        s.waits = []
        s.steps = [functools.partial(s.item, i) for i in range(len(order))]

    def owner(s, zz, fb, fa, core):
        c = s.c
        astep = 2 + 2 * core
        bstep = 4 - 2 * core
        abit = c.x + (c.y - c.x) * core
        bbit = c.y + (c.x - c.y) * core
        return zz * 8 + core + bstep * (bbit + fb * (1 - 2 * bbit)) + astep * (abit + fa * (1 - 2 * abit))

    def source(s, p, fn):
        if len(s.parts) == 1:
            lo, hi, ref = s.parts[0]
            fn(ref.at[p - lo])
            return
        for lo, hi, ref in s.parts:

            @pl.when(jnp.logical_and(p >= lo, p < hi))
            def _():
                fn(ref.at[jnp.clip(p - lo, 0, hi - lo - 1)])

    def slot(s, zz, fb, fa, k):
        return (((zz - s.lo) * 2 + fb) * 2 + fa) * s.K + k

    def places(s, order=None):
        for kind, zz, fa, k in order or s.order:
            if kind != "f":
                yield zz, 1 if kind == "b" else 0, fa, k

    def zero(s):
        c = s.c

        def clear(n):
            s.Z[n] = jnp.zeros((128, D), BF)

        for n in range(3 * s.nz + 3):
            at_zero = n < 3 * s.nz
            at_three = n >= 3 * s.nz or s.lo + n // 3 < 3
            if at_zero:
                pl.when(c.z == 0)(functools.partial(clear, n))
            if at_three:
                pl.when(c.z == 3)(functools.partial(clear, n))

    def to_sibling(s, order=None):
        c = s.c
        for zz, fb, fa, k in s.places(order):
            n = s.slot(zz, fb, fa, k)

            def go(r, n=n):
                pltpu.make_async_remote_copy(
                    r, s.S.at[n], s.sent_s.at[n], s.got_s.at[n], device_id=(c.sib,), device_id_type=MESH
                ).start()

            s.source(s.owner(zz, fb, fa, 1 - c.core) * s.K + k, go)

    def load(s, i):
        if s.direct or i >= len(s.order):
            return
        kind, zz, fa, k = s.order[i]
        n = i % s.nst

        def go(r):
            pltpu.make_async_copy(r, s.stage.at[n], s.loaded.at[n]).start()

        s.source(s.owner(zz, 1 if kind == "b" else 0, fa, s.c.core) * s.K + k, go)

    def prefetch(s):
        for i in range(s.nst - 1):
            s.load(i)

    def flush(s):
        for f in s.later:
            f()
        s.later = []

    @staticmethod
    def wait(ref, sem):
        pltpu.make_async_copy(ref, ref, sem).wait()

    @staticmethod
    def sum(srcs, dst, scale=None):
        def rows(r, _):
            rr = pl.ds(pl.multiple_of(r * 16, 16), 16)
            t = srcs[0][rr, :].astype(F32)
            for q in srcs[1:]:
                t = t + q[rr, :].astype(F32)
            if scale is not None:
                t = t * scale
            dst[rr, :] = t.astype(dst.dtype)
            return 0

        lax.fori_loop(0, 8, rows, 0)

    def item(s, i):
        c, K = s.c, s.K
        kind, zz, fa, k = s.order[i]
        fb = 1 if kind == "b" else 0
        if s.direct:
            lo, hi, ref = s.parts[0]
            own = ref.at[s.owner(zz, fb, fa, c.core) * K + k - lo]
        else:
            own = s.stage.at[i % s.nst]
            s.wait(own, s.loaded.at[i % s.nst])
        s.flush()
        n = s.slot(zz, fb, fa, k)
        out = s.S.at[n]
        bi = ((zz - s.lo) * 2 + fa) * K + k
        zi = (zz - s.lo) * K + k
        z2 = s.nz * K + k

        def gather(kinds):
            srcs = [own]
            if "S" in kinds:
                srcs.append((out, s.got_s.at[n]))
            if "B" in kinds:
                srcs.append((s.B.at[bi], s.got_b.at[bi]))
            if "A" in kinds:
                srcs.append((s.A.at[zi], s.got_a.at[zi]))
            for pair in srcs[1:]:
                s.wait(*pair)
            return srcs[:1] + [ref for ref, _ in srcs[1:]]

        def send(dst, sem, to):
            return pltpu.make_async_remote_copy(
                out, dst, s.sent.at[n], sem, device_id=(to,), device_id_type=MESH
            )

        if kind == "b":
            s.sum(gather("S"), out)
            s.later.append(send(s.B.at[bi], s.got_b.at[bi], c.bp).start)
            s.waits.append((n, None))
        elif kind == "a":
            s.sum(gather("SB"), out)
            s.later.append(send(s.A.at[zi], s.got_a.at[zi], c.ap).start)
            s.waits.append((n, None))
        elif kind == "z":

            @pl.when(c.z != zz)
            def _():
                srcs = gather("SBA")
                comes = jnp.where(c.z <= zz, c.z, 3 - c.z)
                pl.when(comes > 0)(functools.partial(s.wait, s.Z.at[zi], s.got_z.at[zi]))
                s.sum(srcs + [s.Z.at[zi]], out)

            def on():
                @pl.when(c.z < zz)
                def _():
                    send(s.Z.at[zi], s.got_z.at[zi], c.up).start()

                to = jnp.where(c.z == zz + 1, z2, zi)

                @pl.when(c.z > zz)
                def _():
                    send(s.Z.at[to], s.got_z.at[to], c.dn).start()

            s.later.append(on)
            s.waits.append((n, zz))
        else:

            @pl.when(c.z == zz)
            def _():
                srcs = gather("SBA")
                pl.when(c.hasdn)(functools.partial(s.wait, s.Z.at[zi], s.got_z.at[zi]))
                pl.when(c.hasup)(functools.partial(s.wait, s.Z.at[z2], s.got_z.at[z2]))
                s.sum(srcs + [s.Z.at[zi], s.Z.at[z2]], s.out.at[k], s.scale)

        if s.auto:
            s.load(i + s.nst - 1)

    def finish(s):
        s.flush()
        for n, zz in s.waits:
            w = functools.partial(s.wait, s.S.at[0], s.sent.at[n])
            if zz is None:
                w()
            else:
                pl.when(s.c.z != zz)(w)

        for place in s.places():
            s.wait(s.S.at[0], s.sent_s.at[s.slot(*place)])


BACK_STEPS = (
    ("b301", "b211", "b310", "b212",),
    ("b312", "b300", "b210",),
    ("b311", "b110", "a211", "b100", "b201",),
    (),
    (),
    ("b302",),
    ("a311",),
    ("a310",),
    ("z301", "a312", "a210",),
    ("z300", "b200", "a110", "b202",),
    ("a212", "b111", "z302", "z201",),
    (),
    ("z200", "b112",),
    ("b101", "a111", "z100",),
    ("b102", "z202", "f302", "a112", "f301", "f300", "z101",),
    ("f101", "f201", "f100", "f202", "z102",),
    ("f102", "f200",),
)
TAIL_STEPS = (
    (),
    (),
    ("b000", "b010",),
    ("b011", "b001",),
    ("a010", "a011", "b012", "b002",),
    ("z000",),
    ("a012", "f000", "z001",),
    ("f001", "z002",),
    ("f002",),
)


def reduce_order(groups):
    order = [(t[0], int(t[1]), int(t[2]), int(t[3])) for g in groups for t in g]
    ends = [sum(len(g) for g in groups[: i + 1]) for i in range(len(groups))]
    return order, [list(range(e - len(g), e)) for e, g in zip(ends, groups)]


def qkv_kernel(x_ref, vec_ref, w_ref, out_ref, n_ref):
    j = pl.program_id(0)

    @pl.when(j == 0)
    def _():
        for i in range(2):

            def block(rows, dst):
                v = x_ref[i, rows, :].astype(F32)
                c = v - jnp.mean(v, axis=1, keepdims=True)
                rc = lax.rsqrt(jnp.mean(c * c, axis=1, keepdims=True) + EPS)
                return (c * rc * (1.0 + vec_ref[8:9, :]) + vec_ref[9:10, :]).astype(BF)

            def one(c, _):
                n_ref[i, rows_at(c), :] = block(rows_at(c), None)
                return 0

            lax.fori_loop(0, 18, one, 0)
            last = block(slice(576, 577), None).astype(F32)
            n_ref[i, 576:592, :] = jnp.concatenate([last, jnp.zeros((15, D), F32)], axis=0).astype(BF)

    w = w_ref[...].reshape(D, D)
    bias = jnp.where(j == 0, vec_ref[0:1, :], jnp.where(j == 2, vec_ref[1:2, :], 0.0))
    for i in range(2):
        out_ref[0, i] = (nn(n_ref[i], w) + bias).astype(BF)


def qkv(x, vec, w):
    return pl.pallas_call(
        qkv_kernel,
        grid=(3,),
        in_specs=[full((2, S, D)), full((16, D)), pl.BlockSpec((8, 1, 128, D), lambda j: (0, j, 0, 0))],
        out_specs=[pl.BlockSpec((1, 2, SQ, D), lambda j: (j, 0, 0, 0)), full((2, SQ, D))],
        out_shape=[jax.ShapeDtypeStruct((3, 2, SQ, D), BF), jax.ShapeDtypeStruct((2, SQ, D), BF)],
        compiler_params=pltpu.CompilerParams(vmem_limit_bytes=VMEM_ALL),
        name="qkv",
    )(x, vec, w.reshape(32, 3, 128, D))


def padded(v):
    return jnp.concatenate([v, jnp.zeros((640 - SQ, 128), v.dtype)], axis=0)


def attend_pair(q, k, v):
    lane = lax.broadcasted_iota(jnp.int32, (1, 128), 1)
    k = padded(k)
    v = padded(v)
    outs = []
    for h in range(2):
        mine = lane < 64 if h == 0 else lane >= 64
        s = nt(jnp.where(mine, q, jnp.zeros_like(q)), k)
        s = jnp.concatenate([s[:, :512], jnp.where(lane < S - 512, s[:, 512:], -1e30)], axis=1)
        top = jnp.max(s, axis=1, keepdims=True)
        p = jnp.exp2((s - top) * SCORE)
        total = jnp.sum(p, axis=1, keepdims=True)
        outs.append(nn(p.astype(BF), v) * (1.0 / total))
    return jnp.where(lane < 64, outs[0], outs[1]).astype(BF)


def attend_kernel(q_ref, k_ref, v_ref, o_ref):
    half = SQ // 2
    for r in range(2):
        rows = slice(r * half, (r + 1) * half)
        o_ref[0, rows, :] = attend_pair(q_ref[0, 0, rows, :], k_ref[0, 0], v_ref[0, 0])


def attend(z):
    spec = lambda j: pl.BlockSpec((1, 1, SQ, 128), lambda i, h: (j, i, 0, h))
    return pl.pallas_call(
        attend_kernel,
        grid=(2, 8),
        in_specs=[spec(0), spec(1), spec(2)],
        out_specs=pl.BlockSpec((1, SQ, 128), lambda i, h: (i, 0, h)),
        out_shape=jax.ShapeDtypeStruct((2, SQ, D), BF),
        compiler_params=pltpu.CompilerParams(vmem_limit_bytes=VMEM_ALL),
        name="attend",
    )(z, z, z)


def norm_block(v, vec_ref):
    v = v.astype(F32)
    ce = v - jnp.mean(v, axis=1, keepdims=True)
    rc = lax.rsqrt(jnp.mean(ce * ce, axis=1, keepdims=True) + EPS)
    return (ce * rc * (1.0 + vec_ref[8:9, :]) + vec_ref[9:10, :]).astype(BF)


def norm_one(x_ref, vec_ref, n_ref):
    for i in range(2):

        def one(c, _):
            n_ref[i, rows_at(c), :] = norm_block(x_ref[i, rows_at(c), :], vec_ref)
            return 0

        lax.fori_loop(0, 18, one, 0)
        last = norm_block(x_ref[i, 576:577, :], vec_ref).astype(F32)
        n_ref[i, 576:592, :] = jnp.concatenate([last, jnp.zeros((15, D), F32)], axis=0).astype(BF)


FRONT_STEPS = (
    ("ob30", "os11", "os32", "ob00", "oa32", "ou00", "ou20", "ob21", "oa20", "ou21", "od12", "oa31", "oa00", "os10", "od10", "os00", "oa10", "os02", "ob32", "os22", "od31", "od32", "ob10", "ob20", "od22", "ob22", "od11", "ou10", "oa02", "oa30", "z00", "a00", "b00", "os21", "ob01", "oa01", "z01", "z02", "ou01", "ob31", "ou11", "ob02", "od20",),
    ("os20", "ou02", "a01", "ou12", "os12", "ou22", "c00", "a02", "z22", "z10", "z12", "os01", "z20", "b01", "c01", "os30", "ob12", "b02", "od30", "z11", "od21", "oa11", "ou31",),
    ("oa12", "c02", "oa21", "a10", "b10", "ou30", "ou32", "ob11",),
    ("a11",),
    (),
    ("z21",),
    ("a12", "z30",),
    (),
    ("z31", "c10", "b12",),
    ("os31", "z32", "a30",),
    ("b21",),
    ("a20", "a21",),
    (),
    ("oa22", "a31", "c11",),
    (),
    ("b20", "a22", "b31", "b32", "b22", "c21", "a32",),
    ("c30", "c12", "c20",),
    ("c31", "b11",),
    (),
    ("b30", "c22",),
    ("c32",),
)
CROSS_FIRST = ((1, 1), (2, 1), (1, 2), (2, 2), (1, 0))


def front_kernel(
    own, vec_own, x_ref, w, vec, z_out, n_out, mix_out, z_ref, n_ref, mix_ref, osem, vlow, wq, qsem, vsem, ssem, rsem, lsem
):
    c = Ctx()
    g = Gather(c, own, w, ssem, rsem, lsem)
    vector = Vector(c, vec_own, vlow, vsem)
    vector.tell()
    c.barrier(jnp.where(c.me == 31, 31, 0))
    vector.start()
    g.keep()

    def take(n):
        for text in FRONT_STEPS[n]:
            g.step(text)

    take(0)
    vector.wait()
    vec[...] = vlow[...].astype(F32)
    norm_one(x_ref, vec, n_ref)
    leave = [pltpu.make_async_copy(n_ref, n_out, osem.at[0])]
    leave[0].start()
    for j in range(3):
        take(1 + j)
        g.kept(j)
        g.sibling(0, 4, (j,))
        load = pltpu.make_async_copy(w.at[0:8, j], wq.at[j % 2], qsem.at[j])
        load.start()
        load.wait()
        for i in range(2):
            r = nn(n_ref[i], wq[j % 2].reshape(D, D))
            if j != 1:
                r = r + vec[j // 2 : j // 2 + 1, :]
            z_ref[j, i] = r.astype(BF)
    leave.append(pltpu.make_async_copy(z_ref, z_out, osem.at[1]))
    leave[1].start()

    def pair(t, _):
        for n in range(16):
            if FRONT_STEPS[4 + n]:

                @pl.when(t == n)
                def _():
                    take(4 + n)

        i = t // 8
        cols = pl.ds(pl.multiple_of((t % 8) * 128, 128), 128)
        half = SQ // 2
        k = z_ref[1, i, :, cols]
        v = z_ref[2, i, :, cols]
        for r in range(2):
            rows = slice(r * half, (r + 1) * half)
            mix_ref[i, rows, cols] = attend_pair(z_ref[0, i, rows, cols], k, v)
        return 0

    lax.fori_loop(0, 16, pair, 0)
    leave.append(pltpu.make_async_copy(mix_ref, mix_out, osem.at[2]))
    leave[2].start()
    take(20)
    g.sibling(4, 16, (0, 1, 2))
    g.sent()
    vector.sent()
    for cp in leave:
        cp.wait()


def front(own, vec_own, x):
    vm = pl.BlockSpec(memory_space=pltpu.VMEM)
    far = pl.BlockSpec(memory_space=pl.ANY)
    dma = lambda n: pltpu.SemaphoreType.DMA((n,))
    return pl.pallas_call(
        front_kernel,
        in_specs=[vm, vm, vm],
        out_specs=[far, vm, far, far, far],
        out_shape=[
            jax.ShapeDtypeStruct((32, 3, 128, D), BF),
            jax.ShapeDtypeStruct((16, D), F32),
            jax.ShapeDtypeStruct((3, 2, SQ, D), BF),
            jax.ShapeDtypeStruct((2, SQ, D), BF),
            jax.ShapeDtypeStruct((2, SQ, D), BF),
        ],
        scratch_shapes=[pltpu.VMEM((3, 2, SQ, D), BF), pltpu.VMEM((2, SQ, D), BF), pltpu.VMEM((2, SQ, D), BF), dma(3)]
        + [pltpu.VMEM((16, D), BF), pltpu.VMEM((2, 8, 128, D), BF), dma(3), dma(32)]
        + [dma(300), dma(96), dma(3)],
        compiler_params=pltpu.CompilerParams(collective_id=1, has_side_effects=True, vmem_limit_bytes=VMEM_ALL),
        name="front",
    )(own, vec_own, x)


def attend_back_pair(q, k, v, do):
    lane = lax.broadcasted_iota(jnp.int32, (1, 128), 1)
    real = lax.broadcasted_iota(jnp.int32, (16, 1), 0) < S - 576
    q = padded(q)
    do = padded(do)
    dqs, dks, dvs = [], [], []
    for h in range(2):
        mine = lane < 64 if h == 0 else lane >= 64
        s = nt(jnp.where(mine, k, jnp.zeros_like(k)), q)
        s = jnp.concatenate([s[:576], jnp.where(real, s[576:], -1e30)], axis=0)
        top = jnp.max(s, axis=0, keepdims=True)
        p = jnp.exp2((s - top) * SCORE)
        p = p * (1.0 / jnp.sum(p, axis=0, keepdims=True))
        dvs.append(nn(p.astype(BF), do))
        dp = nt(jnp.where(mine, v, jnp.zeros_like(v)), do)
        ds = (p * (dp - jnp.sum(p * dp, axis=0, keepdims=True))).astype(BF)
        dks.append(nn(ds, q))
        dqs.append(tn(ds, k))
    pick = lambda pair, scale: (jnp.where(lane < 64, pair[0], pair[1]) * scale).astype(BF)
    return pick(dqs, 0.125)[:SQ], pick(dks, 0.125), pick(dvs, 1.0)


def attend_back_kernel(q_ref, k_ref, v_ref, do_ref, out_ref):
    dq, dk, dv = attend_back_pair(q_ref[0, 0], k_ref[0, 0], v_ref[0, 0], do_ref[0])
    out_ref[0, 0] = dq
    out_ref[1, 0] = dk
    out_ref[2, 0] = dv


def attend_back(z, do):
    spec = lambda j: pl.BlockSpec((1, 1, SQ, 128), lambda i, h: (j, i, 0, h))
    return pl.pallas_call(
        attend_back_kernel,
        grid=(2, 8),
        in_specs=[spec(0), spec(1), spec(2), pl.BlockSpec((1, SQ, 128), lambda i, h: (i, 0, h))],
        out_specs=pl.BlockSpec((3, 1, SQ, 128), lambda i, h: (0, i, 0, h)),
        out_shape=jax.ShapeDtypeStruct((3, 2, SQ, D), BF),
        compiler_params=pltpu.CompilerParams(vmem_limit_bytes=VMEM_ALL),
        name="attend_back",
    )(z, z, z, do)


def mlp_kernel(x_ref,g_ref,mix_ref,vec_ref,wo_ref,wu_ref,wd_ref,
               out_ref,gup_ref,gdn_ref,gout_ref,dmix_ref,dhid_ref,gvec_ref,
               n2,gs,acc,dn,stat,*,FB,NB):
    jb=pl.program_id(0)
    hid=dhid_ref
    @pl.when(jb==0)
    def _():
        wo=wo_ref[...].reshape(D,D)
        for i in range(2):
            hid[i*SQ:(i+1)*SQ,:]=nn(mix_ref[i],wo)
            gs[i*SQ:i*SQ+576,:]=g_ref[i,:576,:]
            gs[i*SQ+576:(i+1)*SQ,:]=jnp.concatenate([g_ref[i,576:577,:].astype(F32),jnp.zeros((15,D),F32)],axis=0).astype(BF)
            def addx(c,_):
                r=pl.multiple_of(c*CH,CH)
                hid[pl.ds(i*SQ+r,CH),:]+=x_ref[i,pl.ds(r,CH),:].astype(F32)+vec_ref[2:3,:]
                return 0
            lax.fori_loop(0,18,addx,0)
            hid[i*SQ+576:i*SQ+577,:]+=x_ref[i,576:577,:].astype(F32)+vec_ref[2:3,:]
        acc[...]=jnp.zeros_like(acc); dn[...]=jnp.zeros_like(dn)
        gvec_ref[...]=jnp.zeros_like(gvec_ref)
        def ln(c,_):
            r=pl.ds(pl.multiple_of(c*CH,CH),CH)
            h=hid[r,:]
            mu=jnp.mean(h,axis=1,keepdims=True)
            ce=h-mu
            rc=lax.rsqrt(jnp.mean(ce*ce,axis=1,keepdims=True)+EPS)
            n2[r,:]=(ce*rc*(1.0+vec_ref[10:11,:])+vec_ref[11:12,:]).astype(BF)
            stat[r,0:1]=mu; stat[r,1:2]=rc
            return 0
        lax.fori_loop(0,M//CH,ln,0)
        def gsum(c,a):
            r=pl.ds(pl.multiple_of(c*CH,CH),CH)
            return a+gs[r,:].astype(F32)
        t=lax.fori_loop(0,M//CH,gsum,jnp.zeros((CH,D),F32))
        gvec_ref[7:8,:]=jnp.sum(t,axis=0,keepdims=True)
    wu=wu_ref[...].reshape(D,FB); wd=wd_ref[...].reshape(FB,D)
    nper=D//FB
    row=vec_ref[pl.ds(3+jb//nper,1),:]
    bup=row[:,:FB]
    for t in range(1,nper): bup=jnp.where(jb%nper==t,row[:,t*FB:(t+1)*FB],bup)
    g=gs[...]; n=n2[...]
    acts=[];dps=[]
    pres=[nn(n[i*SQ:(i+1)*SQ],wu)+bup for i in range(2)]
    das=[nt(g[i*SQ:(i+1)*SQ],wd) for i in range(2)]
    for i in range(2):
        pre=pres[i]
        cdf=0.5*(1.0+lax.erf(pre*0.7071067811865476))
        act=(pre*cdf).astype(BF)
        slope=cdf+pre*0.3989422804014327*jnp.exp(-0.5*pre*pre)
        dp=(das[i]*slope).astype(BF)
        acc[i*SQ:(i+1)*SQ,:]+=nn(act,wd)
        dn[i*SQ:(i+1)*SQ,:]+=nt(dp,wu)
        acts.append(act);dps.append(dp)
    act=jnp.concatenate(acts,axis=0);dp=jnp.concatenate(dps,axis=0)
    gup_ref[...]=tn(n,dp).astype(BF).reshape(gup_ref.shape)
    gdn_ref[...]=tn(act,g).astype(BF).reshape(gdn_ref.shape)
    bsum=jnp.sum(dp.astype(F32),axis=0,keepdims=True)
    for t in range(nper):
        @pl.when(jb%nper==t)
        def _(): gvec_ref[pl.ds(3+jb//nper,1),t*FB:(t+1)*FB]=bsum
    @pl.when(jb==NB-1)
    def _():
        for i in range(2):
            def ob(c,_):
                r=pl.multiple_of(c*CH,CH)
                out_ref[i,pl.ds(r,CH),:]=(hid[pl.ds(i*SQ+r,CH),:]+(acc[pl.ds(i*SQ+r,CH),:]+vec_ref[7:8,:])).astype(BF)
                return 0
            lax.fori_loop(0,18,ob,0)
            out_ref[i,576:577,:]=(hid[i*SQ+576:i*SQ+577,:]+(acc[i*SQ+576:i*SQ+577,:]+vec_ref[7:8,:])).astype(BF)
        def bk(c,car):
            a,b,d=car
            r=pl.ds(pl.multiple_of(c*CH,CH),CH)
            mu=stat[r,0:1]; rc=stat[r,1:2]
            xh=(hid[r,:]-mu)*rc
            dd=dn[r,:]
            e=dd*(1.0+vec_ref[10:11,:])
            dh=gs[r,:].astype(F32)+rc*(e-jnp.mean(e,axis=1,keepdims=True)-xh*jnp.mean(e*xh,axis=1,keepdims=True))
            dhid_ref[r,:]=dh
            db=dh.astype(BF)
            n2[r,:]=db
            return (a+dd*xh,b+dd,d+db.astype(F32))
        zz=jnp.zeros((CH,D),F32)
        a,b,d=lax.fori_loop(0,M//CH,bk,(zz,zz,zz))
        gvec_ref[10:11,:]=jnp.sum(a,axis=0,keepdims=True)
        gvec_ref[11:12,:]=jnp.sum(b,axis=0,keepdims=True)
        gvec_ref[2:3,:]=jnp.sum(d,axis=0,keepdims=True)
        db=n2[...]
        wo=wo_ref[...].reshape(D,D)
        dmix_ref[...]=nt(db,wo).astype(BF).reshape(2,SQ,D)
        gout_ref[...]=tn(mix_ref[...].reshape(M,D),db).astype(BF).reshape(8,128,D)
def mlp(x,g,mix,vec,W,FB=512):
    NB=4096//FB; nper=D//FB
    W4=W.reshape(96,4,32,1024)
    return pl.pallas_call(functools.partial(mlp_kernel,FB=FB,NB=NB),grid=(NB,),
      in_specs=[full((2,S,D)),full((2,S,D)),full((2,SQ,D)),full((16,D)),
        pl.BlockSpec((8,128,D),lambda j:(3,0,0),pipeline_mode=pl.Buffered(1)),
        pl.BlockSpec((32,1,32,FB),lambda j:(1,j//nper,0,j%nper)),
        pl.BlockSpec((FB//128,128,D),lambda j:(64//(FB//128)+j,0,0))],
      out_specs=[full((2,S,D)),pl.BlockSpec((32,1,32,FB),lambda j:(0,j//nper,0,j%nper)),
        pl.BlockSpec((FB//128,128,D),lambda j:(j,0,0)),full((8,128,D)),full((2,SQ,D)),full((M,D)),full((16,D))],
      out_shape=[jax.ShapeDtypeStruct((2,S,D),BF),jax.ShapeDtypeStruct((32,4,32,D),BF),jax.ShapeDtypeStruct((32,128,D),BF),
        jax.ShapeDtypeStruct((8,128,D),BF),jax.ShapeDtypeStruct((2,SQ,D),BF),jax.ShapeDtypeStruct((M,D),F32),jax.ShapeDtypeStruct((16,D),F32)],
      scratch_shapes=[pltpu.VMEM((M,D),BF),pltpu.VMEM((M,D),BF),pltpu.VMEM((M,D),F32),pltpu.VMEM((M,D),F32),pltpu.VMEM((M,128),F32)],
      compiler_params=pltpu.CompilerParams(vmem_limit_bytes=67043328),name=f"mlp{FB}")(x,g,mix,vec,W,W4,W)


def tail_kernel(x_ref, dz_ref, n_ref, dhid_ref, vec_ref, w_ref, gvin_ref, gx_ref, gw_ref, gvec_ref, acc):
    j = pl.program_id(0)

    @pl.when(j == 0)
    def _():
        gvec_ref[...] = gvin_ref[...]
        acc[...] = jnp.zeros_like(acc)

    w = w_ref[...].reshape(D, D)
    dz = dz_ref[0].reshape(M, D)
    acc[...] += nt(dz, w)
    gw_ref[...] = tn(n_ref[...].reshape(M, D), dz).astype(BF).reshape(8, 1, 128, D)

    @pl.when(j != 1)
    def _():
        def add(c, t):
            return t + dz_ref[0, 0, pl.ds(c * 16, 16), :].astype(F32) + dz_ref[0, 1, pl.ds(c * 16, 16), :].astype(F32)

        t = lax.fori_loop(0, SQ // 16, add, jnp.zeros((16, D), F32))
        gvec_ref[pl.ds(j // 2, 1), :] = jnp.sum(t, axis=0, keepdims=True)

    @pl.when(j == 2)
    def _():
        def back(x, dd, dh):
            v = x.astype(F32)
            ce = v - jnp.mean(v, axis=1, keepdims=True)
            rc = lax.rsqrt(jnp.mean(ce * ce, axis=1, keepdims=True) + EPS)
            xh = ce * rc
            e = dd * (1.0 + vec_ref[8:9, :])
            g = dh + rc * (e - jnp.mean(e, axis=1, keepdims=True) - xh * jnp.mean(e * xh, axis=1, keepdims=True))
            return g.astype(BF), dd * xh, dd

        a = b = jnp.zeros((CH, D), F32)
        la = lb = jnp.zeros((1, D), F32)
        for i in range(2):

            def one(c, carry):
                r = rows_at(c)
                r2 = pl.ds(pl.multiple_of(i * SQ + c * CH, 16), CH)
                g, s1, s2 = back(x_ref[i, r, :], acc[r2, :], dhid_ref[r2, :])
                gx_ref[i, r, :] = g
                return carry[0] + s1, carry[1] + s2

            a, b = lax.fori_loop(0, 18, one, (a, b))
            r2 = slice(i * SQ + 576, i * SQ + 577)
            g, s1, s2 = back(x_ref[i, 576:577, :], acc[r2, :], dhid_ref[r2, :])
            gx_ref[i, 576:577, :] = g
            la, lb = la + s1, lb + s2
        gvec_ref[8:9, :] = jnp.sum(a, axis=0, keepdims=True) + la
        gvec_ref[9:10, :] = jnp.sum(b, axis=0, keepdims=True) + lb


def tail(x, dz, n1, dhid, vec, w, gvec):
    return pl.pallas_call(
        tail_kernel,
        grid=(3,),
        in_specs=[
            full((2, S, D)),
            pl.BlockSpec((1, 2, SQ, D), lambda j: (j, 0, 0, 0)),
            full((2, SQ, D)),
            full((M, D)),
            full((16, D)),
            pl.BlockSpec((8, 1, 128, D), lambda j: (0, j, 0, 0)),
            full((16, D)),
        ],
        out_specs=[full((2, S, D)), pl.BlockSpec((8, 1, 128, D), lambda j: (0, j, 0, 0)), full((16, D))],
        out_shape=[
            jax.ShapeDtypeStruct((2, S, D), BF),
            jax.ShapeDtypeStruct((8, 3, 128, D), BF),
            jax.ShapeDtypeStruct((16, D), F32),
        ],
        scratch_shapes=[pltpu.VMEM((M, D), F32)],
        compiler_params=pltpu.CompilerParams(vmem_limit_bytes=VMEM_ALL),
        name="tail",
    )(x, dz, n1, dhid, vec, w.reshape(32, 3, 128, D), gvec)

def back_kernel(z_in, do_in, *refs, lo, hi, ranges, scale):
    n = len(ranges)
    parts = [(a, b, r) for (a, b), r in zip(ranges, refs[:n])]
    dz_out, chunk, z_ref, do_ref, dz_ref, iosem = refs[n : n + 6]
    c = Ctx()
    loads = [pltpu.make_async_copy(z_in.at[j], z_ref.at[j], iosem.at[j]) for j in range(3)]
    loads.append(pltpu.make_async_copy(do_in, do_ref, iosem.at[3]))
    for cp in loads:
        cp.start()
    order, groups = reduce_order(BACK_STEPS)
    red = Reduce(c, lo, hi, parts, chunk, refs[n + 6 :], scale, order)
    red.zero()
    chunk[...] = jnp.zeros_like(chunk)
    c.barrier()
    red.to_sibling()
    red.prefetch()
    for cp in loads:
        cp.wait()

    def pair(t, _):
        for m in range(16):
            if groups[m]:

                @pl.when(t == m)
                def _():
                    for i in groups[m]:
                        red.steps[i]()
                    red.flush()

        i = t // 8
        cols = pl.ds(pl.multiple_of((t % 8) * 128, 128), 128)
        dq, dk, dv = attend_back_pair(z_ref[0, i, :, cols], z_ref[1, i, :, cols], z_ref[2, i, :, cols], do_ref[i, :, cols])
        dz_ref[0, i, :, cols] = dq
        dz_ref[1, i, :, cols] = dk
        dz_ref[2, i, :, cols] = dv
        return 0

    lax.fori_loop(0, 16, pair, 0)
    leave = pltpu.make_async_copy(dz_ref, dz_out, iosem.at[4])
    leave.start()
    for i in groups[16]:
        red.steps[i]()
    red.finish()
    leave.wait()


def back(z, do, parts, lo, hi, ranges, scale):
    vm = pl.BlockSpec(memory_space=pltpu.VMEM)
    return pl.pallas_call(
        functools.partial(back_kernel, lo=lo, hi=hi, ranges=ranges, scale=scale),
        in_specs=[pl.BlockSpec(memory_space=pl.ANY)] * (2 + len(parts)),
        out_specs=[pl.BlockSpec(memory_space=pl.ANY), vm],
        out_shape=[jax.ShapeDtypeStruct((3, 2, SQ, D), BF), jax.ShapeDtypeStruct((3, 128, D), F32)],
        scratch_shapes=[
            pltpu.VMEM((3, 2, SQ, D), BF),
            pltpu.VMEM((2, SQ, D), BF),
            pltpu.VMEM((3, 2, SQ, D), BF),
            pltpu.SemaphoreType.DMA((5,)),
        ]
        + Reduce.scratch(lo, hi, 6),
        compiler_params=pltpu.CompilerParams(collective_id=2, has_side_effects=True, vmem_limit_bytes=VMEM_ALL),
        name="back",
    )(z, do, *parts)


def back_norm(x, dd, dh, vec_ref):
    v = x.astype(F32)
    ce = v - jnp.mean(v, axis=1, keepdims=True)
    rc = lax.rsqrt(jnp.mean(ce * ce, axis=1, keepdims=True) + EPS)
    xh = ce * rc
    e = dd * (1.0 + vec_ref[8:9, :])
    g = dh + rc * (e - jnp.mean(e, axis=1, keepdims=True) - xh * jnp.mean(e * xh, axis=1, keepdims=True))
    return g.astype(BF), dd * xh


def tail_quick_kernel(
    x_in, dz_ref, n_ref, dhid_in, vec_ref, gvin_ref, w, gx_ref, chunk, gvec_ref,
    x_ref, dhid_ref, xsem, acc, gw, wq, qsem, *scr, scale
):
    c = Ctx()
    order, groups = reduce_order(TAIL_STEPS)
    red = Reduce(c, 0, 0, [(0, 24, gw)], chunk, scr, scale, order, direct=True)
    loads = [pltpu.make_async_copy(w.at[0:8, j], wq.at[j % 2], qsem.at[j]) for j in range(3)]
    loads[0].start()
    loads[1].start()
    late = [pltpu.make_async_copy(x_in, x_ref, xsem.at[0]), pltpu.make_async_copy(dhid_in, dhid_ref, xsem.at[1])]
    for cp in late:
        cp.start()
    red.zero()
    chunk[...] = jnp.zeros_like(chunk)
    gvec_ref[...] = gvin_ref[...]
    c.barrier()

    def take(n):
        for i in groups[n]:
            red.steps[i]()
        red.flush()

    def weights(j):
        g = tn(n_ref[...].reshape(M, D), dz_ref[j].reshape(M, D)).astype(BF)
        for d in range(8):
            gw[3 * d + j] = g[128 * d : 128 * (d + 1)]

    def colsum(j):
        def add(r, t):
            rr = pl.ds(pl.multiple_of(r * 16, 16), 16)
            return t + dz_ref[j, 0, rr, :].astype(F32) + dz_ref[j, 1, rr, :].astype(F32)

        t = lax.fori_loop(0, SQ // 16, add, jnp.zeros((16, D), F32))
        gvec_ref[j // 2 : j // 2 + 1, :] = jnp.sum(t, axis=0, keepdims=True)

    def inputs(j):
        loads[j].wait()
        wj = wq[j % 2].reshape(D, D)
        for i in range(2):
            r = nt(dz_ref[j, i], wj)
            rows = slice(i * SQ, (i + 1) * SQ)
            acc[rows, :] = r if j == 0 else acc[rows, :] + r

    some = lambda k: [o for o in order if o[3] == k]
    weights(0)
    colsum(0)
    red.to_sibling(some(0))
    weights(1)
    red.to_sibling(some(1))
    take(2)
    weights(2)
    colsum(2)
    red.to_sibling(some(2))
    take(3)
    for j in range(3):
        inputs(j)
        if j == 0:
            loads[2].start()
        take(4 + j)
    for cp in late:
        cp.wait()
    a = b = jnp.zeros((CH, D), F32)
    la = lb = jnp.zeros((1, D), F32)
    for i in range(2):

        def one(t, carry):
            r = rows_at(t)
            r2 = pl.ds(pl.multiple_of(i * SQ + t * CH, 16), CH)
            dd = acc[r2, :]
            g, s1 = back_norm(x_ref[i, r, :], dd, dhid_ref[r2, :], vec_ref)
            gx_ref[i, r, :] = g
            return carry[0] + s1, carry[1] + dd

        a, b = lax.fori_loop(0, 18, one, (a, b))
        r2 = slice(i * SQ + 576, i * SQ + 577)
        dd = acc[r2, :]
        g, s1 = back_norm(x_ref[i, 576:577, :], dd, dhid_ref[r2, :], vec_ref)
        gx_ref[i, 576:577, :] = g
        la, lb = la + s1, lb + dd
        take(7 + i)
    gvec_ref[8:9, :] = jnp.sum(a, axis=0, keepdims=True) + la
    gvec_ref[9:10, :] = jnp.sum(b, axis=0, keepdims=True) + lb
    red.finish()


def tail_quick(x, dz, n1, dhid, vec, gvec, w, scale):
    vm = pl.BlockSpec(memory_space=pltpu.VMEM)
    far = pl.BlockSpec(memory_space=pl.ANY)
    return pl.pallas_call(
        functools.partial(tail_quick_kernel, scale=scale),
        in_specs=[far, vm, vm, far, vm, vm, far],
        out_specs=[vm] * 3,
        out_shape=[
            jax.ShapeDtypeStruct((2, S, D), BF),
            jax.ShapeDtypeStruct((3, 128, D), F32),
            jax.ShapeDtypeStruct((16, D), F32),
        ],
        scratch_shapes=[
            pltpu.VMEM((2, S, D), BF),
            pltpu.VMEM((M, D), F32),
            pltpu.SemaphoreType.DMA((2,)),
            pltpu.VMEM((M, D), F32),
            pltpu.VMEM((24, 128, D), BF),
            pltpu.VMEM((2, 8, 128, D), BF),
            pltpu.SemaphoreType.DMA((3,)),
        ]
        + Reduce.scratch(0, 0, 1),
        compiler_params=pltpu.CompilerParams(collective_id=3, has_side_effects=True, vmem_limit_bytes=VMEM_ALL),
        name="tail_quick",
    )(x, dz, n1, dhid, vec, gvec, w)


def close_kernel(chunk_a, chunk_b, gvec, wg, clip_ref, flat, e, es, ea, eb, ez, sem, *, scale):
    c = Ctx()
    me = c.me
    bar = pltpu.get_barrier_semaphore()
    others = [c.sib, c.ap, c.bp] + [lax.rem(me + 8 * i, 32) for i in (1, 2, 3)]
    for to in others:
        pl.semaphore_signal(bar, inc=1, device_id=(to,), device_id_type=MESH)
    first, last = me == 0, me == 31

    @pl.when(jnp.logical_not(first))
    def _():
        pl.semaphore_signal(bar, inc=1, device_id=(me - 1,), device_id_type=MESH)

    @pl.when(jnp.logical_not(last))
    def _():
        pl.semaphore_signal(bar, inc=1, device_id=(me + 1,), device_id_type=MESH)

    def unfold(src, k, kind):
        for t in range(8):
            cols = slice(128 * t, 128 * (t + 1))
            if kind == 0:
                flat[pl.ds(8 * k + t, 128, stride=24), :] = src[k, :, cols]
            elif kind == 1:
                flat[pl.ds(1024 * k + t, 128, stride=8), :] = src[k, :, cols]
            else:
                for j in range(4):
                    flat[pl.ds(1024 * k + 8 * j + t, 32, stride=32), :] = src[k, 32 * j : 32 * j + 32, cols]

    for k in range(3):
        p = 3 * me + k
        up = jnp.logical_and(p >= 32, p < 64)
        pl.when(c.z == 0)(functools.partial(unfold, chunk_b, k, 0))
        pl.when(up)(functools.partial(unfold, chunk_a, k, 2))
        pl.when(jnp.logical_and(c.z > 0, jnp.logical_not(up)))(functools.partial(unfold, chunk_a, k, 1))

    def square(i, t):
        v = flat[pl.ds(pl.multiple_of(i * 64, 64), 64), :]
        return t + v * v

    sq = jnp.sum(lax.fori_loop(0, 48, square, jnp.zeros((64, 128), F32)))
    e[0:12, :] = gvec[0:12, :]
    e[12:16, :] = jnp.full((4, D), sq, F32)
    pl.semaphore_wait(bar, 6 + jnp.where(first, 0, 1) + jnp.where(last, 0, 1))
    head = flat.at[0:96]
    room = flat.at[3072:3168]
    edge = pltpu.make_async_remote_copy(
        head, room, sem.at[14], sem.at[15], device_id=(jnp.maximum(me - 1, 0),), device_id_type=MESH
    )
    pl.when(jnp.logical_not(first))(edge.start)
    for n, (to, dst) in enumerate(((c.sib, es), (c.ap, ea), (c.bp, eb))):
        cp = pltpu.make_async_remote_copy(e, dst, sem.at[n], sem.at[3 + n], device_id=(to,), device_id_type=MESH)
        cp.start()
        cp.wait()
        e[...] = e[...] + dst[...]
    ez[c.z] = e[...]
    cps = []
    for i in (1, 2, 3):
        to = lax.rem(me + 8 * i, 32)
        cp = pltpu.make_async_remote_copy(
            e, ez.at[c.z], sem.at[6 + i], sem.at[9 + i], device_id=(to,), device_id_type=MESH
        )
        cp.start()
        cps.append(cp)
    for i in (1, 2, 3):
        cps[i - 1].wait_send()
        zz = lax.rem(c.z + 4 - i, 4)
        pltpu.make_async_copy(ez.at[zz], ez.at[zz], sem.at[9 + i]).wait()
    total = ((ez[0] + ez[1]) + ez[2]) + ez[3]
    vec = total[0:12, :]
    square_sum = (total[12:13, 0:128] + jnp.sum(vec * vec)) * (scale * scale)
    clip_ref[...] = jnp.broadcast_to(jnp.minimum(1.0, max_norm / (jnp.sqrt(square_sum) + 1e-06)), (8, 128))

    @pl.when(last)
    def _():
        for t in range(8):
            flat[pl.ds(3072 + t, 12, stride=8), :] = vec[:, 128 * t : 128 * (t + 1)]

    @pl.when(jnp.logical_not(last))
    def _():
        pltpu.make_async_copy(room, room, sem.at[15]).wait()

    pl.when(jnp.logical_not(first))(edge.wait_send)

    def block(i, _):
        wg[pl.ds(pl.multiple_of(i * 64, 64), 64), :] = flat[pl.ds(i * 64 + 3 * me, 64), :]
        return 0

    lax.fori_loop(0, 48, block, 0)
    wg[3072:3075, :] = flat[pl.ds(3072 + 3 * me, 3), :]


def close(chunk_a, chunk_b, gvec, scale):
    vm = pl.BlockSpec(memory_space=pltpu.VMEM)
    small = pltpu.VMEM((16, D), F32)
    return pl.pallas_call(
        functools.partial(close_kernel, scale=scale),
        in_specs=[vm] * 3,
        out_specs=[vm] * 2,
        out_shape=[jax.ShapeDtypeStruct((3075, 128), F32), jax.ShapeDtypeStruct((8, 128), F32)],
        scratch_shapes=[pltpu.VMEM((3168, 128), F32)]
        + [small] * 4
        + [pltpu.VMEM((4, 16, D), F32), pltpu.SemaphoreType.DMA((16,))],
        compiler_params=pltpu.CompilerParams(collective_id=4, has_side_effects=True, vmem_limit_bytes=VMEM_ALL),
        name="close",
    )(chunk_a, chunk_b, gvec)


def to_pieces(rows, first):
    n = rows.shape[0] // 128
    plain = rows.reshape(n, 128, D)
    three = rows.reshape(n // 3, 128, 3, D).transpose(0, 2, 1, 3).reshape(n, 128, D)
    four = rows.reshape(n, 32, 4, D).transpose(0, 2, 1, 3).reshape(n, 128, D)
    p = first + lax.broadcasted_iota(jnp.int32, (n, 1, 1), 0)
    return jnp.where(p < 24, three, jnp.where((p >= 32) & (p < 64), four, plain))


def from_pieces(pieces, first):
    n = pieces.shape[0]
    plain = pieces.reshape(n * 128, D)
    three = pieces.reshape(n // 3, 3, 128, D).transpose(0, 2, 1, 3).reshape(n * 128, D)
    four = pieces.reshape(n, 4, 32, D).transpose(0, 2, 1, 3).reshape(n * 128, D)
    p = first + lax.broadcasted_iota(jnp.int32, (n * 128, 1), 0) // 128
    return jnp.where(p < 24, three, jnp.where((p >= 32) & (p < 64), four, plain))


def update(params, moment_one, moment_two, weight_grad, clip_factor):
    clipped = clip_factor * weight_grad
    moment_one_new = beta_one * moment_one + (1.0 - beta_one) * clipped
    moment_two_new = beta_two * moment_two + (1.0 - beta_two) * clipped * clipped
    correct_one = 1.0 - beta_one**STEP
    correct_two = 1.0 - beta_two**STEP
    params_new = params - learn_rate * (
        moment_one_new / correct_one / (jnp.sqrt(moment_two_new / correct_two) + adam_eps) + decay_rate * params
    )
    return params_new, moment_one_new, moment_two_new


def shards(tokens, cotangent, params, moment_one, moment_two):
    n = lax.axis_size("dp")
    me = lax.axis_index("dp")
    shard_len = params.shape[0]
    images_all = tokens.shape[0] * n
    mats = PIECES * 128 * D
    scale = 1.0 / images_all
    if n == 32:
        unit = 128
        extra = 12 * D // unit
        own_units = shard_len // unit
        gap = extra // n
        low = params.reshape(own_units, unit)
        before = lax.ppermute(low[own_units - extra :].astype(BF), "dp", [(i, (i + 1) % n) for i in range(n)])
        joined = jnp.concatenate([before.astype(F32), low], axis=0)
        aligned = lax.dynamic_slice(joined, (extra - gap * me, 0), (own_units - gap, unit))
        own = to_pieces(aligned.reshape(-1, D), 3 * me).astype(BF)
        vec_own = jnp.pad(low[own_units - extra :].reshape(12, D), ((0, 4), (0, 0))).astype(BF)
        w, vec, z, n1, mixed = front(own, vec_own, tokens)
        flat_w = w.reshape(PIECES, 128, D)
        outputs, gup, gdn, gout, dmix, dhid, gvec = mlp(tokens, cotangent, mixed, vec, flat_w)
        parts = [gout, gup.reshape(32, 128, D), gdn]
        dz, chunk_a = back(z, dmix, parts, 1, 3, [(24, 32), (32, 64), (64, 96)], None)
        grad_tokens, chunk_b, gvec = tail_quick(tokens, dz, n1, dhid, vec, gvec, w, None)
        sums, clip = close(chunk_a, chunk_b, gvec, scale)
        weight_grad = sums.reshape(shard_len) * scale
        news = update(params, moment_one, moment_two, weight_grad, clip[0, 0])
        return (outputs, grad_tokens, weight_grad, *news)
    flat = lax.all_gather(params.astype(BF), "dp", axis=0, tiled=True)
    w = to_pieces(flat[:mats].reshape(-1, D), 0)
    vec = jnp.pad(flat[mats:].reshape(12, D).astype(F32), ((0, 4), (0, 0)))
    z, n1 = qkv(tokens, vec, w)
    mixed = attend(z)
    outputs, gup, gdn, gout, dmix, dhid, gvec = mlp(tokens, cotangent, mixed, vec, w)
    dz = attend_back(z, dmix)
    grad_tokens, gqkv, gvec = tail(tokens, dz, n1, dhid, vec, w, gvec)
    parts = [gqkv.reshape(24, 128, D), gout, gup.reshape(32, 128, D), gdn]
    flat = jnp.concatenate([from_pieces(jnp.concatenate(parts, axis=0), 0).reshape(-1), gvec[:12].reshape(-1).astype(BF)])
    arrived = lax.all_to_all(flat.reshape(n, shard_len), "dp", split_axis=0, concat_axis=0, tiled=True)
    weight_grad = jnp.sum(arrived.astype(F32), axis=0) * scale
    square_sum = lax.psum(jnp.sum(weight_grad * weight_grad), "dp")
    clip = jnp.minimum(1.0, max_norm / (jnp.sqrt(square_sum) + 1e-06))
    news = update(params, moment_one, moment_two, weight_grad, clip)
    return (outputs, grad_tokens, weight_grad, *news)


def solution(mesh):
    in_specs = (P("dp", None, None), P("dp", None, None), P("dp"), P("dp"), P("dp"))
    out_specs = (P("dp", None, None), P("dp", None, None), P("dp"), P("dp"), P("dp"), P("dp"))
    return jax.shard_map(shards, mesh=mesh, in_specs=in_specs, out_specs=out_specs, check_vma=False)
```
